32 devices in a mesh: dp: 16 (over z, y, x), mp: 2 (over core).
Axes of the slice: x: 2, y: 2, z: 4, core: 2. Of those that a mesh axis runs over, the one named last changes fastest.
Arguments:
- tokens: bfloat16 [16384, 768], P('dp'), may hold values from -6 to 6
- cotangent: bfloat16 [16384, 768], P('dp'), may hold values from -6 to 6
- lengths: int32 [16, 16], P('dp'), may hold values from 0 to 900, as said below
- ln1_gain: float32 [768], replicated, may hold values from 0.5 to 1.5
- ln1_bias: float32 [768], replicated, may hold values from -1.5 to 1.5
- qkv_weight: bfloat16 [768, 3, 768], P(None, None, 'mp'), may hold values from -0.21875 to 0.21875
- qv_bias: float32 [2, 768], P(None, 'mp'), may hold values from -2.5 to 2.5
- out_weight: bfloat16 [768, 768], P('mp'), may hold values from -0.875 to 0.875
- out_bias: float32 [768], replicated, may hold values from -1.5 to 1.5
- ln2_gain: float32 [768], replicated, may hold values from 0.5 to 1.5
- ln2_bias: float32 [768], replicated, may hold values from -1.5 to 1.5
- up_weight: bfloat16 [768, 3072], P(None, 'mp'), may hold values from -0.21875 to 0.21875
- up_bias: float32 [3072], P('mp'), may hold values from -2.5 to 2.5
- down_weight: bfloat16 [3072, 768], P('mp'), may hold values from -0.109375 to 0.109375
- down_bias: float32 [768], replicated, may hold values from -1.5 to 1.5
Outputs:
- output: bfloat16 [16384, 768], P('dp')
- tokens_grad: float32 [16384, 768], P('dp')
- ln1_gain_grad: float32 [768], replicated
- ln1_bias_grad: float32 [768], replicated
- qkv_weight_grad: float32 [768, 3, 768], P('dp', None, 'mp')
- qv_bias_grad: float32 [2, 768], P(None, 'mp')
- out_weight_grad: float32 [768, 768], P('mp', 'dp')
- out_bias_grad: float32 [768], replicated
- ln2_gain_grad: float32 [768], replicated
- ln2_bias_grad: float32 [768], replicated
- up_weight_grad: float32 [768, 3072], P('dp', 'mp')
- up_bias_grad: float32 [3072], P('mp')
- down_weight_grad: float32 [3072, 768], P('mp', 'dp')
- down_bias_grad: float32 [768], replicated
The draws below stay inside these ranges and needn't reach their ends.
Inputs may be any that keep to these rules, and one draw needn't show every extreme that they name: Each length is 0 or the square of one of 30, 15, 10, 6, 5. The lengths of one index of dp sum to at most 1024; its images lie one after another from its row 0 in slot order, and its remaining rows are padding.
All inputs are finite; a program needn't handle non-finite values.
Results may differ from the reference program's by a relative error of at most 0.012.
The reference program's roundings to bfloat16 on the way count: a program that leaves them out, or rounds other values in their place, can miss the bound.
Values may be sent and summed in bfloat16 or wider, within the bound.
No kernel may reach another device: no remote copies, remote signals or barrier semaphores. Data moves between devices by JAX's collectives and lax.ppermute only.
A program may use at most 192 MiB of HBM per device.

```python
import jax
import jax.numpy as jnp
from jax import lax

D = 768
HEADS = 12
HEAD_DIM = 64
FF = 3072
CAP = 1024
IMG_DEV = 16
GRID = 30
ROWS = 16384
N_DP = 16


def draw_lengths(key, part):
    key_heavy, key_pick, key_rank = jax.random.split(key, 3)
    coarse_sizes = jnp.array([(GRID // 2) ** 2, (GRID // 3) ** 2, (GRID // 5) ** 2, (GRID // 6) ** 2], jnp.int32)
    is_heavy = jax.random.randint(key_heavy, (N_DP,), 0, 8) == 0
    chosen = jax.random.randint(key_rank, (), 0, N_DP)
    is_heavy = jnp.logical_or(is_heavy, jnp.arange(N_DP) == chosen)
    drawn = jax.random.randint(key_pick, (N_DP, IMG_DEV), 0, 4)
    wanted = coarse_sizes[drawn]
    wanted = wanted.at[:, 0].set(jnp.where(is_heavy, GRID * GRID, wanted[:, 0]))
    running = jnp.zeros((N_DP,), jnp.int32)
    columns = []
    for slot_index in range(IMG_DEV):
        fitting = running + wanted[:, slot_index] <= CAP
        accepted = jnp.where(fitting, wanted[:, slot_index], 0).astype(jnp.int32)
        running = running + accepted
        columns.append(accepted)
    return jnp.stack(columns, axis=1).astype(jnp.int32)


def strengthened(values, stream_key, source, target, blocks, factor):
    owner, partner = [(jnp.arange(values.shape[axis_at]) // (values.shape[axis_at] // blocks)).reshape([-1 if axis == axis_at else 1 for axis in range(values.ndim)]) for axis_at in (source, target)]
    chosen = jax.random.permutation(stream_key, blocks)[partner]
    strong = (owner == chosen) | (owner == (partner + blocks // 2) % blocks)
    return jnp.where(strong, factor * values, values)


def levels(stream_key, extent, cuts, least, high):
    def one(dim, blocks):
        heights = jax.random.uniform(jax.random.fold_in(jax.random.fold_in(stream_key, 6), dim), (blocks,), jnp.float32, least / len(cuts), high / len(cuts))
        return jnp.repeat(jnp.exp(heights), extent[dim] // blocks).reshape((-1,) + (1,) * (len(extent) - dim - 1))

    level = one(*cuts[0])
    for cut in cuts[1:]:
        level = level * one(*cut)
    return level


def normal_values(key, extent, scale, bound, pieces=(), held_as=jnp.bfloat16):
    level = levels(key, extent, pieces, -0.22, 0.18) if pieces else 1.0
    values = jax.random.normal(key, extent, jnp.float32) * scale * level
    return jnp.minimum(jnp.maximum(values, -bound), bound).astype(held_as)


def gaussian_with(own_key, shape, spread, most, cuts, heavy, held_as=jnp.bfloat16):
    values = spread * jax.random.normal(own_key, shape, jnp.float32)
    if cuts:
        values = values * levels(own_key, shape, cuts, -0.22, 0.18)
    return jnp.clip(strengthened(values, jax.random.fold_in(own_key, 3), *heavy), -most, most).astype(held_as)


def setup_inputs(seed: int = 0) -> dict:
    key_list = jax.random.split(jax.random.key(seed), 16)
    return {
        "tokens": normal_values(key_list[0], (ROWS, D), 1.0, 6.0, ((0, 16),)),
        "cotangent": gaussian_with(key_list[1], (ROWS, D), 1.0, 6.0, ((0, 16),), (0, 1, 16, 2.0)),
        "lengths": draw_lengths(jax.random.fold_in(key_list[15], 71), 0),
        "ln1_gain": jnp.clip(1.0 + 0.1 * jax.random.normal(key_list[3], (D,), jnp.float32), 0.5, 1.5),
        "ln1_bias": normal_values(key_list[4], (D,), 0.3, 1.5, (), jnp.float32),
        "qkv_weight": normal_values(key_list[5], (D, 3, D), D ** -0.5, 0.21875, ((2, 2),)),
        "qv_bias": normal_values(key_list[6], (2, D), 0.5, 2.5, ((1, 2),), jnp.float32),
        "out_weight": normal_values(key_list[7], (D, D), (D // 16) ** -0.5, 0.875, ((0, 2),)),
        "out_bias": normal_values(key_list[8], (D,), 0.3, 1.5, (), jnp.float32),
        "ln2_gain": jnp.clip(1.0 + 0.1 * jax.random.normal(key_list[9], (D,), jnp.float32), 0.5, 1.5),
        "ln2_bias": normal_values(key_list[10], (D,), 0.3, 1.5, (), jnp.float32),
        "up_weight": normal_values(key_list[11], (D, FF), D ** -0.5, 0.21875, ((1, 2),)),
        "up_bias": normal_values(key_list[12], (FF,), 0.5, 2.5, ((0, 2),), jnp.float32),
        "down_weight": normal_values(key_list[13], (FF, D), FF ** -0.5, 0.109375, ((0, 2),)),
        "down_bias": normal_values(key_list[14], (D,), 0.3, 1.5, (), jnp.float32),
    }


EPSILON = 1e-06
HIGHEST_PRECISION = lax.Precision.HIGHEST

@jax.custom_vjp
def low(v):
    return lax.optimization_barrier(v.astype(jnp.bfloat16)).astype(jnp.float32)

@jax.custom_vjp
def low_back(v):
    return v

def low_keep(v):
    return (low(v), None)

def low_pass(kept, grad):
    return (grad,)

def back_keep(v):
    return (v, None)

def back_low(kept, grad):
    return (low(grad),)
low.defvjp(low_keep, low_pass)
low_back.defvjp(back_keep, back_low)

def layer_norm(values, gain, shift):
    centered = values - lax.optimization_barrier(jnp.mean(values, axis=-1, keepdims=True))
    variance = lax.optimization_barrier(jnp.mean(centered * centered, axis=-1, keepdims=True))
    return centered * lax.rsqrt(variance + EPSILON) * gain + shift

def device_rows(params, row_pair):
    tokens_dev, image_ids = row_pair
    ln1_gain, ln1_bias, qkv_weight, qv_bias, out_weight, out_bias, ln2_gain, ln2_bias, up_weight, up_bias, down_weight, down_bias = params
    row_count = tokens_dev.shape[0]
    hidden_one = low(layer_norm(tokens_dev, ln1_gain, ln1_bias))
    queries = jnp.dot(hidden_one, qkv_weight[:, 0, :], precision=HIGHEST_PRECISION) + qv_bias[0]
    keys_all = jnp.dot(hidden_one, qkv_weight[:, 1, :], precision=HIGHEST_PRECISION)
    values_all = jnp.dot(hidden_one, qkv_weight[:, 2, :], precision=HIGHEST_PRECISION) + qv_bias[1]
    queries = low(low_back(queries)).reshape(row_count, HEADS, HEAD_DIM)
    keys_all = low(low_back(keys_all)).reshape(row_count, HEADS, HEAD_DIM)
    values_all = low(low_back(values_all)).reshape(row_count, HEADS, HEAD_DIM)
    scores = jnp.einsum('qhd,khd->hqk', queries, keys_all, precision=HIGHEST_PRECISION) * HEAD_DIM ** (-0.5)
    scores = low_back(scores)
    same_image = image_ids[:, None] == image_ids[None, :]
    scores = jnp.where(same_image[None], scores, -1e+30)
    largest = lax.optimization_barrier(jnp.max(scores, axis=-1, keepdims=True))
    exponent = jnp.exp(scores - largest)
    probs = exponent / lax.optimization_barrier(jnp.sum(exponent, axis=-1, keepdims=True))
    mixed = jnp.einsum('hqk,khd->qhd', low(probs), values_all, precision=HIGHEST_PRECISION)
    mixed = low(low_back(mixed)).reshape(row_count, HEADS * HEAD_DIM)
    attended = jnp.dot(mixed, out_weight, precision=HIGHEST_PRECISION) + out_bias
    after_attn = tokens_dev + low_back(attended)
    hidden_two = low(layer_norm(after_attn, ln2_gain, ln2_bias))
    hidden_pre = low_back(jnp.dot(hidden_two, up_weight, precision=HIGHEST_PRECISION) + up_bias)
    activated = low(jax.nn.gelu(hidden_pre, approximate=True))
    branch = low_back(jnp.dot(activated, down_weight, precision=HIGHEST_PRECISION) + down_bias)
    return after_attn + branch

def reference(tokens, cotangent, lengths, ln1_gain, ln1_bias, qkv_weight, qv_bias, out_weight, out_bias, ln2_gain, ln2_bias, up_weight, up_bias, down_weight, down_bias):
    ends = jnp.cumsum(lengths, axis=1).astype(jnp.int32)
    positions = jnp.arange(CAP).astype(jnp.int32)
    image_ids = lax.optimization_barrier(jnp.sum((ends[:, None, :] <= positions[None, :, None]).astype(jnp.int32), axis=2)).astype(jnp.int32)
    valid = (image_ids < IMG_DEV).astype(jnp.float32).reshape(N_DP * CAP)
    params = tuple((item.astype(jnp.float32) for item in (ln1_gain, ln1_bias, qkv_weight, qv_bias, out_weight, out_bias, ln2_gain, ln2_bias, up_weight, up_bias, down_weight, down_bias)))
    checked = jax.checkpoint(device_rows)

    def forward(inputs_all, weights_all):
        stacked = inputs_all.reshape(N_DP, CAP, D)
        results = lax.map(lambda row_pair: checked(weights_all, row_pair), (stacked, image_ids))
        return results.reshape(N_DP * CAP, D)
    result, pullback = jax.vjp(forward, tokens.astype(jnp.float32), params)
    grad_out = cotangent.astype(jnp.float32) * valid[:, None]
    grad_in, grads = pullback(grad_out)
    return (result.astype(jnp.bfloat16), grad_in, grads[0], grads[1], grads[2], grads[3], grads[4], grads[5], grads[6], grads[7], grads[8], grads[9], grads[10], grads[11])
```

```python
import functools

import jax
import jax.numpy as jnp
from jax import lax
from jax.experimental import pallas as pl
from jax.experimental.pallas import tpu as pltpu
from jax.sharding import PartitionSpec as P

HEAD_DIM = 64
EPSILON = 1e-06
MASKED = 1e30
LANES = 128
TOTALS_AT = 32
bf16 = jnp.bfloat16
f32 = jnp.float32
Shape = jax.ShapeDtypeStruct
VMEM = pl.BlockSpec(memory_space=pltpu.VMEM)
SMEM = pl.BlockSpec(memory_space=pltpu.SMEM)


def call(kernel, name, outs, args, scalars=0, scratch=(), flops=0, limit=24):
    moved = sum(a.size * a.dtype.itemsize for a in (*args, *outs))
    return pl.pallas_call(
        kernel,
        name=name,
        out_shape=tuple(outs),
        in_specs=[SMEM] * scalars + [VMEM] * (len(args) - scalars),
        out_specs=tuple([VMEM] * len(outs)),
        scratch_shapes=scratch,
        compiler_params=pltpu.CompilerParams(vmem_limit_bytes=limit << 20),
        cost_estimate=pl.CostEstimate(
            flops=int(flops), bytes_accessed=int(moved), transcendentals=0
        ),
    )(*args)


def dot(a, b):
    return jnp.dot(a, b, preferred_element_type=f32)


def dot_t(a, b):
    return lax.dot_general(a, b, (((1,), (1,)), ((), ())), preferred_element_type=f32)


def lane_of(shape):
    return lax.broadcasted_iota(jnp.int32, shape, 1)


def head_half(values, half):
    return jnp.where(lane_of(values.shape) // HEAD_DIM == half, values, jnp.zeros_like(values))


def normalize(values):
    centered = values - jnp.mean(values, axis=-1, keepdims=True)
    variance = jnp.mean(centered * centered, axis=-1, keepdims=True)
    inverse = lax.rsqrt(variance + EPSILON)
    return centered * inverse, inverse


def norm_back(grad_out, normed, inverse, gain):
    scaled = grad_out * gain
    return inverse * (
        scaled
        - jnp.mean(scaled, axis=-1, keepdims=True)
        - normed * jnp.mean(scaled * normed, axis=-1, keepdims=True)
    )


def column_sum(values):
    return jnp.sum(values, axis=0, keepdims=True)


def qkv_kernel(
    lengths, tokens, gain, bias, weight, qv_bias, hidden, queries, keys, values, id_q, id_k
):
    rows = tokens.shape[0]
    slots = lengths.shape[1]
    lane = lane_of((1, LANES))
    starts = jnp.where(lane == 0, 0, rows)
    ends = jnp.full((1, LANES), rows, jnp.int32)
    running = jnp.int32(0)
    for slot in range(slots):
        running = running + lengths[0, slot]
        ends = jnp.where(lane == slot, running, ends)
        starts = jnp.where(lane == slot + 1, running, starts)
    scale = HEAD_DIM**-0.5
    block = 256

    @pl.loop(0, rows // block)
    def _(index):
        span = pl.ds(pl.multiple_of(index * block, block), block)
        row = index * block + lax.broadcasted_iota(jnp.int32, (block, LANES), 0)
        same = (row >= starts) & (row < ends)
        id_q[span, :] = same.astype(f32).astype(bf16)
        id_k[span, :] = jnp.where(same | (lane > slots), 0.0, -MASKED).astype(bf16)
        normed, _ = normalize(tokens[span, :].astype(f32))
        low = (normed * gain[...] + bias[...]).astype(bf16)
        hidden[span, :] = low
        raised = (dot(low, weight[0]) + qv_bias[0:1, :]).astype(bf16)
        queries[span, :] = (raised.astype(f32) * scale).astype(bf16)
        keys[span, :] = dot(low, weight[1]).astype(bf16)
        values[span, :] = (dot(low, weight[2]) + qv_bias[1:2, :]).astype(bf16)


def attention_kernel(row0, queries, keys, values, id_q, id_k, weight, mixed, features, part):
    rows = mixed.shape[0]
    span = slice(row0, row0 + rows)
    lane = lane_of((rows, LANES))
    ids = id_q[span, :]
    feature = ids.astype(f32)
    for pair in range(queries.shape[1] // LANES):
        cols = slice(pair * LANES, (pair + 1) * LANES)
        wide_keys = jnp.concatenate([keys[:, cols], id_k[...]], axis=1)
        query, value = queries[span, cols], values[:, cols]
        total = None
        inverses = []
        for half in range(2):
            wide_query = jnp.concatenate([head_half(query, half), ids], axis=1)
            scores = dot_t(wide_query, wide_keys)
            largest = jnp.max(scores, axis=1, keepdims=True)
            exponent = jnp.exp(scores - largest)
            totals = jnp.sum(exponent, axis=1, keepdims=True)
            term = dot(exponent.astype(bf16), head_half(value, half))
            total = term if total is None else total + term
            inverses.append(1.0 / totals)
            rest = -(largest + jnp.log(totals))
            for piece in range(3):
                part_of = rest.astype(bf16).astype(f32)
                rest = rest - part_of
                at = TOTALS_AT + 3 * (2 * pair + half) + piece
                feature = jnp.where(lane == at, part_of, feature)
        mixed[:, cols] = (total * jnp.where(lane < HEAD_DIM, inverses[0], inverses[1])).astype(bf16)
    features[...] = feature.astype(bf16)
    part[...] = dot(mixed[...], weight[...]).astype(bf16)


def mlp_kernel(
    row0, lengths, tokens, cotangent, mine, other, out_bias, gain, bias, up, up_bias, down,
    hidden, grad_mlp, activated, grad_pre, part, down_bias_grad,
):
    rows = hidden.shape[0]
    used = jnp.int32(0)
    for slot in range(lengths.shape[1]):
        used = used + lengths[0, slot]
    block, tile = 256, 512
    down_bias_grad[...] = jnp.zeros_like(down_bias_grad)

    @pl.loop(0, rows // block)
    def _(index):
        span = pl.ds(pl.multiple_of(index * block, block), block)
        source = pl.ds(pl.multiple_of(row0 + index * block, block), block)
        after = tokens[source, :].astype(f32) + (
            mine[span, :].astype(f32) + other[span, :].astype(f32) + out_bias[...]
        )
        normed, _ = normalize(after)
        low = (normed * gain[...] + bias[...]).astype(bf16)
        hidden[span, :] = low
        row = row0 + index * block + lax.broadcasted_iota(jnp.int32, (block, 1), 0)
        grad = jnp.where(row < used, cotangent[source, :].astype(f32), 0.0)
        down_bias_grad[...] += column_sum(grad)
        grad = grad.astype(bf16)
        grad_mlp[span, :] = grad
        total = None
        for start in range(0, up.shape[1], tile):
            cols = slice(start, start + tile)
            pre = dot(low, up[:, cols]) + up_bias[:, cols]
            square = pre * pre
            inner = pre * (0.7978845608028654 + (0.7978845608028654 * 0.044715) * square)
            tanh = jnp.tanh(inner)
            half = 0.5 + 0.5 * tanh
            activated[span, cols] = (pre * half).astype(bf16)
            slope = half + (0.5 * pre) * (1.0 - tanh * tanh) * (
                0.7978845608028654 + (3 * 0.7978845608028654 * 0.044715) * square
            )
            grad_low = (dot_t(grad, down[cols, :]) * slope).astype(bf16)
            grad_pre[span, cols] = grad_low
            term = dot_t(grad_low, up[:, cols])
            total = term if total is None else total + term
        part[span, :] = total.astype(bf16)


def down_kernel(first, second, weight, part):
    rows = first.shape[0]
    for index, chunk in enumerate((first, second)):
        part[index * rows : (index + 1) * rows, :] = dot(chunk[...], weight[...]).astype(bf16)


def weight_kernel(parts_left, parts_right, blocks, with_sums, *refs):
    place, refs = refs[0], refs[1:]
    left, right = refs[:parts_left], refs[parts_left : parts_left + parts_right]
    outs = refs[parts_left + parts_right :]
    keep, send = outs[0], outs[1]
    joined = jnp.concatenate([ref[...] for ref in left], axis=0)
    rows, width = joined.shape
    size = width // blocks
    turned = joined.T
    if with_sums:
        turned = jnp.concatenate([turned, jnp.ones((16, rows), bf16)], axis=0)
    columns = keep.shape[1]
    tile = 384
    sources = right if len(right[0].shape) == 2 else None
    chunks = len(left)
    groups = len(right) // chunks
    start = 0
    for group in range(groups):
        pieces = right[group * chunks : (group + 1) * chunks]
        for begin in range(0, pieces[0].shape[1], tile):
            stop = min(begin + tile, pieces[0].shape[1])
            cols = slice(start + begin, start + stop)
            operand = jnp.concatenate([piece[:, begin:stop] for piece in pieces], axis=0)
            result = dot(turned, operand)
            if with_sums:
                outs[2][:, cols] = result[width : width + 8]
            for index in range(blocks):
                low = result[index * size : (index + 1) * size].astype(bf16)
                to = place[index]

                @pl.when(to < blocks // 2)
                def _(low=low, to=to, cols=cols):
                    keep[pl.ds(pl.multiple_of(to * size, size), size), cols] = low

                @pl.when(to >= blocks // 2)
                def _(low=low, to=to, cols=cols):
                    at = (to - blocks // 2) * size
                    send[pl.ds(pl.multiple_of(at, size), size), cols] = low

        start += pieces[0].shape[1]


def plain_weight_kernel(parts_left, parts_right, blocks, with_sums, *refs):
    refs = refs[1:]
    left, right = refs[:parts_left], refs[parts_left : parts_left + parts_right]
    outs = refs[parts_left + parts_right :]
    turned = jnp.concatenate([ref[...] for ref in left], axis=0).T
    rows = turned.shape[1]
    width = turned.shape[0]
    chunks = len(left)
    start = 0
    for group in range(len(right) // chunks):
        pieces = right[group * chunks : (group + 1) * chunks]
        cols = slice(start, start + pieces[0].shape[1])
        operand = jnp.concatenate([piece[...] for piece in pieces], axis=0)
        result = dot(turned, operand)
        if with_sums:
            outs[2][:, cols] = dot(jnp.ones((8, rows), bf16), operand)
        outs[0][:, cols] = result[: width // 2].astype(bf16)
        outs[1][:, cols] = result[width // 2 :].astype(bf16)
        start += pieces[0].shape[1]


def middle_kernel(
    row0, lengths, tokens, cotangent, mine, other, out_bias, gain, norm_mine, norm_other,
    weight, resid, grad_attn, grad_mixed, sums,
):
    rows = resid.shape[0]
    used = jnp.int32(0)
    for slot in range(lengths.shape[1]):
        used = used + lengths[0, slot]
    block = 128
    sums[...] = jnp.zeros_like(sums)

    @pl.loop(0, rows // block)
    def _(index):
        span = pl.ds(pl.multiple_of(index * block, block), block)
        source = pl.ds(pl.multiple_of(row0 + index * block, block), block)
        after = tokens[source, :].astype(f32) + (
            mine[span, :].astype(f32) + other[span, :].astype(f32) + out_bias[...]
        )
        normed, inverse = normalize(after)
        grad_norm = norm_mine[span, :].astype(f32) + norm_other[span, :].astype(f32)
        row = row0 + index * block + lax.broadcasted_iota(jnp.int32, (block, 1), 0)
        grad = jnp.where(row < used, cotangent[source, :].astype(f32), 0.0)
        grad = grad + norm_back(grad_norm, normed, inverse, gain[...])
        resid[span, :] = grad
        low = grad.astype(bf16)
        grad_attn[span, :] = low
        sums[0:1, :] += column_sum(grad_norm * normed)
        sums[1:2, :] += column_sum(grad_norm)
        sums[2:3, :] += column_sum(low.astype(f32))

    grad_mixed[...] = dot_t(grad_attn[...], weight[...]).astype(bf16)


def attention_back_kernel(
    pair, queries, keys, values, id_k, features0, features1, grad0, grad1,
    query_grad, key_grad, value_grad, wide_keys, turned, key_total, value_total,
):
    rows = queries.shape[0]
    cols = slice(pair * LANES, (pair + 1) * LANES)
    lane = lane_of((1, LANES))
    key = keys[:, cols]
    turned[...] = key.T
    for half in range(2):
        at = TOTALS_AT + 3 * (2 * pair + half)
        wide_keys[half, :, :LANES] = key
        wide_keys[half, :, LANES:] = id_k[...] + ((lane >= at) & (lane < at + 3)).astype(f32).astype(bf16)
    for index, (features, grads) in enumerate(((features0, grad0), (features1, grad1))):
        block = features.shape[0]
        span = slice(index * block, (index + 1) * block)
        query, grad, feature = queries[span, cols], grads[:, cols], features[...]
        value = values[:, cols]
        key_term = value_term = None
        turned_grads = []
        for half in range(2):
            one_query, one_grad = head_half(query, half), head_half(grad, half)
            probs = jnp.exp(dot_t(wide_keys[half], jnp.concatenate([one_query, feature], axis=1)))
            grad_probs = dot_t(value, one_grad)
            centre = jnp.sum(probs * grad_probs, axis=0, keepdims=True)
            grad_scores = (probs * (grad_probs - centre)).astype(bf16)
            value_one = dot(probs.astype(bf16), one_grad)
            key_one = dot(grad_scores, one_query)
            value_term = value_one if half == 0 else value_term + value_one
            key_term = key_one if half == 0 else key_term + key_one
            turned_grads.append(dot(turned[half * HEAD_DIM : (half + 1) * HEAD_DIM, :], grad_scores))
        if index == 0:
            key_total[...] = key_term
            value_total[...] = value_term
        else:
            key_grad[...] = (key_total[...] + key_term).astype(bf16)
            value_grad[...] = (value_total[...] + value_term).astype(bf16)
        query_grad[span, :] = (jnp.concatenate(turned_grads, axis=0).T * HEAD_DIM**-0.5).astype(bf16)


def first_kernel(*refs):
    weight, part = refs[-2], refs[-1]
    grads = refs[:-2]
    pairs = len(grads) // 3
    total = None
    for pair in range(pairs):
        cols = slice(pair * LANES, (pair + 1) * LANES)
        for kind in range(3):
            term = dot_t(grads[3 * pair + kind][...], weight[kind, :, cols])
            total = term if total is None else total + term
    part[...] = total.astype(bf16)


def last_kernel(tokens, gain, mine, other, resid0, resid1, out, sums):
    block = 128
    sums[...] = jnp.zeros_like(sums)
    for index, resid in enumerate((resid0, resid1)):
        rows = resid.shape[0]

        @pl.loop(0, rows // block)
        def _(step, index=index, rows=rows, resid=resid):
            span = pl.ds(pl.multiple_of(step * block, block), block)
            source = pl.ds(pl.multiple_of(index * rows + step * block, block), block)
            normed, inverse = normalize(tokens[source, :].astype(f32))
            grad_first = mine[source, :].astype(f32) + other[source, :].astype(f32)
            out[source, :] = resid[span, :] + norm_back(grad_first, normed, inverse, gain[...])
            sums[0:1, :] += column_sum(grad_first * normed)
            sums[1:2, :] += column_sum(grad_first)


def swap(values, axis, bit, size):
    return lax.ppermute(values, axis, [(i, i ^ (1 << bit)) for i in range(size)])


def all_sum(values, bits, size):
    for bit in bits:
        values = values + swap(values, "dp", bit, size)
    return values


def scatter_sum(keep, send, order, size):
    for step, bit in enumerate(order):
        total = keep.astype(f32) + swap(send, "dp", bit, size).astype(f32)
        if step + 1 < len(order):
            middle = total.shape[0] // 2
            keep, send = total[:middle], total[middle:].astype(bf16)
    return total


def weight_grad(name, left, right, order, size, me, with_sums=False):
    width = left[0].shape[1]
    columns = sum(group[0].shape[1] for group in right)
    source = jnp.arange(size, dtype=jnp.int32) ^ me
    place = jnp.zeros((size,), jnp.int32)
    for step, bit in enumerate(order):
        place = place + (((source >> bit) & 1) << (size.bit_length() - 2 - step))
    outs = [Shape((width // 2, columns), bf16)] * 2
    if with_sums:
        outs.append(Shape((8, columns), f32))
    kernel = weight_kernel
    if (width // size) % 16:
        kernel = plain_weight_kernel
        spots = jnp.zeros((size,), jnp.int32).at[place].set(jnp.arange(size, dtype=jnp.int32))
        left = [
            chunk.reshape(chunk.shape[0], size, width // size)[:, spots].reshape(chunk.shape)
            for chunk in left
        ]
    flat = [piece for group in right for piece in group]
    return call(
        functools.partial(kernel, len(left), len(flat), size, with_sums),
        name,
        outs,
        [place, *left, *flat],
        scalars=1,
        flops=2 * width * columns * sum(chunk.shape[0] for chunk in left),
        limit=30,
    )


def per_device(
    n_dp, tokens, cotangent, lengths, ln1_gain, ln1_bias, qkv_weight, qv_bias, out_weight, out_bias,
    ln2_gain, ln2_bias, up_weight, up_bias, down_weight, down_bias,
):
    rows, width = tokens.shape
    local = qkv_weight.shape[2]
    hidden_units = up_weight.shape[1]
    pairs = local // LANES
    half = rows // 2
    me = lax.axis_index("dp")
    bits = list(range(n_dp.bit_length() - 1))
    order_a = bits
    order_b = [bits[1], bits[0], *bits[2:]]
    weight = jnp.transpose(qkv_weight, (1, 0, 2))
    row = lambda vector: vector.reshape(1, -1)
    wide = Shape((rows, width), bf16)
    thin = Shape((rows, local), bf16)
    block = Shape((rows, LANES), bf16)

    hidden_one, queries, keys, values, id_q, id_k = call(
        qkv_kernel,
        "qkv",
        [wide, thin, thin, thin, block, block],
        [lengths, tokens, row(ln1_gain), row(ln1_bias), weight, qv_bias],
        scalars=1,
        flops=2 * rows * width * 3 * local,
    )
    mixed, features, parts, others = [], [], [], []
    for chunk in range(2):
        one, feature, part = call(
            functools.partial(attention_kernel, chunk * half),
            "attention",
            [Shape((half, local), bf16), Shape((half, LANES), bf16), Shape((half, width), bf16)],
            [queries, keys, values, id_q, id_k, out_weight],
            flops=8 * half * rows * local,
            limit=34,
        )
        mixed.append(one)
        features.append(feature)
        parts.append(part)
        others.append(swap(part, "mp", 0, 2))
    hidden_two, grad_mlp, activated, grad_pre, norm_parts, norm_others, down_sums = (
        [] for _ in range(7)
    )
    for chunk in range(2):
        results = call(
            functools.partial(mlp_kernel, chunk * half),
            "mlp",
            [
                Shape((half, width), bf16),
                Shape((half, width), bf16),
                Shape((half, hidden_units), bf16),
                Shape((half, hidden_units), bf16),
                Shape((half, width), bf16),
                Shape((1, width), f32),
            ],
            [
                lengths, tokens, cotangent, parts[chunk], others[chunk], row(out_bias), row(ln2_gain),
                row(ln2_bias), up_weight, row(up_bias), down_weight,
            ],
            scalars=1,
            flops=6 * half * width * hidden_units,
        )
        for group, result in zip(
            (hidden_two, grad_mlp, activated, grad_pre, norm_parts, down_sums), results
        ):
            group.append(result)
        norm_others.append(swap(results[4], "mp", 0, 2))
    down_keep, down_send = weight_grad(
        "down_grad", grad_mlp, [activated], order_a, n_dp, me
    )
    up_keep, up_send, up_sums = weight_grad(
        "up_grad", hidden_two, [grad_pre], order_b, n_dp, me, True
    )
    resid, grad_attn, grad_mixed, middle_sums = [], [], [], []
    for chunk in range(2):
        results = call(
            functools.partial(middle_kernel, chunk * half),
            "middle",
            [
                Shape((half, width), f32),
                Shape((half, width), bf16),
                Shape((half, local), bf16),
                Shape((8, width), f32),
            ],
            [
                lengths, tokens, cotangent, parts[chunk], others[chunk], row(out_bias), row(ln2_gain),
                norm_parts[chunk], norm_others[chunk], out_weight,
            ],
            scalars=1,
            flops=2 * half * width * local,
        )
        for group, result in zip((resid, grad_attn, grad_mixed, middle_sums), results):
            group.append(result)
    out_keep, out_send = weight_grad("out_grad", grad_attn, [mixed], order_a, n_dp, me)
    grads = []
    for pair in range(pairs):
        grads.append(
            call(
                functools.partial(attention_back_kernel, pair),
                "attention_back",
                [block, block, block],
                [queries, keys, values, id_k, *features, *grad_mixed],
                scratch=[
                    pltpu.VMEM((2, rows, 2 * LANES), bf16),
                    pltpu.VMEM((LANES, rows), bf16),
                    pltpu.VMEM((rows, LANES), f32),
                    pltpu.VMEM((rows, LANES), f32),
                ],
                flops=4 * 10 * rows * rows * LANES,
                limit=34,
            )
        )
    flat_grads = [piece for group in grads for piece in group]
    (first_part,) = call(
        first_kernel,
        "first",
        [wide],
        [*flat_grads, weight],
        flops=2 * rows * width * 3 * local,
    )
    first_other = swap(first_part, "mp", 0, 2)
    qkv_keep, qkv_send, qkv_sums = weight_grad(
        "qkv_grad", [hidden_one], [[piece] for piece in flat_grads], order_b, n_dp, me, True
    )
    tokens_grad, last_sums = call(
        last_kernel,
        "last",
        [Shape((rows, width), f32), Shape((8, width), f32)],
        [tokens, row(ln1_gain), first_part, first_other, *resid],
    )
    (down_part,) = call(
        down_kernel,
        "down",
        [wide],
        [*activated, down_weight],
        flops=2 * rows * width * hidden_units,
    )
    down_other = swap(down_part, "mp", 0, 2)
    attended = jnp.concatenate(parts, axis=0).astype(f32) + jnp.concatenate(others, axis=0).astype(f32)
    after_attn = tokens.astype(f32) + (attended + out_bias)
    output = (
        after_attn + (down_part.astype(f32) + down_other.astype(f32) + down_bias)
    ).astype(bf16)

    middle_vectors = jnp.concatenate(
        [
            (middle_sums[0] + middle_sums[1])[:3],
            down_sums[0] + down_sums[1],
            up_sums[0].reshape(-1, width),
        ],
        axis=0,
    )
    middle_vectors = all_sum(middle_vectors, bits, n_dp)
    qkv_sums = qkv_sums[0].reshape(pairs, 3, LANES)
    last_vectors = jnp.concatenate(
        [last_sums[:2], qkv_sums[:, 0].reshape(1, local), qkv_sums[:, 2].reshape(1, local)]
        if width == local
        else [
            last_sums[:2],
            jnp.concatenate([qkv_sums[:, 0].reshape(1, local), qkv_sums[:, 2].reshape(1, local)], axis=1),
        ],
        axis=0,
    )
    last_vectors = all_sum(last_vectors, bits, n_dp)
    qv_sum = last_vectors[2:].reshape(2, local)

    down_total = scatter_sum(down_keep, down_send, order_a, n_dp)
    up_total = scatter_sum(up_keep, up_send, order_b, n_dp)
    out_total = scatter_sum(out_keep, out_send, order_a, n_dp)
    qkv_total = scatter_sum(qkv_keep, qkv_send, order_b, n_dp)
    mine = qkv_total.shape[0]
    qkv_total = qkv_total.reshape(mine, pairs, 3, LANES).transpose(2, 0, 1, 3).reshape(3, mine, local)
    return (
        output,
        tokens_grad,
        last_vectors[0],
        last_vectors[1],
        jnp.transpose(qkv_total, (1, 0, 2)),
        qv_sum,
        out_total.T,
        middle_vectors[2],
        middle_vectors[0],
        middle_vectors[1],
        up_total,
        middle_vectors[4:].reshape(-1),
        down_total.T,
        middle_vectors[3],
    )


def solution(mesh):
    return jax.shard_map(
        functools.partial(per_device, mesh.shape["dp"]),
        mesh=mesh,
        in_specs=(
            P("dp", None),
            P("dp", None),
            P("dp", None),
            P(),
            P(),
            P(None, None, "mp"),
            P(None, "mp"),
            P("mp", None),
            P(),
            P(),
            P(),
            P(None, "mp"),
            P("mp"),
            P("mp", None),
            P(),
        ),
        out_specs=(
            P("dp", None),
            P("dp", None),
            P(),
            P(),
            P("dp", None, "mp"),
            P(None, "mp"),
            P("mp", "dp"),
            P(),
            P(),
            P(),
            P("dp", "mp"),
            P("mp"),
            P("mp", "dp"),
            P(),
        ),
        check_vma=False,
    )
```

```python
import functools

import jax
import jax.numpy as jnp
from jax import lax
from jax.experimental import pallas as pl
from jax.experimental.pallas import tpu as pltpu
from jax.sharding import PartitionSpec as P

HEAD_DIM = 64
EPSILON = 1e-06
MASKED = 1e30
LANES = 128
TOTALS_AT = 32
bf16 = jnp.bfloat16
f32 = jnp.float32


class Given:
    def __init__(self, array, kind, pieces=1, columns=None):
        self.array, self.kind, self.pieces, self.columns = array, kind, pieces, columns

    @property
    def shape(self):
        if self.columns is None:
            return self.array.shape
        return (self.array.shape[0], self.columns[1])


class Made:
    def __init__(self, shape, dtype, kind, pieces=1):
        self.shape, self.dtype, self.kind, self.pieces = shape, dtype, kind, pieces


def piece_span(piece, rows):
    if isinstance(piece, int):
        return pl.ds(piece * rows, rows)
    return pl.ds(pl.multiple_of(piece * rows, rows), rows)


class Arriving:
    def __init__(self, ref, source=None, semaphores=None, pieces=1, columns=None):
        self.ref, self.source, self.semaphores, self.pieces = ref, source, semaphores, pieces
        self.pending, self.columns = source is not None, columns

    def copy(self, piece):
        span = piece_span(piece, self.ref.shape[0] // self.pieces)
        source = self.source.at[span]
        if self.columns is not None:
            source = self.source.at[span, pl.ds(*self.columns)]
        return pltpu.make_async_copy(source, self.ref.at[span], self.semaphores.at[piece])

    def ready(self, piece):
        if self.source is not None:
            self.pending = False
            self.copy(piece).wait()
        return self.ref

    def __call__(self):
        if self.pending:
            for piece in range(self.pieces):
                self.copy(piece).wait()
            self.pending = False
        return self.ref


class Leaving:
    def __init__(self, ref, target, semaphores, pieces):
        self.ref, self.target, self.semaphores, self.pieces = ref, target, semaphores, pieces
        self.started = False

    def copy(self, piece):
        span = piece_span(piece, self.ref.shape[0] // self.pieces)
        return pltpu.make_async_copy(
            self.ref.at[span], self.target.at[span], self.semaphores.at[piece]
        )

    def send(self, piece=0):
        self.started = True
        self.copy(piece).start()

    def finish(self):
        if not self.started:
            for piece in range(self.pieces):
                self.send(piece)

    def wait(self):
        for piece in range(self.pieces):
            self.copy(piece).wait()


class Staying:
    def __init__(self, ref):
        self.ref = ref

    def send(self, piece=0):
        pass


pins = {"v": pltpu.VMEM, "h": pltpu.HBM, "c": pltpu.HBM}


def pinned(given):
    if given.kind in "sw":
        return given.array
    return pltpu.with_memory_space_constraint(given.array, pins[given.kind])


class Chain:
    last = None


def call(chain, kernel, name, outs, args, scratch=(), flops=0, limit=9):
    if chain.last is not None and all(g.array is not chain.last for g in args):
        args = [*args, Given(chain.last, "w")]
    near = [g for g in args if g.kind == "h"]
    far = [m for m in outs if m.kind == "h"]
    copied = [m for m in outs if m.kind in "hc"]
    scratches = [pltpu.VMEM(g.shape, g.array.dtype) for g in near]
    scratches += [pltpu.VMEM(m.shape, m.dtype) for m in far]
    scratches += [pltpu.SemaphoreType.DMA((g.pieces,)) for g in near]
    scratches += [pltpu.SemaphoreType.DMA((m.pieces,)) for m in copied]

    def body(*refs):
        refs = list(refs)

        def take(count):
            taken = refs[:count]
            del refs[:count]
            return taken

        ins, results = take(len(args)), take(len(outs))
        arrivals, departures = take(len(near)), take(len(far))
        ready, gone = take(len(near)), take(len(copied))
        given, made = [], []
        for g, ref in zip(args, ins):
            if g.kind == "h":
                given.append(Arriving(arrivals.pop(0), ref, ready.pop(0), g.pieces, g.columns))
            elif g.kind != "w":
                given.append(ref if g.kind == "s" else Arriving(ref))
        waiting = [one for one in given if isinstance(one, Arriving) and one.pending]
        for piece in range(max((one.pieces for one in waiting), default=0)):
            for one in waiting:
                if piece < one.pieces:
                    one.copy(piece).start()
        for m, ref in zip(outs, results):
            if m.kind == "h":
                made.append(Leaving(departures.pop(0), ref, gone.pop(0), m.pieces))
            elif m.kind == "c":
                made[-1] = Leaving(made[-1].ref, ref, gone.pop(0), m.pieces)
            else:
                made.append(Staying(ref))
        kernel(given, made, *refs)
        for one in waiting:
            one()
        leaving = [one for one in made if isinstance(one, Leaving)]
        for one in leaving:
            one.finish()
        for one in leaving:
            one.wait()

    spaces = {"s": pltpu.SMEM, "v": pltpu.VMEM, "h": pltpu.HBM, "c": pltpu.HBM, "w": pl.ANY}
    results = pl.pallas_call(
        body,
        name=name,
        out_shape=tuple(pins[m.kind](m.shape, m.dtype) for m in outs),
        in_specs=[pl.BlockSpec(memory_space=spaces[g.kind]) for g in args],
        out_specs=tuple(pl.BlockSpec(memory_space=spaces[m.kind]) for m in outs),
        scratch_shapes=[*scratches, *scratch],
        compiler_params=pltpu.CompilerParams(vmem_limit_bytes=limit << 20),
        cost_estimate=pl.CostEstimate(flops=int(flops), bytes_accessed=1, transcendentals=0),
    )(*(pinned(g) for g in args))
    chain.last = min(results, key=lambda result: result.size * result.dtype.itemsize)
    return results


def dot(a, b):
    return jnp.dot(a, b, preferred_element_type=f32)


def dot_t(a, b):
    return lax.dot_general(a, b, (((1,), (1,)), ((), ())), preferred_element_type=f32)


def lane_of(shape):
    return lax.broadcasted_iota(jnp.int32, shape, 1)


def head_half(values, half):
    return jnp.where(lane_of(values.shape) // HEAD_DIM == half, values, jnp.zeros_like(values))


def normalize(values):
    centered = values - jnp.mean(values, axis=-1, keepdims=True)
    variance = jnp.mean(centered * centered, axis=-1, keepdims=True)
    inverse = lax.rsqrt(variance + EPSILON)
    return centered * inverse, inverse


def norm_back(grad_out, normed, inverse, gain):
    scaled = grad_out * gain
    return inverse * (
        scaled
        - jnp.mean(scaled, axis=-1, keepdims=True)
        - normed * jnp.mean(scaled * normed, axis=-1, keepdims=True)
    )


def column_sum(values):
    return jnp.sum(values, axis=0, keepdims=True)


def rows_used(lengths):
    used = jnp.int32(0)
    for slot in range(lengths.shape[1]):
        used = used + lengths[0, slot]
    return used


def row_span(index, size):
    return pl.ds(pl.multiple_of(index * size, size), size)


def vector(ref):
    return ref[...][None, :]


def attend(queries, keys, values, id_q, id_k, mixed, features, block, shifted):
    lane = lane_of((block, LANES))

    @pl.loop(0, queries.shape[0] // block)
    def _(index):
        span = row_span(index, block)
        ids = id_q[span, :]
        feature = ids.astype(f32)
        for pair in range(queries.shape[1] // LANES):
            cols = slice(pair * LANES, (pair + 1) * LANES)
            wide_keys = jnp.concatenate([keys[:, cols], id_k[...]], axis=1)
            query, value = queries[span, cols], values[:, cols]
            total = None
            inverses = []
            for half in range(2):
                wide_query = jnp.concatenate([head_half(query, half), ids], axis=1)
                scores = dot_t(wide_query, wide_keys)
                largest = 0.0
                if shifted:
                    largest = jnp.max(scores, axis=1, keepdims=True)
                    scores = scores - largest
                exponent = jnp.exp(scores)
                totals = jnp.sum(exponent, axis=1, keepdims=True)
                term = dot(exponent.astype(bf16), head_half(value, half))
                total = term if total is None else total + term
                inverses.append(1.0 / totals)
                rest = -(largest + jnp.log(totals))
                for piece in range(3):
                    part_of = rest.astype(bf16).astype(f32)
                    rest = rest - part_of
                    at = TOTALS_AT + 3 * (2 * pair + half) + piece
                    feature = jnp.where(lane == at, part_of, feature)
            mixed.ref[span, cols] = (
                total * jnp.where(lane < HEAD_DIM, inverses[0], inverses[1])
            ).astype(bf16)
        features[span, :] = feature.astype(bf16)
        mixed.send(index)


def largest_norms(array):
    found = jnp.zeros((1, LANES), f32)
    for start in range(0, array.shape[1], LANES):
        values = array[:, start : start + LANES].astype(f32)
        squares = values * values
        found = jnp.maximum(found, jnp.max(jnp.sum(squares, axis=1, keepdims=True), axis=0, keepdims=True))
    return jnp.max(found)


def qkv_kernel(given, made):
    lengths, gain, bias, tokens, weight, qv_bias, out_weight = given
    hidden, queries, keys, values, id_k, mixed, features, part = made[:8]
    rows = tokens.ref.shape[0]
    slots = lengths.shape[1]
    lane = lane_of((1, LANES))
    starts = jnp.where(lane == 0, 0, rows)
    ends = jnp.full((1, LANES), rows, jnp.int32)
    running = jnp.int32(0)
    for slot in range(slots):
        running = running + lengths[0, slot]
        ends = jnp.where(lane == slot, running, ends)
        starts = jnp.where(lane == slot + 1, running, starts)
    scale = HEAD_DIM**-0.5
    block = rows // tokens.pieces
    gain, bias = gain(), bias()

    @pl.loop(0, tokens.pieces)
    def _(index):
        span = row_span(index, block)
        row = index * block + lax.broadcasted_iota(jnp.int32, (block, LANES), 0)
        same = (row >= starts) & (row < ends)
        features.ref[span, :] = same.astype(f32).astype(bf16)
        id_k.ref[span, :] = jnp.where(same | (lane > slots), 0.0, -MASKED).astype(bf16)
        normed, _ = normalize(tokens.ready(index)[span, :].astype(f32))
        hidden.ref[span, :] = (normed * vector(gain) + vector(bias)).astype(bf16)
        hidden.send(index)
        id_k.send(index)

    weight, qv_bias = weight(), qv_bias()

    @pl.loop(0, tokens.pieces)
    def _(index):
        span = row_span(index, block)
        low = hidden.ref[span, :]
        raised = (dot(low, weight[0]) + qv_bias[0:1, :]).astype(bf16)
        queries.ref[span, :] = (raised.astype(f32) * scale).astype(bf16)
        keys.ref[span, :] = dot(low, weight[1]).astype(bf16)
        values.ref[span, :] = (dot(low, weight[2]) + qv_bias[1:2, :]).astype(bf16)
        for one in (queries, keys, values):
            one.send(index)

    bounded = largest_norms(queries.ref) * largest_norms(keys.ref) <= 1600.0
    operands = (queries.ref, keys.ref, values.ref, features.ref, id_k.ref, mixed, features.ref)

    @pl.when(bounded)
    def _():
        attend(*operands, rows // 2, False)

    @pl.when(jnp.logical_not(bounded))
    def _():
        attend(*operands, rows // 2, True)

    out_weight = out_weight()

    @pl.loop(0, 4)
    def _(index):
        span = row_span(index, rows // 4)
        part.ref[span, :] = dot(mixed.ref[span, :], out_weight[...]).astype(bf16)
        part.send(index)


def mlp_kernel(blocks, given, made, ordered):
    lengths, place, out_bias, gain, bias, tokens, mine, other, up_bias, up, down, cotangent = given
    hidden, normed_two, inverse_two, grad_mlp, active_out, grad_pre, part, down_bias_grad, keep, send = made
    rows = hidden.ref.shape[0]
    used = rows_used(lengths)
    block, tile = rows // tokens.pieces, 512
    down_bias_grad.ref[...] = jnp.zeros_like(down_bias_grad.ref)
    out_bias, gain, bias = out_bias(), gain(), bias()

    @pl.loop(0, rows // block)
    def _(index):
        span = row_span(index, block)
        for one in (tokens, mine, other):
            one.ready(index)
        after = tokens.ref[span, :].astype(f32) + (
            mine.ref[span, :].astype(f32) + other.ref[span, :].astype(f32) + vector(out_bias)
        )
        normed, inverse = normalize(after)
        normed_two.ref[span, :] = normed
        inverse_two.ref[span, :] = jnp.broadcast_to(inverse, (block, LANES))
        hidden.ref[span, :] = (normed * vector(gain) + vector(bias)).astype(bf16)
        row = index * block + lax.broadcasted_iota(jnp.int32, (block, 1), 0)
        grad = jnp.where(row < used, cotangent.ready(index)[span, :].astype(f32), 0.0)
        down_bias_grad.ref[...] += column_sum(grad)
        grad_mlp.ref[span, :] = grad.astype(bf16)
        for one in (hidden, normed_two, inverse_two, grad_mlp):
            one.send(index)

    up_bias, up, down = up_bias(), up(), down()

    @pl.loop(0, rows // block)
    def _(index):
        span = row_span(index, block)
        low, grad = hidden.ref[span, :], grad_mlp.ref[span, :]
        total = None
        for start in range(0, up.shape[1], tile):
            cols = slice(start, start + tile)
            pre = dot(low, up[:, cols]) + up_bias[cols][None, :]
            square = pre * pre
            inner = pre * (0.7978845608028654 + (0.7978845608028654 * 0.044715) * square)
            share = 0.5 + 0.5 * jnp.tanh(inner)
            active = pre * share
            active_out.ref[span, cols] = active.astype(bf16)
            slope = share + (active * (1.0 - share)) * (
                (2 * 0.7978845608028654) + (6 * 0.7978845608028654 * 0.044715) * square
            )
            grad_low = (dot_t(grad, down[cols, :]) * slope).astype(bf16)
            grad_pre.ref[span, cols] = grad_low
            term = dot_t(grad_low, up[:, cols])
            total = term if total is None else total + term
        active_out.send(index)
        part.ref[span, :] = total.astype(bf16)

    order_columns(grad_mlp.ref[...], place, ordered, blocks)
    weight_grad(ordered, column_tiles(active_out.ref, 512), keep, send)


def down_kernel(given, made):
    weight, activated = given
    part = made[0]
    rows = activated.ref.shape[0] // 4
    weight = weight()
    for index in range(4):
        span = slice(index * rows, (index + 1) * rows)
        part.ref[span, :] = dot(activated.ready(index)[span, :], weight[...]).astype(bf16)
        part.send(index)


def order_columns(values, place, ordered, blocks):
    turned = values.T
    width = turned.shape[0]
    size = width // blocks
    if size % 16:
        ordered[:width, :] = turned
    else:
        for index in range(blocks):
            at = pl.multiple_of(place[index] * size, size)
            ordered[pl.ds(at, size), :] = turned[index * size : (index + 1) * size]
    ordered[width:, :] = jnp.ones((16, turned.shape[1]), bf16)


def weight_grad(ordered, right, keep, send, sums=None):
    width = ordered.shape[0] - 16
    middle = width // 2
    for begin, operand in right:
        cols = slice(begin, begin + operand.shape[1])
        result = dot(ordered[...], operand)
        send.ref[:, cols] = result[middle:width].astype(bf16)
        keep.ref[:, cols] = result[:middle].astype(bf16)
        if sums is not None:
            sums.ref[:, begin - right[0][0] : begin - right[0][0] + operand.shape[1]] = result[
                width : width + 8
            ]


def column_tiles(values, tile):
    return [(at, values[:, at : at + tile]) for at in range(0, values.shape[1], tile)]


def weight_kernel(blocks, given, made, ordered):
    place, left, right = given
    order_columns(left()[...], place, ordered, blocks)
    weight_grad(ordered, column_tiles(right(), 512), *made)


def middle_kernel(blocks, given, made, normed_back, ordered):
    place, gain, norm_mine, norm_other, normed_two, inverse_two, grad_mlp, weight, mixed = given
    resid, grad_mixed, sums, keep, send = made
    rows = norm_mine.ref.shape[0]
    block = 256
    sums.ref[...] = jnp.zeros_like(sums.ref)
    gain = gain()

    @pl.loop(0, rows // block)
    def _(index):
        span = row_span(index, block)
        for one in (normed_two, inverse_two, grad_mlp):
            one.ready(index)
        normed = normed_two.ref[span, :]
        grad_norm = norm_mine.ready(index)[span, :].astype(f32) + norm_other.ready(index)[
            span, :
        ].astype(f32)
        inverse = inverse_two.ref[span, 0:1]
        grad = grad_mlp.ref[span, :].astype(f32) + norm_back(grad_norm, normed, inverse, vector(gain))
        resid.ref[span, :] = grad
        resid.send(index)
        low = grad.astype(bf16)
        normed_back[span, :] = low
        sums.ref[0:1, :] += column_sum(grad_norm * normed)
        sums.ref[1:2, :] += column_sum(grad_norm)
        sums.ref[2:3, :] += column_sum(low.astype(f32))

    grad_mixed.ref[...] = dot_t(normed_back[...], weight()[...]).astype(bf16)
    order_columns(normed_back[...], place, ordered, blocks)
    weight_grad(ordered, [(0, mixed()[...])], keep, send)


def attention_back_kernel(pair, blocks, given, made, wide_keys, turned, key_total, value_total):
    given, before = given[:8], given[8:]
    place, keys, queries, values, id_k, features, grad_mixed, hidden = given
    if pair == 0:
        *made, ordered = made
        ordered = ordered.ref
    queries, keys, values, id_k, features, grad_mixed = (
        one() for one in (queries, keys, values, id_k, features, grad_mixed)
    )
    grads, sums, keep, send = made
    rows = queries.shape[0]
    cols = slice(pair * LANES, (pair + 1) * LANES)
    lane = lane_of((1, LANES))
    key = keys[:, cols]
    turned[...] = key.T
    for half in range(2):
        at = TOTALS_AT + 3 * (2 * pair + half)
        wide_keys[half, :, :LANES] = key
        wide_keys[half, :, LANES:] = id_k[...] + ((lane >= at) & (lane < at + 3)).astype(f32).astype(bf16)
    block = rows // 2
    for index in range(2):
        span = slice(index * block, (index + 1) * block)
        query, grad, feature = queries[span, cols], grad_mixed[span, cols], features[span, :]
        value = values[:, cols]
        key_term = value_term = None
        turned_grads = []
        for half in range(2):
            one_query, one_grad = head_half(query, half), head_half(grad, half)
            probs = jnp.exp(dot_t(wide_keys[half], jnp.concatenate([one_query, feature], axis=1)))
            grad_probs = dot_t(value, one_grad)
            centre = jnp.sum(probs * grad_probs, axis=0, keepdims=True)
            grad_scores = (probs * (grad_probs - centre)).astype(bf16)
            value_one = dot(probs.astype(bf16), one_grad)
            key_one = dot(grad_scores, one_query)
            value_term = value_one if half == 0 else value_term + value_one
            key_term = key_one if half == 0 else key_term + key_one
            turned_grads.append(dot(turned[half * HEAD_DIM : (half + 1) * HEAD_DIM, :], grad_scores))
        if index == 0:
            key_total[...] = key_term
            value_total[...] = value_term
        else:
            grads.ref[:, LANES : 2 * LANES] = (key_total[...] + key_term).astype(bf16)
            grads.ref[:, 2 * LANES :] = (value_total[...] + value_term).astype(bf16)
        grads.ref[span, :LANES] = (jnp.concatenate(turned_grads, axis=0).T * HEAD_DIM**-0.5).astype(bf16)
    if pair == 0:
        order_columns(hidden()[...], place, ordered, blocks)
    else:
        ordered = hidden()
    at = 0
    for index in range(0, len(before), 2):
        columns = before[index].ref.shape[1]
        for target, source in zip((keep, send), before[index : index + 2]):
            target.ref[:, at : at + columns] = source()[...]
        at += columns
    weight_grad(ordered, [(at, grads.ref[...])], keep, send, sums)


def first_kernel(given, made):
    *grads, weight = given
    weight, part = weight(), made[0]
    rows = part.ref.shape[0] // 4
    grads = [one() for one in grads]
    for index in range(4):
        span = slice(index * rows, (index + 1) * rows)
        operand = jnp.concatenate(
            [one[span, kind * LANES : (kind + 1) * LANES] for kind in range(3) for one in grads], axis=1
        )
        full = jnp.concatenate([weight[kind] for kind in range(3)], axis=1)
        part.ref[span, :] = dot_t(operand, full).astype(bf16)
        part.send(index)


def last_kernel(given, made):
    gain, tokens, mine, other, resid = given
    out, sums = made
    block = tokens.ref.shape[0] // tokens.pieces
    sums.ref[...] = jnp.zeros_like(sums.ref)
    gain = gain()

    @pl.loop(0, tokens.pieces)
    def _(index):
        span = row_span(index, block)
        for one in (tokens, mine, other, resid):
            one.ready(index)
        normed, inverse = normalize(tokens.ref[span, :].astype(f32))
        grad_first = mine.ref[span, :].astype(f32) + other.ref[span, :].astype(f32)
        out.ref[span, :] = resid.ref[span, :] + norm_back(grad_first, normed, inverse, vector(gain))
        out.send(index)
        sums.ref[0:1, :] += column_sum(grad_first * normed)
        sums.ref[1:2, :] += column_sum(grad_first)


def fold_kernel(given, made):
    keep, came = given
    stays, sent = made
    rows = keep.ref.shape[0] // 4
    for piece in (2, 3, 0, 1):
        span = slice(piece * rows, (piece + 1) * rows)
        total = keep.ready(piece)[span].astype(f32) + came.ready(piece)[span].astype(f32)
        target = sent if piece >= 2 else stays
        target.ref[piece % 2 * rows : (piece % 2 + 1) * rows] = total.astype(target.ref.dtype)
        target.send(piece % 2)


def swap(values, axis, bit, size):
    return lax.ppermute(values, axis, [(i, i ^ (1 << bit)) for i in range(size)])


def all_sum(values, bits, size):
    for bit in bits:
        values = values + swap(values, "dp", bit, size)
    return values


class Flow:
    def __init__(self, orders, size, keep, send):
        self.orders, self.size, self.keep, self.send, self.step = orders, size, keep, send, 0

    def exchange(self):
        pairs = [
            (2 * index + core, 2 * (index ^ (1 << order[self.step])) + core)
            for index in range(self.size)
            for core, order in enumerate(self.orders)
        ]
        self.came = lax.ppermute(self.send, ("dp", "mp"), pairs)
        self.step += 1

    @property
    def done(self):
        return self.step == len(self.orders[0])


def fold(chain, flow):
    rows, columns = flow.keep.shape
    if rows * columns < 1 << 17 or flow.done:
        total = flow.keep.astype(f32) + flow.came.astype(f32)
        if flow.done:
            flow.total = total
        else:
            flow.keep, flow.send = total[: rows // 2], total[rows // 2 :].astype(bf16)
        return
    flow.keep, flow.send = call(
        chain,
        fold_kernel,
        "fold",
        [Made((rows // 2, columns), f32, "v", 2), Made((rows // 2, columns), bf16, "v", 2)],
        [Given(flow.keep, "v", 4), Given(flow.came, "v", 4)],
        limit=4,
    )


def places(orders, size, me, core):
    source = jnp.arange(size, dtype=jnp.int32) ^ me
    found = []
    for order in orders:
        place = jnp.zeros((size,), jnp.int32)
        for step, bit in enumerate(order):
            place = place + (((source >> bit) & 1) << (size.bit_length() - 2 - step))
        found.append(place)
    return jnp.where(core == 0, *found)


def arranged(halves, place, size):
    keep, send = halves
    rows, columns = keep.shape
    if (2 * rows // size) % 16 == 0:
        return halves
    spots = jnp.zeros((size,), jnp.int32).at[place].set(jnp.arange(size, dtype=jnp.int32))
    both = jnp.concatenate(halves, axis=0).reshape(size, 2 * rows // size, columns)[spots]
    both = both.reshape(2 * rows, columns)
    return both[:rows], both[rows:]


def per_device(
    n_dp, tokens, cotangent, lengths, ln1_gain, ln1_bias, qkv_weight, qv_bias, out_weight, out_bias,
    ln2_gain, ln2_bias, up_weight, up_bias, down_weight, down_bias,
):
    chain = Chain()
    rows, width = tokens.shape
    local = qkv_weight.shape[2]
    units = up_weight.shape[1]
    pairs = local // LANES
    me, core = lax.axis_index("dp"), lax.axis_index("mp")
    bits = list(range(n_dp.bit_length() - 1))
    rest = bits[3:]
    near_orders = [[0, 1, 2, *rest], [1, 0, 2, *rest]]
    long_orders = [[2, 0, 1, *rest], [2, 1, 0, *rest]]
    near_place, long_place = (places(orders, n_dp, me, core) for orders in (near_orders, long_orders))
    weight = jnp.transpose(qkv_weight, (1, 0, 2))
    scalars = Given(lengths, "s")
    near = lambda array: Given(array, "v")
    far = lambda array, pieces=1: Given(array, "h", pieces)
    halves = lambda columns: [Made((width // 2, columns), bf16, "v")] * 2
    turned = pltpu.VMEM((width + 16, rows), bf16)

    hidden_one, queries, keys, values, id_k, mixed, features, part = call(
        chain,
        qkv_kernel,
        "qkv_attention",
        [
            Made((rows, width), bf16, "h", 4),
            *[Made((rows, local), bf16, "h", 4)] * 3,
            Made((rows, LANES), bf16, "h", 4),
            Made((rows, local), bf16, "h", 2),
            Made((rows, LANES), bf16, "h"),
            Made((rows, width), bf16, "v", 4),
        ],
        [
            scalars, far(ln1_gain), far(ln1_bias), far(tokens, 4), far(weight), far(qv_bias), far(out_weight)
        ],
        flops=2 * rows * width * 3 * local + 8 * rows * rows * local,
        limit=22,
    )
    other = swap(part, "mp", 0, 2)
    (
        hidden_two, normed_two, inverse_two, grad_mlp, activated, grad_pre, norm_part, down_sums,
        down_keep, down_send,
    ) = call(
        chain,
        functools.partial(mlp_kernel, n_dp),
        "mlp",
        [
            Made((rows, width), bf16, "v"),
            Made((rows, width), f32, "h", 4),
            Made((rows, LANES), f32, "h", 4),
            Made((rows, width), bf16, "h", 4),
            Made((rows, units), bf16, "h", 4),
            Made((rows, units), bf16, "v"),
            Made((rows, width), bf16, "v"),
            Made((1, width), f32, "v"),
            *halves(units),
        ],
        [
            scalars,
            Given(near_place, "s"),
            *map(far, (out_bias, ln2_gain, ln2_bias)),
            far(tokens, 4),
            near(part),
            near(other),
            *map(far, (up_bias, up_weight, down_weight)),
            far(cotangent, 4),
        ],
        scratch=[turned],
        flops=8 * rows * width * units,
        limit=32,
    )
    norm_other = swap(norm_part, "mp", 0, 2)

    def weights(name, left, right, place, with_sums=False):
        return call(
        chain,
            functools.partial(weight_kernel, n_dp),
            name,
            [*halves(units), *[Made((8, units), f32, "v")] * with_sums],
            [Given(place, "s"), near(left), near(right)],
            scratch=[turned],
            flops=2 * rows * width * units,
            limit=12,
        )

    flow_down = Flow(near_orders, n_dp, *arranged((down_keep, down_send), near_place, n_dp))
    flow_down.exchange()
    up_keep, up_send, up_sums = weights("up_grad", hidden_two, grad_pre, long_place, True)
    flow_up = Flow(long_orders, n_dp, *arranged((up_keep, up_send), long_place, n_dp))
    flow_up.exchange()
    resid, grad_mixed, middle_sums, out_keep, out_send = call(
        chain,
        functools.partial(middle_kernel, n_dp),
        "middle",
        [
            Made((rows, width), f32, "h", 4),
            Made((rows, local), bf16, "v"),
            Made((8, width), f32, "v"),
            *halves(local),
        ],
        [
            Given(near_place, "s"),
            far(ln2_gain),
            *map(near, (norm_part, norm_other, normed_two, inverse_two, grad_mlp)),
            far(out_weight),
            near(mixed),
        ],
        scratch=[pltpu.VMEM((rows, width), bf16), turned],
        flops=4 * rows * width * local,
        limit=16,
    )
    grads, sums, halves_qkv = [], [], []
    hiddens = [hidden_one]

    def attention_back(pair, before=()):
        columns = 3 * LANES + sum(keep.shape[1] for keep, _ in before)
        three, sums_one, keep, send, *order = call(
            chain,
            functools.partial(attention_back_kernel, pair, n_dp),
            "attention_back%d" % pair,
            [
                Made((rows, 3 * LANES), bf16, "v"),
                Made((8, 3 * LANES), f32, "v"),
                *halves(columns),
                *[Made((width + 16, rows), bf16, "h")] * (pair == 0),
            ],
            [
                Given(near_place, "s"),
                *map(near, (keys, queries, values, id_k, features, grad_mixed)),
                far(hiddens[-1]),
                *(near(array) for pieces in before for array in pieces),
            ],
            scratch=[
                pltpu.VMEM((2, rows, 2 * LANES), bf16),
                pltpu.VMEM((LANES, rows), bf16),
                pltpu.VMEM((rows, LANES), f32),
                pltpu.VMEM((rows, LANES), f32),
            ],
            flops=4 * 10 * rows * rows * LANES,
            limit=18,
        )
        hiddens.extend(order)
        grads.append(three)
        sums.append(sums_one)
        halves_qkv.append((keep, send))

    def advance(*flows):
        for flow in flows:
            fold(chain, flow)
            if not flow.done:
                flow.exchange()

    attention_back(0)
    advance(flow_down)
    for pair in range(1, pairs - 1):
        last = pair == pairs - 2
        attention_back(pair, [(out_keep, out_send), *halves_qkv] if last else ())
    flow_early = Flow(near_orders, n_dp, *arranged(halves_qkv[-1], near_place, n_dp))
    flow_early.exchange()
    advance(flow_down, flow_up)
    attention_back(pairs - 1)
    flow_late = Flow(near_orders, n_dp, *arranged(halves_qkv[-1], near_place, n_dp))
    flow_late.exchange()
    advance(flow_up, flow_down)
    (first_part,) = call(
        chain,
        first_kernel,
        "first",
        [Made((rows, width), bf16, "v", 4)],
        [*map(near, grads), far(weight)],
        flops=2 * rows * width * 3 * local,
        limit=12,
    )
    first_other = swap(first_part, "mp", 0, 2)
    advance(flow_early)
    (down_part,) = call(
        chain,
        down_kernel,
        "down",
        [Made((rows, width), bf16, "v", 4)],
        [far(down_weight), near(activated)],
        flops=2 * rows * width * units,
        limit=6,
    )
    down_other = swap(down_part, "mp", 0, 2)
    advance(flow_down, flow_up, flow_late)
    tokens_grad, last_sums = call(
        chain,
        last_kernel,
        "last",
        [Made((rows, width), f32, "h", 4), Made((8, width), f32, "v")],
        [far(ln1_gain), far(tokens, 4), near(first_part), near(first_other), far(resid, 4)],
        limit=18,
    )
    qkv_sums = jnp.stack([one[0] for one in sums]).reshape(pairs, 3, LANES)
    qv_sums = jnp.stack([qkv_sums[:, 0], qkv_sums[:, 2]]).reshape(-1, width)
    vectors = jnp.concatenate(
        [last_sums[:2], qv_sums, middle_sums[:3], down_sums, up_sums[0].reshape(-1, width)], axis=0
    )
    vectors = all_sum(vectors, bits, n_dp)
    flows = [flow_late, flow_early, flow_up, flow_down]
    while not all(hasattr(flow, "total") for flow in flows):
        for flow in flows:
            if not hasattr(flow, "total"):
                advance(flow)
    after_attn = tokens.astype(f32) + (part.astype(f32) + other.astype(f32) + out_bias)
    output = (
        after_attn + (down_part.astype(f32) + down_other.astype(f32) + down_bias)
    ).astype(bf16)

    qkv_total = jnp.concatenate([flow_early.total[:, local:], flow_late.total], axis=1)
    mine = qkv_total.shape[0]
    qkv_total = qkv_total.reshape(mine, pairs, 3, LANES).transpose(2, 0, 1, 3).reshape(3, mine, local)
    return (
        output,
        tokens_grad,
        vectors[0],
        vectors[1],
        jnp.transpose(qkv_total, (1, 0, 2)),
        vectors[2:3].reshape(2, local),
        flow_early.total[:, :local].T,
        vectors[5],
        vectors[3],
        vectors[4],
        flow_up.total,
        vectors[7:].reshape(-1),
        flow_down.total.T,
        vectors[6],
    )


def solution(mesh):
    return jax.shard_map(
        functools.partial(per_device, mesh.shape["dp"]),
        mesh=mesh,
        in_specs=(
            P("dp", None),
            P("dp", None),
            P("dp", None),
            P(),
            P(),
            P(None, None, "mp"),
            P(None, "mp"),
            P("mp", None),
            P(),
            P(),
            P(),
            P(None, "mp"),
            P("mp"),
            P("mp", None),
            P(),
        ),
        out_specs=(
            P("dp", None),
            P("dp", None),
            P(),
            P(),
            P("dp", None, "mp"),
            P(None, "mp"),
            P("mp", "dp"),
            P(),
            P(),
            P(),
            P("dp", "mp"),
            P("mp"),
            P("mp", "dp"),
            P(),
        ),
        check_vma=False,
    )
```

```python
import functools

import jax
import jax.numpy as jnp
from jax import lax
from jax.experimental import pallas as pl
from jax.experimental.pallas import tpu as pltpu
from jax.sharding import PartitionSpec as P

HEAD_DIM = 64
EPSILON = 1e-06
MASKED = 1e30
LANES = 128
TOTALS_AT = 32
bf16 = jnp.bfloat16
f32 = jnp.float32


class Given:
    def __init__(self, array, kind, pieces=1, columns=None):
        self.array, self.kind, self.pieces, self.columns = array, kind, pieces, columns

    @property
    def shape(self):
        if self.columns is None:
            return self.array.shape
        return (self.array.shape[0], self.columns[1])


class Made:
    def __init__(self, shape, dtype, kind, pieces=1, source=None):
        self.shape, self.dtype, self.kind, self.pieces, self.source = shape, dtype, kind, pieces, source


def piece_span(piece, rows):
    if isinstance(piece, int):
        return pl.ds(piece * rows, rows)
    return pl.ds(pl.multiple_of(piece * rows, rows), rows)


class Arriving:
    def __init__(self, ref, source=None, semaphores=None, pieces=1, columns=None):
        self.ref, self.source, self.semaphores, self.pieces = ref, source, semaphores, pieces
        self.pending, self.columns = source is not None, columns

    def copy(self, piece):
        span = piece_span(piece, self.ref.shape[0] // self.pieces)
        source = self.source.at[span]
        if self.columns is not None:
            source = self.source.at[span, pl.ds(*self.columns)]
        return pltpu.make_async_copy(source, self.ref.at[span], self.semaphores.at[piece])

    def ready(self, piece):
        if self.source is not None:
            self.pending = False
            self.copy(piece).wait()
        return self.ref

    def __call__(self):
        if self.pending:
            for piece in range(self.pieces):
                self.copy(piece).wait()
            self.pending = False
        return self.ref


class Leaving:
    def __init__(self, ref, target, semaphores, pieces):
        self.ref, self.target, self.semaphores, self.pieces = ref, target, semaphores, pieces
        self.started = False

    def copy(self, piece):
        span = piece_span(piece, self.ref.shape[0] // self.pieces)
        return pltpu.make_async_copy(
            self.ref.at[span], self.target.at[span], self.semaphores.at[piece]
        )

    def send(self, piece=0):
        self.started = True
        self.copy(piece).start()

    def finish(self):
        if not self.started:
            for piece in range(self.pieces):
                self.send(piece)

    def wait(self):
        for piece in range(self.pieces):
            self.copy(piece).wait()


class Staying:
    def __init__(self, ref):
        self.ref = ref

    def send(self, piece=0):
        pass


pins = {"v": pltpu.VMEM, "h": pltpu.HBM, "c": pltpu.HBM, "p": pltpu.VMEM, "q": pltpu.HBM}


def pinned(given):
    if given.kind in "sw":
        return given.array
    return pltpu.with_memory_space_constraint(given.array, pins[given.kind])


class Chain:
    last = None


def call(chain, kernel, name, outs, args, scratch=(), flops=0, limit=9):
    if chain.last is not None and all(g.array is not chain.last for g in args):
        args = [*args, Given(chain.last, "w")]
    ahead = [m for m in outs if m.kind == "p"]
    kernel_args = len(args)
    args = [*args, *(Given(m.source, "q") for m in ahead)]
    near = [g for g in args if g.kind == "h"]
    far = [m for m in outs if m.kind == "h"]
    copied = [m for m in outs if m.kind in "hc"]
    scratches = [pltpu.VMEM(g.shape, g.array.dtype) for g in near]
    scratches += [pltpu.VMEM(m.shape, m.dtype) for m in far]
    scratches += [pltpu.SemaphoreType.DMA((g.pieces,)) for g in near]
    scratches += [pltpu.SemaphoreType.DMA((m.pieces,)) for m in copied]
    scratches += [pltpu.SemaphoreType.DMA(()) for _ in ahead]

    def body(*refs):
        refs = list(refs)

        def take(count):
            taken = refs[:count]
            del refs[:count]
            return taken

        ins, results = take(len(args)), take(len(outs))
        arrivals, departures = take(len(near)), take(len(far))
        ready, gone = take(len(near)), take(len(copied))
        fetched = take(len(ahead))
        given, made, fetches = [], [], []
        for m, result in zip(outs, results):
            if m.kind == "p":
                source = ins[kernel_args + len(fetches)]
                fetches.append(pltpu.make_async_copy(source, result, fetched[len(fetches)]))
        for g, ref in zip(args, ins):
            if g.kind == "h":
                given.append(Arriving(arrivals.pop(0), ref, ready.pop(0), g.pieces, g.columns))
            elif g.kind not in "wq":
                given.append(ref if g.kind == "s" else Arriving(ref))
        waiting = [one for one in given if isinstance(one, Arriving) and one.pending]
        small = [one for one in waiting if len(one.ref.shape) == 1]
        pieced = [one for one in waiting if one.pieces > 1]
        order = [(one, 0) for one in small]
        for piece in range(max((one.pieces for one in pieced), default=0)):
            order += [(one, piece) for one in pieced if piece < one.pieces]
        order += [(one, 0) for one in waiting if one not in small and one not in pieced]
        for one, piece in order:
            one.copy(piece).start()
        for copy in fetches:
            copy.start()
        for m, ref in zip(outs, results):
            if m.kind == "h":
                made.append(Leaving(departures.pop(0), ref, gone.pop(0), m.pieces))
            elif m.kind == "p":
                continue
            elif m.kind == "c":
                made[-1] = Leaving(made[-1].ref, ref, gone.pop(0), m.pieces)
            else:
                made.append(Staying(ref))
        kernel(given, made, *refs)
        for one in waiting:
            one()
        leaving = [one for one in made if isinstance(one, Leaving)]
        for one in leaving:
            one.finish()
        for one in leaving:
            one.wait()
        for copy in fetches:
            copy.wait()

    spaces = {"s": pltpu.SMEM, "v": pltpu.VMEM, "h": pltpu.HBM, "c": pltpu.HBM, "w": pl.ANY, "p": pltpu.VMEM, "q": pltpu.HBM}
    results = pl.pallas_call(
        body,
        name=name,
        out_shape=tuple(pins[m.kind](m.shape, m.dtype) for m in outs),
        in_specs=[pl.BlockSpec(memory_space=spaces[g.kind]) for g in args],
        out_specs=tuple(pl.BlockSpec(memory_space=spaces[m.kind]) for m in outs),
        scratch_shapes=[*scratches, *scratch],
        compiler_params=pltpu.CompilerParams(vmem_limit_bytes=limit << 20),
        cost_estimate=pl.CostEstimate(flops=int(flops), bytes_accessed=1, transcendentals=0),
    )(*(pinned(g) for g in args))
    chain.last = min(results, key=lambda result: result.size * result.dtype.itemsize)
    return results


def dot(a, b):
    return jnp.dot(a, b, preferred_element_type=f32)


def dot_t(a, b):
    return lax.dot_general(a, b, (((1,), (1,)), ((), ())), preferred_element_type=f32)


def lane_of(shape):
    return lax.broadcasted_iota(jnp.int32, shape, 1)


def head_half(values, half):
    return jnp.where(lane_of(values.shape) // HEAD_DIM == half, values, jnp.zeros_like(values))


def normalize(values):
    centered = values - jnp.mean(values, axis=-1, keepdims=True)
    variance = jnp.mean(centered * centered, axis=-1, keepdims=True)
    inverse = lax.rsqrt(variance + EPSILON)
    return centered * inverse, inverse


def norm_back(grad_out, normed, inverse, gain):
    scaled = grad_out * gain
    return inverse * (
        scaled
        - jnp.mean(scaled, axis=-1, keepdims=True)
        - normed * jnp.mean(scaled * normed, axis=-1, keepdims=True)
    )


def column_sum(values):
    return jnp.sum(values, axis=0, keepdims=True)


def rows_used(lengths):
    used = jnp.int32(0)
    for slot in range(lengths.shape[1]):
        used = used + lengths[0, slot]
    return used


def row_span(index, size):
    return pl.ds(pl.multiple_of(index * size, size), size)


def vector(ref):
    return ref[...][None, :]


def log_total_lanes(feature, head, log_total):
    lane = lane_of(feature.shape)
    rest = -log_total
    for piece in range(3):
        part_of = rest.astype(bf16).astype(f32)
        rest = rest - part_of
        feature = jnp.where(lane == TOTALS_AT + 3 * head + piece, part_of, feature)
    return feature


def attend(queries, keys, values, id_k, mixed, features, block):
    lane = lane_of((block, LANES))

    @pl.loop(0, queries.shape[0] // block)
    def _(index):
        span = row_span(index, block)
        ids = features[span, :]
        feature = ids.astype(f32)
        for pair in range(queries.shape[1] // LANES):
            cols = slice(pair * LANES, (pair + 1) * LANES)
            wide_keys = jnp.concatenate([keys[:, cols], id_k[...]], axis=1)
            query, value = queries[span, cols], values[:, cols]
            total = None
            inverses = []
            for half in range(2):
                wide_query = jnp.concatenate([head_half(query, half), ids], axis=1)
                exponent = jnp.exp(dot_t(wide_query, wide_keys))
                totals = jnp.sum(exponent, axis=1, keepdims=True)
                term = dot(exponent.astype(bf16), head_half(value, half))
                total = term if total is None else total + term
                inverses.append(1.0 / totals)
                feature = log_total_lanes(feature, 2 * pair + half, jnp.log(totals))
            mixed[span, cols] = (
                total * jnp.where(lane < HEAD_DIM, inverses[0], inverses[1])
            ).astype(bf16)
        features[span, :] = feature.astype(bf16)


def attend_shifted(queries, keys, values, id_k, mixed, features, block):
    @pl.loop(0, queries.shape[0] // block)
    def _(index):
        span = row_span(index, block)
        ids = jnp.where(lane_of((block, LANES)) < TOTALS_AT, features[span, :], jnp.zeros((), bf16))

        @pl.loop(0, queries.shape[1] // LANES)
        def _(pair):
            cols = row_span(pair, LANES)
            total = None
            for half in range(2):
                wide_query = jnp.concatenate([head_half(queries[span, cols], half), ids], axis=1)
                scores = dot_t(wide_query, jnp.concatenate([keys[:, cols], id_k[...]], axis=1))
                largest = jnp.max(scores, axis=1, keepdims=True)
                exponent = jnp.exp(scores - largest)
                totals = jnp.sum(exponent, axis=1, keepdims=True)
                term = dot(exponent.astype(bf16), head_half(values[:, cols], half)) / totals
                total = term if total is None else total + term
                features[span, :] = log_total_lanes(
                    features[span, :].astype(f32), 2 * pair + half, largest + jnp.log(totals)
                ).astype(bf16)
            mixed[span, cols] = total.astype(bf16)


def largest_norms(array):
    found = jnp.zeros((1, LANES), f32)
    for start in range(0, array.shape[1], LANES):
        values = array[:, start : start + LANES].astype(f32)
        squares = values * values
        found = jnp.maximum(found, jnp.max(jnp.sum(squares, axis=1, keepdims=True), axis=0, keepdims=True))
    return jnp.max(found)


def qkv_kernel(given, made):
    lengths, gain, bias, tokens, weight, qv_bias, out_weight = given
    hidden, queries, keys, values, id_k, mixed, features, part = made[:8]
    rows = tokens.ref.shape[0]
    slots = lengths.shape[1]
    lane = lane_of((1, LANES))
    starts = jnp.where(lane == 0, 0, rows)
    ends = jnp.full((1, LANES), rows, jnp.int32)
    running = jnp.int32(0)
    for slot in range(slots):
        running = running + lengths[0, slot]
        ends = jnp.where(lane == slot, running, ends)
        starts = jnp.where(lane == slot + 1, running, starts)
    scale = HEAD_DIM**-0.5
    block = rows // tokens.pieces
    gain, bias = gain(), bias()

    @pl.loop(0, tokens.pieces)
    def _(index):
        span = row_span(index, block)
        row = index * block + lax.broadcasted_iota(jnp.int32, (block, LANES), 0)
        same = (row >= starts) & (row < ends)
        features.ref[span, :] = same.astype(f32).astype(bf16)
        id_k.ref[span, :] = jnp.where(same | (lane > slots), 0.0, -MASKED).astype(bf16)
        normed, _ = normalize(tokens.ready(index)[span, :].astype(f32))
        hidden.ref[span, :] = (normed * vector(gain) + vector(bias)).astype(bf16)
        hidden.send(index)
        id_k.send(index)

    weight, qv_bias = weight(), qv_bias()

    @pl.loop(0, tokens.pieces)
    def _(index):
        span = row_span(index, block)
        low = hidden.ref[span, :]
        raised = (dot(low, weight[0]) + qv_bias[0:1, :]).astype(bf16)
        queries.ref[span, :] = (raised.astype(f32) * scale).astype(bf16)
        keys.ref[span, :] = dot(low, weight[1]).astype(bf16)
        values.ref[span, :] = (dot(low, weight[2]) + qv_bias[1:2, :]).astype(bf16)
        for one in (queries, keys, values):
            one.send(index)

    bounded = largest_norms(queries.ref) * largest_norms(keys.ref) <= 1600.0
    operands = [one.ref for one in (queries, keys, values, id_k, mixed, features)]

    @pl.when(bounded)
    def _():
        attend(*operands, rows // 2)

    @pl.when(jnp.logical_not(bounded))
    def _():
        attend_shifted(*operands, LANES)

    mixed.send()
    features.send()
    out_weight = out_weight()

    @pl.loop(0, 4)
    def _(index):
        span = row_span(index, rows // 4)
        part.ref[span, :] = dot(mixed.ref[span, :], out_weight[...]).astype(bf16)
        part.send(index)


def mlp_kernel(blocks, given, made, ordered, grad_mlp):
    lengths, place, out_bias, gain, bias, tokens, mine, other, up_bias, up, down, cotangent = given
    hidden, normed_two, inverse_two, active_out, grad_pre, part, down_bias_grad, keep, send = made
    rows = hidden.ref.shape[0]
    used = rows_used(lengths)
    block, tile = rows // 4, 512
    down_bias_grad.ref[...] = jnp.zeros_like(down_bias_grad.ref)
    out_bias, gain, bias = out_bias(), gain(), bias()

    @pl.loop(0, rows // block)
    def _(index):
        span = row_span(index, block)
        for one in (tokens, mine, other):
            one.ready(index)
        after = tokens.ref[span, :].astype(f32) + (
            mine.ref[span, :].astype(f32) + other.ref[span, :].astype(f32) + vector(out_bias)
        )
        normed, inverse = normalize(after)
        normed_two.ref[span, :] = normed.astype(bf16)
        inverse_two.ref[span, :] = jnp.broadcast_to(inverse, (block, LANES))
        hidden.ref[span, :] = (normed * vector(gain) + vector(bias)).astype(bf16)
        row = index * block + lax.broadcasted_iota(jnp.int32, (block, 1), 0)
        grad = jnp.where(row < used, cotangent.ready(index)[span, :].astype(f32), 0.0)
        down_bias_grad.ref[...] += column_sum(grad)
        grad_mlp[span, :] = grad.astype(bf16)
        for one in (normed_two, inverse_two):
            one.send(index)

    up_bias, up, down = up_bias(), up(), down()

    block = rows // 2

    @pl.loop(0, rows // block)
    def _(index):
        span = row_span(index, block)
        low, grad = hidden.ref[span, :], grad_mlp[span, :]
        total = None
        for start in range(0, up.shape[1], tile):
            cols = slice(start, start + tile)
            pre = dot(low, up[:, cols]) + up_bias[cols][None, :]
            square = pre * pre
            inner = pre * (0.7978845608028654 + (0.7978845608028654 * 0.044715) * square)
            share = 0.5 + 0.5 * jnp.tanh(inner)
            active = pre * share
            active_out.ref[span, cols] = active.astype(bf16)
            slope = share + (active * (1.0 - share)) * (
                (2 * 0.7978845608028654) + (6 * 0.7978845608028654 * 0.044715) * square
            )
            grad_low = (dot_t(grad, down[cols, :]) * slope).astype(bf16)
            grad_pre.ref[span, cols] = grad_low
            term = dot_t(grad_low, up[:, cols])
            total = term if total is None else total + term
        active_out.send(index)
        part.ref[span, :] = total.astype(bf16)

    order_columns(grad_mlp[...], place, ordered, blocks)
    weight_grad(ordered, active_out.ref, keep, send)


def down_kernel(given, made):
    weight, activated = given
    part = made[0]
    rows = activated.ref.shape[0] // 4
    weight = weight()
    activated = activated()

    @pl.loop(0, 4)
    def _(index):
        span = row_span(index, rows)
        part.ref[span, :] = dot(activated[span, :], weight[...]).astype(bf16)


def order_columns(values, place, ordered, blocks):
    turned = values.T
    width = turned.shape[0]
    size = width // blocks
    if size % 16:
        ordered[:width, :] = turned
    else:
        for index in range(blocks):
            at = pl.multiple_of(place[index] * size, size)
            ordered[pl.ds(at, size), :] = turned[index * size : (index + 1) * size]
    ordered[width:, :] = jnp.ones((16, turned.shape[1]), bf16)


def weight_grad(ordered, right, keep, send, sums=None, at=0):
    width = ordered.shape[0] - 16
    middle, columns = width // 2, right.shape[1]
    tile = 512 if columns % 512 == 0 else columns

    def one(start):
        source = pl.ds(start, tile)
        target = pl.ds(at + start, tile)
        result = dot(ordered[...], right[:, source])
        send.ref[:, target] = result[middle:width].astype(bf16)
        keep.ref[:, target] = result[:middle].astype(bf16)
        if sums is not None:
            sums.ref[:, source] = result[width : width + 8]

    if tile == columns:
        one(0)
    else:

        @pl.loop(0, columns // tile)
        def _(index):
            one(pl.multiple_of(index * tile, tile))


def weight_kernel(blocks, given, made, ordered):
    place, left, right = given
    order_columns(left()[...], place, ordered, blocks)
    weight_grad(ordered, right(), *made)


def middle_kernel(blocks, given, made, normed_back, ordered):
    lengths, place, gain, norm_mine, norm_other, normed_two, inverse_two, cotangent, weight, mixed = given
    used = rows_used(lengths)
    resid, grad_mixed, sums, keep, send = made
    rows = norm_mine.ref.shape[0]
    block = 256
    sums.ref[...] = jnp.zeros_like(sums.ref)
    gain = gain()

    @pl.loop(0, rows // block)
    def _(index):
        span = row_span(index, block)
        for one in (normed_two, inverse_two, cotangent):
            one.ready(index)
        normed = normed_two.ref[span, :].astype(f32)
        grad_norm = norm_mine.ready(index)[span, :].astype(f32) + norm_other.ready(index)[
            span, :
        ].astype(f32)
        inverse = inverse_two.ref[span, 0:1]
        row = index * block + lax.broadcasted_iota(jnp.int32, (block, 1), 0)
        grad = jnp.where(row < used, cotangent.ref[span, :].astype(f32), 0.0)
        grad = grad + norm_back(grad_norm, normed, inverse, vector(gain))
        resid.ref[span, :] = grad
        resid.send(index)
        low = grad.astype(bf16)
        normed_back[span, :] = low
        sums.ref[0:1, :] += column_sum(grad_norm * normed)
        sums.ref[1:2, :] += column_sum(grad_norm)
        sums.ref[2:3, :] += column_sum(low.astype(f32))

    grad_mixed.ref[...] = dot_t(normed_back[...], weight()[...]).astype(bf16)
    order_columns(normed_back[...], place, ordered, blocks)
    weight_grad(ordered, mixed(), keep, send)


def attention_back_kernel(pair, blocks, given, made, wide_keys, turned, key_total, value_total):
    given, before = given[:8], given[8:]
    place, keys, queries, values, id_k, features, grad_mixed, hidden = given
    if pair == 0:
        *made, ordered = made
        ordered = ordered.ref
    queries, keys, values, id_k, features, grad_mixed = (
        one() for one in (queries, keys, values, id_k, features, grad_mixed)
    )
    grads, sums, keep, send = made
    rows = queries.shape[0]
    cols = slice(pair * LANES, (pair + 1) * LANES)
    lane = lane_of((1, LANES))
    key = keys[:, cols]
    turned[...] = key.T
    for half in range(2):
        at = TOTALS_AT + 3 * (2 * pair + half)
        wide_keys[half, :, :LANES] = key
        wide_keys[half, :, LANES:] = id_k[...] + ((lane >= at) & (lane < at + 3)).astype(f32).astype(bf16)
    block = rows // 2
    key_total[...] = jnp.zeros_like(key_total)
    value_total[...] = jnp.zeros_like(value_total)

    @pl.loop(0, 2)
    def _(index):
        span = row_span(index, block)
        query, grad, feature = queries[span, cols], grad_mixed[span, cols], features[span, :]
        value = values[:, cols]
        key_term = value_term = None
        turned_grads = []
        for half in range(2):
            one_query, one_grad = head_half(query, half), head_half(grad, half)
            probs = jnp.exp(dot_t(wide_keys[half], jnp.concatenate([one_query, feature], axis=1)))
            grad_probs = dot_t(value, one_grad)
            centre = jnp.sum(probs * grad_probs, axis=0, keepdims=True)
            grad_scores = (probs * (grad_probs - centre)).astype(bf16)
            value_one = dot(probs.astype(bf16), one_grad)
            key_one = dot(grad_scores, one_query)
            value_term = value_one if half == 0 else value_term + value_one
            key_term = key_one if half == 0 else key_term + key_one
            turned_grads.append(dot(turned[half * HEAD_DIM : (half + 1) * HEAD_DIM, :], grad_scores))
        key_total[...] += key_term
        value_total[...] += value_term
        grads.ref[span, :LANES] = (jnp.concatenate(turned_grads, axis=0).T * HEAD_DIM**-0.5).astype(bf16)

    grads.ref[:, LANES : 2 * LANES] = key_total[...].astype(bf16)
    grads.ref[:, 2 * LANES :] = value_total[...].astype(bf16)
    if pair == 0:
        order_columns(hidden()[...], place, ordered, blocks)
    else:
        ordered = hidden()
    at = 0
    for index in range(0, len(before), 2):
        columns = before[index].ref.shape[1]
        for target, source in zip((keep, send), before[index : index + 2]):
            target.ref[:, at : at + columns] = source()[...]
        at += columns
    weight_grad(ordered, grads.ref, keep, send, sums, at)


def first_kernel(given, made):
    *grads, weight = given
    weight, part = weight(), made[0]
    rows = part.ref.shape[0] // 4
    grads = [one() for one in grads]
    @pl.loop(0, 4)
    def _(index):
        span = row_span(index, rows)
        operand = jnp.concatenate(
            [one[span, kind * LANES : (kind + 1) * LANES] for kind in range(3) for one in grads], axis=1
        )
        full = jnp.concatenate([weight[kind] for kind in range(3)], axis=1)
        part.ref[span, :] = dot_t(operand, full).astype(bf16)


def last_kernel(given, made):
    gain, tokens, mine, other, resid, *sums = given
    out, vectors = made
    middle_sums, down_sums, up_sums, *pair_sums = (one()[...] for one in sums)
    block = tokens.ref.shape[0] // 4
    width = tokens.ref.shape[1]
    vectors.ref[...] = jnp.zeros_like(vectors.ref)
    gain, tokens, mine, other, resid = gain(), tokens(), mine(), other(), resid()

    @pl.loop(0, 4)
    def _(index):
        span = row_span(index, block)
        normed, inverse = normalize(tokens[span, :].astype(f32))
        grad_first = mine[span, :].astype(f32) + other[span, :].astype(f32)
        out.ref[span, :] = resid[span, :] + norm_back(grad_first, normed, inverse, vector(gain))
        out.send(index)
        vectors.ref[0:1, :] += column_sum(grad_first * normed)
        vectors.ref[1:2, :] += column_sum(grad_first)

    pairs = len(pair_sums)
    for pair, one in enumerate(pair_sums):
        for kind, start in ((0, 0), (2, pairs * LANES)):
            at = start + pair * LANES
            vectors.ref[2:3, at : at + LANES] = one[0:1, kind * LANES : (kind + 1) * LANES]
    vectors.ref[3:6, :] = middle_sums[0:3, :]
    vectors.ref[6:7, :] = down_sums
    for index in range(up_sums.shape[1] // width):
        vectors.ref[7 + index : 8 + index, :] = up_sums[0:1, index * width : (index + 1) * width]


def fold_kernel(joined, folded, given, made):
    at = 0
    for index in range(len(given) // 2):
        keep, came = given[2 * index](), given[2 * index + 1]()
        stays, sent = made[:2] if joined else made[2 * index : 2 * index + 2]
        cols = slice(at, at + keep.shape[1])
        at += keep.shape[1] if joined else 0
        if index < folded:
            stays.ref[:, cols] = keep[...]
            sent.ref[:, cols] = came[...]
            continue
        middle = keep.shape[0] // 2
        sent.ref[:, cols] = (keep[middle:].astype(f32) + came[middle:].astype(f32)).astype(bf16)
        stays.ref[:, cols] = keep[:middle].astype(f32) + came[:middle].astype(f32)


def add_kernel(given, made):
    made[0].ref[...] = given[0]()[...] + given[1]()[...]


def output_kernel(given, made):
    out_bias, down_bias, tokens, part, other, down_part, down_other = given
    out = made[0]
    out_bias, down_bias, down_part, down_other = out_bias(), down_bias(), down_part(), down_other()
    block = out.ref.shape[0] // out.pieces

    @pl.loop(0, out.pieces)
    def _(index):
        span = row_span(index, block)
        for one in (tokens, part, other):
            one.ready(index)
        after = tokens.ref[span, :].astype(f32) + (
            part.ref[span, :].astype(f32) + other.ref[span, :].astype(f32) + vector(out_bias)
        )
        branch = down_part[span, :].astype(f32) + down_other[span, :].astype(f32) + vector(down_bias)
        out.ref[span, :] = (after + branch).astype(bf16)
        out.send(index)


def final_kernel(given, made):
    keep, came = given
    made[0].ref[...] = keep()[...] + came()[...].astype(f32)


def final_qkv_kernel(given, made):
    qkv, out = made
    keep, came = given
    total = keep()[...] + came()[...].astype(f32)
    local = out.ref.shape[1]
    out.ref[...] = total[:, :local]
    for pair in range(local // LANES):
        for kind in range(3):
            at = local + (3 * pair + kind) * LANES
            qkv.ref[kind, :, pair * LANES : (pair + 1) * LANES] = total[:, at : at + LANES]


def swap(values, axis, bit, size):
    return lax.ppermute(values, axis, [(i, i ^ (1 << bit)) for i in range(size)])


class Flow:
    def __init__(self, orders, size, keep, send):
        self.orders, self.size, self.keep, self.send, self.step = orders, size, keep, send, 0

    def exchange(self):
        pairs = [
            (2 * index + core, 2 * (index ^ (1 << order[self.step])) + core)
            for index in range(self.size)
            for core, order in enumerate(self.orders)
        ]
        self.came = lax.ppermute(self.send, ("dp", "mp"), pairs)
        self.step += 1


def fold(chain, flows, ready=()):
    halved = [(flow.keep.shape[0] // 2, flow.keep.shape[1]) for flow in flows]
    if ready:
        columns = sum(flow.keep.shape[1] for flow in (*ready, *flows))
        halved = [(halved[0][0], columns)]
    outs = []
    for rows, columns in halved:
        outs += [Made((rows, columns), f32, "h" if rows <= 48 else "v"), Made((rows, columns), bf16, "v")]
    pairs = [(flow.keep, flow.send) for flow in ready] + [(flow.keep, flow.came) for flow in flows]
    results = call(
        chain,
        functools.partial(fold_kernel, bool(ready), len(ready)),
        "fold",
        outs,
        [Given(array, "v") for pair in pairs for array in pair],
        limit=8,
    )
    for index in range(len(halved)):
        flows[index].keep, flows[index].send = results[2 * index : 2 * index + 2]


def finish(chain, flow, kernel=final_kernel, shapes=None):
    shapes = [flow.keep.shape] if shapes is None else shapes
    return call(
        chain,
        kernel,
        "final",
        [Made(shape, f32, "h") for shape in shapes],
        [Given(flow.keep, "h"), Given(flow.came, "v")],
        limit=8,
    )


def places(orders, size, me, core):
    source = jnp.arange(size, dtype=jnp.int32) ^ me
    found = []
    for order in orders:
        place = jnp.zeros((size,), jnp.int32)
        for step, bit in enumerate(order):
            place = place + (((source >> bit) & 1) << (size.bit_length() - 2 - step))
        found.append(place)
    return jnp.where(core == 0, *found)


def arranged(halves, place, size):
    keep, send = halves
    rows, columns = keep.shape
    if (2 * rows // size) % 16 == 0:
        return halves
    spots = jnp.zeros((size,), jnp.int32).at[place].set(jnp.arange(size, dtype=jnp.int32))
    both = jnp.concatenate(halves, axis=0).reshape(size, 2 * rows // size, columns)[spots]
    both = both.reshape(2 * rows, columns)
    return both[:rows], both[rows:]


def per_device(
    n_dp, tokens, cotangent, lengths, ln1_gain, ln1_bias, qkv_weight, qv_bias, out_weight, out_bias,
    ln2_gain, ln2_bias, up_weight, up_bias, down_weight, down_bias,
):
    chain = Chain()
    rows, width = tokens.shape
    local = qkv_weight.shape[2]
    units = up_weight.shape[1]
    pairs = local // LANES
    me, core = lax.axis_index("dp"), lax.axis_index("mp")
    bits = list(range(n_dp.bit_length() - 1))
    rest = bits[3:]
    near_orders = [[0, 1, 2, *rest], [1, 0, 2, *rest]]
    long_orders = [[2, 0, 1, *rest], [2, 1, 0, *rest]]
    near_place, long_place = (places(orders, n_dp, me, core) for orders in (near_orders, long_orders))
    weight = jnp.transpose(qkv_weight, (1, 0, 2))
    scalars = Given(lengths, "s")
    near = lambda array: Given(array, "v")
    far = lambda array, pieces=1: Given(array, "h", pieces)
    fetch = lambda array: Made(array.shape, array.dtype, "p", source=array)
    halves = lambda columns: [Made((width // 2, columns), bf16, "v")] * 2
    turned = pltpu.VMEM((width + 16, rows), bf16)

    hidden_one, queries, keys, values, id_k, mixed, features, part = call(
        chain,
        qkv_kernel,
        "qkv_attention",
        [
            Made((rows, width), bf16, "h", 4),
            *[Made((rows, local), bf16, "h", 4)] * 3,
            Made((rows, LANES), bf16, "h", 4),
            Made((rows, local), bf16, "h"),
            Made((rows, LANES), bf16, "h"),
            Made((rows, width), bf16, "v", 4),
        ],
        [
            scalars, far(ln1_gain), far(ln1_bias), far(tokens, 4), far(weight), far(qv_bias), far(out_weight)
        ],
        flops=2 * rows * width * 3 * local + 8 * rows * rows * local,
        limit=28,
    )
    other = swap(part, "mp", 0, 2)
    (
        hidden_two, normed_two, inverse_two, activated, grad_pre, norm_part, down_sums,
        down_keep, down_send,
    ) = call(
        chain,
        functools.partial(mlp_kernel, n_dp),
        "mlp",
        [
            Made((rows, width), bf16, "v"),
            Made((rows, width), bf16, "h", 4),
            Made((rows, LANES), f32, "h", 4),
            Made((rows, units), bf16, "h", 2),
            Made((rows, units), bf16, "v"),
            Made((rows, width), bf16, "v"),
            Made((1, width), f32, "v"),
            *halves(units),
        ],
        [
            scalars,
            Given(near_place, "s"),
            *map(far, (out_bias, ln2_gain, ln2_bias)),
            far(tokens, 4),
            near(part),
            near(other),
            *map(far, (up_bias, up_weight, down_weight)),
            far(cotangent, 4),
        ],
        scratch=[turned, pltpu.VMEM((rows, width), bf16)],
        flops=8 * rows * width * units,
        limit=30,
    )
    norm_other = swap(norm_part, "mp", 0, 2)

    def weights(name, left, right, place, with_sums=False):
        return call(
        chain,
            functools.partial(weight_kernel, n_dp),
            name,
            [*halves(units), *[Made((8, units), f32, "v")] * with_sums],
            [Given(place, "s"), near(left), near(right)],
            scratch=[turned],
            flops=2 * rows * width * units,
            limit=10,
        )

    flow_down = Flow(near_orders, n_dp, *arranged((down_keep, down_send), near_place, n_dp))
    flow_down.exchange()
    up_keep, up_send, up_sums = weights("up_grad", hidden_two, grad_pre, long_place, True)
    flow_up = Flow(long_orders, n_dp, *arranged((up_keep, up_send), long_place, n_dp))
    flow_up.exchange()
    resid, grad_mixed, middle_sums, out_keep, out_send = call(
        chain,
        functools.partial(middle_kernel, n_dp),
        "middle",
        [
            Made((rows, width), f32, "h", 4),
            Made((rows, local), bf16, "v"),
            Made((8, width), f32, "v"),
            *halves(local),
        ],
        [
            scalars,
            Given(near_place, "s"),
            far(ln2_gain),
            near(norm_part),
            near(norm_other),
            *map(near, (normed_two, inverse_two, cotangent)),
            near(out_weight),
            near(mixed),
        ],
        scratch=[pltpu.VMEM((rows, width), bf16), turned],
        flops=4 * rows * width * local,
        limit=16,
    )
    grads, sums, halves_qkv = [], [], []
    hiddens = [hidden_one]

    def attention_back(pair, before=()):
        columns = 3 * LANES + sum(keep.shape[1] for keep, _ in before)
        three, sums_one, keep, send, *order = call(
            chain,
            functools.partial(attention_back_kernel, pair, n_dp),
            "attention_back%d" % pair,
            [
                Made((rows, 3 * LANES), bf16, "v"),
                Made((8, 3 * LANES), f32, "v"),
                *halves(columns),
                *[Made((width + 16, rows), bf16, "h")] * (pair == 0),
            ],
            [
                Given(near_place, "s"),
                *map(near, (keys, queries, values, id_k, features, grad_mixed)),
                near(hiddens[-1]),
                *(near(array) for pieces in before for array in pieces),
            ],
            scratch=[
                pltpu.VMEM((2, rows, 2 * LANES), bf16),
                pltpu.VMEM((LANES, rows), bf16),
                pltpu.VMEM((rows, LANES), f32),
                pltpu.VMEM((rows, LANES), f32),
            ],
            flops=4 * 10 * rows * rows * LANES,
            limit=18,
        )
        hiddens.extend(order)
        grads.append(three)
        sums.append(sums_one)
        halves_qkv.append((keep, send))

    def exchange(*flows):
        for flow in flows:
            flow.exchange()

    def flow_of(pieces):
        return Flow(near_orders, n_dp, *arranged(pieces, near_place, n_dp))

    flow_out = flow_of((out_keep, out_send))
    exchange(flow_out)
    attention_back(0)
    flow_first = flow_of(halves_qkv[0])
    fold(chain, [flow_down, flow_out])
    exchange(flow_down, flow_first)
    for pair in range(1, pairs - 1):
        attention_back(pair)
    flows_next = [flow_of(pieces) for pieces in halves_qkv[1:]]
    fold(chain, [flow_down, flow_up, flow_first])
    exchange(flow_down, flow_up, *flows_next)
    attention_back(pairs - 1)
    flow_qkv = flow_of(halves_qkv[-1])
    exchange(flow_qkv)
    fold(chain, [flow_down, flow_up, *flows_next])
    (first_part,) = call(
        chain,
        first_kernel,
        "first",
        [Made((rows, width), bf16, "v", 4)],
        [*map(near, grads), near(weight)],
        flops=2 * rows * width * 3 * local,
        limit=10,
    )
    first_other = swap(first_part, "mp", 0, 2)
    fold(chain, [flow_qkv], [flow_out, flow_first, *flows_next])
    exchange(flow_qkv, flow_up)
    (down_part,) = call(
        chain,
        down_kernel,
        "down",
        [Made((rows, width), bf16, "v", 4)],
        [near(down_weight), near(activated)],
        flops=2 * rows * width * units,
        limit=10,
    )
    down_other = swap(down_part, "mp", 0, 2)
    tokens_grad, vectors = call(
        chain,
        last_kernel,
        "last",
        [Made((rows, width), f32, "h", 4), Made((16, width), f32, "v")],
        [
            far(ln1_gain),
            *map(near, (tokens, first_part, first_other, resid, middle_sums, down_sums, up_sums, *sums)),
        ],
        flops=1 << 31,
        limit=14,
    )
    fold(chain, [flow_qkv, flow_up])
    last_step = len(rest) == 1
    exchange(flow_qkv, flow_up, flow_down)

    def all_sum_step(bit):
        nonlocal vectors
        other = swap(vectors, "dp", bit, n_dp)
        (vectors,) = call(
            chain, add_kernel, "add", [Made((16, width), f32, "v")], [near(vectors), near(other)], limit=4
        )

    (output,) = call(
        chain,
        output_kernel,
        "output",
        [Made((rows, width), bf16, "h", 4)],
        [
            far(out_bias), far(down_bias), *(far(array, 4) for array in (tokens, part, other)), near(down_part),
            near(down_other),
        ],
        flops=1 << 31,
        limit=16,
    )
    all_sum_step(bits[0])
    fold(chain, [flow_qkv])
    exchange(flow_qkv)
    all_sum_step(bits[1])
    if last_step:
        (down_total,) = finish(chain, flow_down)
        (up_total,) = finish(chain, flow_up)
    for bit in bits[2:-1]:
        all_sum_step(bit)
    flows = [flow_qkv, flow_up, flow_down]
    for step in range(1, len(rest)):
        fold(chain, flows)
        exchange(*flows)
    if not last_step:
        (down_total,) = finish(chain, flow_down)
        (up_total,) = finish(chain, flow_up)
    mine = width // n_dp
    qkv_total, out_total = finish(
        chain, flow_qkv, final_qkv_kernel, [(3, mine, local), (mine, local)]
    )
    all_sum_step(bits[-1])
    ups = units // width
    return (
        output,
        tokens_grad,
        vectors[0],
        vectors[1],
        jnp.transpose(qkv_total, (1, 0, 2)),
        vectors[2].reshape(2, local),
        out_total.T,
        vectors[5],
        vectors[3],
        vectors[4],
        up_total,
        vectors[7 : 7 + ups].reshape(-1),
        down_total.T,
        vectors[6],
    )


def solution(mesh):
    return jax.shard_map(
        functools.partial(per_device, mesh.shape["dp"]),
        mesh=mesh,
        in_specs=(
            P("dp", None),
            P("dp", None),
            P("dp", None),
            P(),
            P(),
            P(None, None, "mp"),
            P(None, "mp"),
            P("mp", None),
            P(),
            P(),
            P(),
            P(None, "mp"),
            P("mp"),
            P("mp", None),
            P(),
        ),
        out_specs=(
            P("dp", None),
            P("dp", None),
            P(),
            P(),
            P("dp", None, "mp"),
            P(None, "mp"),
            P("mp", "dp"),
            P(),
            P(),
            P(),
            P("dp", "mp"),
            P("mp"),
            P("mp", "dp"),
            P(),
        ),
        check_vma=False,
    )
```

```python
import functools

import jax
import jax.numpy as jnp
from jax import lax
from jax.experimental import pallas as pl
from jax.experimental.pallas import tpu as pltpu
from jax.sharding import PartitionSpec as P

HEAD_DIM = 64
EPSILON = 1e-06
MASKED = 1e30
LANES = 128
TOTALS_AT = 32
bf16 = jnp.bfloat16
f32 = jnp.float32


class Given:
    def __init__(self, array, kind, pieces=1, columns=None):
        self.array, self.kind, self.pieces, self.columns = array, kind, pieces, columns

    @property
    def shape(self):
        if self.columns is None:
            return self.array.shape
        return (self.array.shape[0], self.columns[1])


class Made:
    def __init__(self, shape, dtype, kind, pieces=1, source=None):
        self.shape, self.dtype, self.kind, self.pieces, self.source = shape, dtype, kind, pieces, source


def piece_span(piece, rows):
    if isinstance(piece, int):
        return pl.ds(piece * rows, rows)
    return pl.ds(pl.multiple_of(piece * rows, rows), rows)


class Arriving:
    def __init__(self, ref, source=None, semaphores=None, pieces=1, columns=None):
        self.ref, self.source, self.semaphores, self.pieces = ref, source, semaphores, pieces
        self.pending, self.columns = source is not None, columns

    def copy(self, piece):
        span = piece_span(piece, self.ref.shape[0] // self.pieces)
        source = self.source.at[span]
        if self.columns is not None:
            source = self.source.at[span, pl.ds(*self.columns)]
        return pltpu.make_async_copy(source, self.ref.at[span], self.semaphores.at[piece])

    def ready(self, piece):
        if self.source is not None:
            self.pending = False
            self.copy(piece).wait()
        return self.ref

    def __call__(self):
        if self.pending:
            for piece in range(self.pieces):
                self.copy(piece).wait()
            self.pending = False
        return self.ref


class Leaving:
    def __init__(self, ref, target, semaphores, pieces):
        self.ref, self.target, self.semaphores, self.pieces = ref, target, semaphores, pieces
        self.started = False

    def copy(self, piece):
        span = piece_span(piece, self.ref.shape[0] // self.pieces)
        return pltpu.make_async_copy(
            self.ref.at[span], self.target.at[span], self.semaphores.at[piece]
        )

    def send(self, piece=0):
        self.started = True
        self.copy(piece).start()

    def finish(self):
        if not self.started:
            for piece in range(self.pieces):
                self.send(piece)

    def wait(self):
        for piece in range(self.pieces):
            self.copy(piece).wait()


class Staying:
    def __init__(self, ref):
        self.ref = ref

    def send(self, piece=0):
        pass


pins = {"v": pltpu.VMEM, "h": pltpu.HBM, "c": pltpu.HBM, "p": pltpu.VMEM, "q": pltpu.HBM}


def pinned(given):
    if given.kind in "sw":
        return given.array
    return pltpu.with_memory_space_constraint(given.array, pins[given.kind])


class Chain:
    last = None


def call(chain, kernel, name, outs, args, scratch=(), limit=9, covers=True):
    if chain.last is not None and all(g.array is not chain.last for g in args):
        args = [*args, Given(chain.last, "w")]
    ahead = [m for m in outs if m.kind == "p"]
    kernel_args = len(args)
    args = [*args, *(Given(m.source, "q") for m in ahead)]
    near = [g for g in args if g.kind == "h"]
    far = [m for m in outs if m.kind == "h"]
    copied = [m for m in outs if m.kind in "hc"]
    scratches = [pltpu.VMEM(g.shape, g.array.dtype) for g in near]
    scratches += [pltpu.VMEM(m.shape, m.dtype) for m in far]
    scratches += [pltpu.SemaphoreType.DMA((g.pieces,)) for g in near]
    scratches += [pltpu.SemaphoreType.DMA((m.pieces,)) for m in copied]
    scratches += [pltpu.SemaphoreType.DMA(()) for _ in ahead]

    def body(*refs):
        refs = list(refs)

        def take(count):
            taken = refs[:count]
            del refs[:count]
            return taken

        ins, results = take(len(args)), take(len(outs))
        arrivals, departures = take(len(near)), take(len(far))
        ready, gone = take(len(near)), take(len(copied))
        fetched = take(len(ahead))
        given, made, fetches = [], [], []
        for m, result in zip(outs, results):
            if m.kind == "p":
                source = ins[kernel_args + len(fetches)]
                fetches.append(pltpu.make_async_copy(source, result, fetched[len(fetches)]))
        for g, ref in zip(args, ins):
            if g.kind == "h":
                given.append(Arriving(arrivals.pop(0), ref, ready.pop(0), g.pieces, g.columns))
            elif g.kind not in "wq":
                given.append(ref if g.kind == "s" else Arriving(ref))
        waiting = [one for one in given if isinstance(one, Arriving) and one.pending]
        small = [one for one in waiting if len(one.ref.shape) == 1]
        pieced = [one for one in waiting if one.pieces > 1]
        order = [(one, 0) for one in small]
        for piece in range(max((one.pieces for one in pieced), default=0)):
            order += [(one, piece) for one in pieced if piece < one.pieces]
        order += [(one, 0) for one in waiting if one not in small and one not in pieced]
        for one, piece in order:
            one.copy(piece).start()
        for copy in fetches:
            copy.start()
        for m, ref in zip(outs, results):
            if m.kind == "h":
                made.append(Leaving(departures.pop(0), ref, gone.pop(0), m.pieces))
            elif m.kind == "p":
                continue
            elif m.kind == "c":
                made[-1] = Leaving(made[-1].ref, ref, gone.pop(0), m.pieces)
            else:
                made.append(Staying(ref))
        kernel(given, made, *refs)
        for one in waiting:
            one()
        leaving = [one for one in made if isinstance(one, Leaving)]
        for one in leaving:
            one.finish()
        for one in leaving:
            one.wait()
        for copy in fetches:
            copy.wait()

    spaces = {"s": pltpu.SMEM, "v": pltpu.VMEM, "h": pltpu.HBM, "c": pltpu.HBM, "w": pl.ANY, "p": pltpu.VMEM, "q": pltpu.HBM}
    results = pl.pallas_call(
        body,
        name=name,
        out_shape=tuple(pins[m.kind](m.shape, m.dtype) for m in outs),
        in_specs=[pl.BlockSpec(memory_space=spaces[g.kind]) for g in args],
        out_specs=tuple(pl.BlockSpec(memory_space=spaces[m.kind]) for m in outs),
        scratch_shapes=[*scratches, *scratch],
        compiler_params=pltpu.CompilerParams(vmem_limit_bytes=limit << 20),
        cost_estimate=pl.CostEstimate(flops=2 * 10**10 * covers, bytes_accessed=1, transcendentals=0),
    )(*(pinned(g) for g in args))
    chain.last = min(results, key=lambda result: result.size * result.dtype.itemsize)
    return results


def dot(a, b):
    return jnp.dot(a, b, preferred_element_type=f32)


def dot_t(a, b):
    return lax.dot_general(a, b, (((1,), (1,)), ((), ())), preferred_element_type=f32)


def lane_of(shape):
    return lax.broadcasted_iota(jnp.int32, shape, 1)


def head_half(values, half):
    return jnp.where(lane_of(values.shape) // HEAD_DIM == half, values, jnp.zeros_like(values))


def normalize(values):
    centered = values - jnp.mean(values, axis=-1, keepdims=True)
    variance = jnp.mean(centered * centered, axis=-1, keepdims=True)
    inverse = lax.rsqrt(variance + EPSILON)
    return centered * inverse, inverse


def norm_back(grad_out, normed, inverse, gain):
    scaled = grad_out * gain
    return inverse * (
        scaled
        - jnp.mean(scaled, axis=-1, keepdims=True)
        - normed * jnp.mean(scaled * normed, axis=-1, keepdims=True)
    )


def column_sum(values):
    return jnp.sum(values, axis=0, keepdims=True)


def rows_used(lengths):
    used = jnp.int32(0)
    for slot in range(lengths.shape[1]):
        used = used + lengths[0, slot]
    return used


def row_span(index, size):
    return pl.ds(pl.multiple_of(index * size, size), size)


def vector(ref):
    return ref[...][None, :]


def log_total_lanes(feature, head, log_total):
    lane = lane_of(feature.shape)
    rest = -log_total
    for piece in range(3):
        part_of = rest.astype(bf16).astype(f32)
        rest = rest - part_of
        feature = jnp.where(lane == TOTALS_AT + 3 * head + piece, part_of, feature)
    return feature


def attend(queries, keys, values, id_k, mixed, features, block):
    lane = lane_of((block, LANES))

    @pl.loop(0, queries.shape[0] // block)
    def _(index):
        span = row_span(index, block)
        ids = features[span, :]
        feature = ids.astype(f32)
        for pair in range(queries.shape[1] // LANES):
            cols = slice(pair * LANES, (pair + 1) * LANES)
            wide_keys = jnp.concatenate([keys[:, cols], id_k[...]], axis=1)
            query, value = queries[span, cols], values[:, cols]
            total = None
            inverses = []
            for half in range(2):
                wide_query = jnp.concatenate([head_half(query, half), ids], axis=1)
                exponent = jnp.exp(dot_t(wide_query, wide_keys))
                totals = jnp.sum(exponent, axis=1, keepdims=True)
                term = dot(exponent.astype(bf16), head_half(value, half))
                total = term if total is None else total + term
                inverses.append(1.0 / totals)
                feature = log_total_lanes(feature, 2 * pair + half, jnp.log(totals))
            mixed[span, cols] = (
                total * jnp.where(lane < HEAD_DIM, inverses[0], inverses[1])
            ).astype(bf16)
        features[span, :] = feature.astype(bf16)


def attend_shifted(queries, keys, values, id_k, mixed, features, block):
    @pl.loop(0, queries.shape[0] // block)
    def _(index):
        span = row_span(index, block)
        ids = jnp.where(lane_of((block, LANES)) < TOTALS_AT, features[span, :], jnp.zeros((), bf16))

        @pl.loop(0, queries.shape[1] // LANES)
        def _(pair):
            cols = row_span(pair, LANES)
            total = None
            for half in range(2):
                wide_query = jnp.concatenate([head_half(queries[span, cols], half), ids], axis=1)
                scores = dot_t(wide_query, jnp.concatenate([keys[:, cols], id_k[...]], axis=1))
                largest = jnp.max(scores, axis=1, keepdims=True)
                exponent = jnp.exp(scores - largest)
                totals = jnp.sum(exponent, axis=1, keepdims=True)
                term = dot(exponent.astype(bf16), head_half(values[:, cols], half)) / totals
                total = term if total is None else total + term
                features[span, :] = log_total_lanes(
                    features[span, :].astype(f32), 2 * pair + half, largest + jnp.log(totals)
                ).astype(bf16)
            mixed[span, cols] = total.astype(bf16)


def largest_norms(array):
    found = jnp.zeros((1, 1), f32)
    for start in range(0, array.shape[1], LANES):
        values = array[:, start : start + LANES].astype(f32)
        squares = values * values
        both = jnp.sum(squares, axis=1, keepdims=True)
        one = jnp.sum(head_half(squares, 0), axis=1, keepdims=True)
        found = jnp.maximum(found, jnp.max(jnp.maximum(one, both - one), axis=0, keepdims=True))
    return jnp.max(found)


def qkv_kernel(given, made):
    lengths, gain, bias, tokens, weight, qv_bias, out_weight = given
    hidden, queries, keys, values, id_k, mixed, features, part = made[:8]
    rows = tokens.ref.shape[0]
    slots = lengths.shape[1]
    lane = lane_of((1, LANES))
    starts = jnp.where(lane == 0, 0, rows)
    ends = jnp.full((1, LANES), rows, jnp.int32)
    running = jnp.int32(0)
    for slot in range(slots):
        running = running + lengths[0, slot]
        ends = jnp.where(lane == slot, running, ends)
        starts = jnp.where(lane == slot + 1, running, starts)
    scale = HEAD_DIM**-0.5
    block = rows // tokens.pieces
    gain, bias = gain(), bias()

    @pl.loop(0, tokens.pieces)
    def _(index):
        span = row_span(index, block)
        row = index * block + lax.broadcasted_iota(jnp.int32, (block, LANES), 0)
        same = (row >= starts) & (row < ends)
        features.ref[span, :] = same.astype(f32).astype(bf16)
        id_k.ref[span, :] = jnp.where(same | (lane > slots), 0.0, -MASKED).astype(bf16)
        normed, _ = normalize(tokens.ready(index)[span, :].astype(f32))
        hidden.ref[span, :] = (normed * vector(gain) + vector(bias)).astype(bf16)
        hidden.send(index)
        id_k.send(index)

    weight, qv_bias = weight(), qv_bias()

    @pl.loop(0, tokens.pieces)
    def _(index):
        span = row_span(index, block)
        low = hidden.ref[span, :]
        raised = (dot(low, weight[0]) + qv_bias[0:1, :]).astype(bf16)
        queries.ref[span, :] = (raised.astype(f32) * scale).astype(bf16)
        keys.ref[span, :] = dot(low, weight[1]).astype(bf16)
        values.ref[span, :] = (dot(low, weight[2]) + qv_bias[1:2, :]).astype(bf16)
        for one in (queries, keys, values):
            one.send(index)

    bounded = largest_norms(queries.ref) * largest_norms(keys.ref) <= 4000.0
    operands = [one.ref for one in (queries, keys, values, id_k, mixed, features)]

    @pl.when(bounded)
    def _():
        attend(*operands, rows // 2)

    @pl.when(jnp.logical_not(bounded))
    def _():
        attend_shifted(*operands, LANES)

    mixed.send()
    features.send()
    out_weight = out_weight()

    @pl.loop(0, 4)
    def _(index):
        span = row_span(index, rows // 4)
        part.ref[span, :] = dot(mixed.ref[span, :], out_weight[...]).astype(bf16)
        part.send(index)


def mlp_kernel(blocks, given, made, ordered, grad_mlp):
    lengths, place, out_bias, gain, bias, tokens, mine, other, up_bias, up, down, cotangent = given
    hidden, normed_two, inverse_two, active_out, grad_pre, part, down_bias_grad, keep, send = made
    rows = hidden.ref.shape[0]
    used = rows_used(lengths)
    block, tile = rows // 4, 512
    down_bias_grad.ref[...] = jnp.zeros_like(down_bias_grad.ref)
    out_bias, gain, bias = out_bias(), gain(), bias()

    @pl.loop(0, rows // block)
    def _(index):
        span = row_span(index, block)
        for one in (tokens, mine, other):
            one.ready(index)
        after = tokens.ref[span, :].astype(f32) + (
            mine.ref[span, :].astype(f32) + other.ref[span, :].astype(f32) + vector(out_bias)
        )
        normed, inverse = normalize(after)
        normed_two.ref[span, :] = normed.astype(bf16)
        inverse_two.ref[span, :] = jnp.broadcast_to(inverse, (block, LANES))
        hidden.ref[span, :] = (normed * vector(gain) + vector(bias)).astype(bf16)
        row = index * block + lax.broadcasted_iota(jnp.int32, (block, 1), 0)
        grad = jnp.where(row < used, cotangent.ready(index)[span, :].astype(f32), 0.0)
        down_bias_grad.ref[...] += column_sum(grad)
        grad_mlp[span, :] = grad.astype(bf16)
        for one in (normed_two, inverse_two):
            one.send(index)

    up_bias, up, down = up_bias(), up(), down()

    block = rows // 2

    @pl.loop(0, rows // block)
    def _(index):
        span = row_span(index, block)
        low, grad = hidden.ref[span, :], grad_mlp[span, :]
        total = None
        for start in range(0, up.shape[1], tile):
            cols = slice(start, start + tile)
            pre = dot(low, up[:, cols]) + up_bias[cols][None, :]
            square = pre * pre
            inner = pre * (0.7978845608028654 + (0.7978845608028654 * 0.044715) * square)
            share = 0.5 + 0.5 * jnp.tanh(inner)
            active = pre * share
            active_out.ref[span, cols] = active.astype(bf16)
            slope = share + (active * (1.0 - share)) * (
                (2 * 0.7978845608028654) + (6 * 0.7978845608028654 * 0.044715) * square
            )
            grad_low = (dot_t(grad, down[cols, :]) * slope).astype(bf16)
            grad_pre.ref[span, cols] = grad_low
            term = dot_t(grad_low, up[:, cols])
            total = term if total is None else total + term
        active_out.send(index)
        part.ref[span, :] = total.astype(bf16)

    order_columns(grad_mlp[...], place, ordered, blocks)
    weight_grad(ordered, active_out.ref, keep, send)


def down_kernel(given, made):
    weight, activated = given
    part = made[0]
    rows = activated.ref.shape[0] // 4
    weight = weight()
    activated = activated()

    @pl.loop(0, 4)
    def _(index):
        span = row_span(index, rows)
        part.ref[span, :] = dot(activated[span, :], weight[...]).astype(bf16)


def order_columns(values, place, ordered, blocks):
    turned = values.T
    width = turned.shape[0]
    size = width // blocks
    if size % 16:
        ordered[:width, :] = turned
    else:
        for index in range(blocks):
            at = pl.multiple_of(place[index] * size, size)
            ordered[pl.ds(at, size), :] = turned[index * size : (index + 1) * size]
    ordered[width:, :] = jnp.ones((16, turned.shape[1]), bf16)


def weight_grad(ordered, right, keep, send, sums=None, at=0):
    width = ordered.shape[0] - 16
    middle, columns = width // 2, right.shape[1]
    tile = 512 if columns % 512 == 0 else columns

    def one(start):
        source = pl.ds(start, tile)
        target = pl.ds(at + start, tile)
        result = dot(ordered[...], right[:, source])
        send.ref[:, target] = result[middle:width].astype(bf16)
        keep.ref[:, target] = result[:middle].astype(bf16)
        if sums is not None:
            sums.ref[:, source] = result[width : width + 8]

    if tile == columns:
        one(0)
    else:

        @pl.loop(0, columns // tile)
        def _(index):
            one(pl.multiple_of(index * tile, tile))


def weight_kernel(blocks, given, made, ordered):
    place, left, right = given
    order_columns(left()[...], place, ordered, blocks)
    weight_grad(ordered, right(), *made)


def middle_kernel(blocks, given, made, normed_back, ordered):
    lengths, place, gain, norm_mine, norm_other, normed_two, inverse_two, cotangent, weight, mixed = given
    used = rows_used(lengths)
    resid, grad_mixed, sums, keep, send = made
    rows = norm_mine.ref.shape[0]
    block = 256
    sums.ref[...] = jnp.zeros_like(sums.ref)
    gain = gain()

    @pl.loop(0, rows // block)
    def _(index):
        span = row_span(index, block)
        for one in (normed_two, inverse_two, cotangent):
            one.ready(index)
        normed = normed_two.ref[span, :].astype(f32)
        grad_norm = norm_mine.ready(index)[span, :].astype(f32) + norm_other.ready(index)[
            span, :
        ].astype(f32)
        inverse = inverse_two.ref[span, 0:1]
        row = index * block + lax.broadcasted_iota(jnp.int32, (block, 1), 0)
        grad = jnp.where(row < used, cotangent.ref[span, :].astype(f32), 0.0)
        grad = grad + norm_back(grad_norm, normed, inverse, vector(gain))
        resid.ref[span, :] = grad
        resid.send(index)
        low = grad.astype(bf16)
        normed_back[span, :] = low
        sums.ref[0:1, :] += column_sum(grad_norm * normed)
        sums.ref[1:2, :] += column_sum(grad_norm)
        sums.ref[2:3, :] += column_sum(low.astype(f32))

    grad_mixed.ref[...] = dot_t(normed_back[...], weight()[...]).astype(bf16)
    order_columns(normed_back[...], place, ordered, blocks)
    weight_grad(ordered, mixed(), keep, send)


def attention_back_kernel(pair, blocks, given, made, wide_keys, turned, key_total, value_total):
    given, before = given[:8], given[8:]
    place, keys, queries, values, id_k, features, grad_mixed, hidden = given
    if pair == 0:
        *made, ordered = made
        ordered = ordered.ref
    queries, keys, values, id_k, features, grad_mixed = (
        one() for one in (queries, keys, values, id_k, features, grad_mixed)
    )
    grads, sums, keep, send = made
    rows = queries.shape[0]
    cols = slice(pair * LANES, (pair + 1) * LANES)
    lane = lane_of((1, LANES))
    key = keys[:, cols]
    turned[...] = key.T
    for half in range(2):
        at = TOTALS_AT + 3 * (2 * pair + half)
        wide_keys[half, :, :LANES] = key
        wide_keys[half, :, LANES:] = id_k[...] + ((lane >= at) & (lane < at + 3)).astype(f32).astype(bf16)
    block = rows // 2
    key_total[...] = jnp.zeros_like(key_total)
    value_total[...] = jnp.zeros_like(value_total)

    @pl.loop(0, 2)
    def _(index):
        span = row_span(index, block)
        query, grad, feature = queries[span, cols], grad_mixed[span, cols], features[span, :]
        value = values[:, cols]
        key_term = value_term = None
        turned_grads = []
        for half in range(2):
            one_query, one_grad = head_half(query, half), head_half(grad, half)
            probs = jnp.exp(dot_t(wide_keys[half], jnp.concatenate([one_query, feature], axis=1)))
            grad_probs = dot_t(value, one_grad)
            centre = jnp.sum(probs * grad_probs, axis=0, keepdims=True)
            grad_scores = (probs * (grad_probs - centre)).astype(bf16)
            value_one = dot(probs.astype(bf16), one_grad)
            key_one = dot(grad_scores, one_query)
            value_term = value_one if half == 0 else value_term + value_one
            key_term = key_one if half == 0 else key_term + key_one
            turned_grads.append(dot(turned[half * HEAD_DIM : (half + 1) * HEAD_DIM, :], grad_scores))
        key_total[...] += key_term
        value_total[...] += value_term
        grads.ref[span, :LANES] = (jnp.concatenate(turned_grads, axis=0).T * HEAD_DIM**-0.5).astype(bf16)

    grads.ref[:, LANES : 2 * LANES] = key_total[...].astype(bf16)
    grads.ref[:, 2 * LANES :] = value_total[...].astype(bf16)
    if pair == 0:
        order_columns(hidden()[...], place, ordered, blocks)
    else:
        ordered = hidden()
    at = 0
    for index in range(0, len(before), 2):
        columns = before[index].ref.shape[1]
        for target, source in zip((keep, send), before[index : index + 2]):
            target.ref[:, at : at + columns] = source()[...]
        at += columns
    weight_grad(ordered, grads.ref, keep, send, sums, at)


def first_kernel(given, made):
    *grads, weight = given
    weight, part = weight(), made[0]
    rows = part.ref.shape[0] // 4
    grads = [one() for one in grads]
    @pl.loop(0, 4)
    def _(index):
        span = row_span(index, rows)
        operand = jnp.concatenate(
            [one[span, kind * LANES : (kind + 1) * LANES] for kind in range(3) for one in grads], axis=1
        )
        full = jnp.concatenate([weight[kind] for kind in range(3)], axis=1)
        part.ref[span, :] = dot_t(operand, full).astype(bf16)


def last_kernel(given, made):
    gain, tokens, mine, other, resid, *sums = given
    out, vectors = made
    middle_sums, down_sums, up_sums, *pair_sums = (one()[...] for one in sums)
    block = tokens.ref.shape[0] // 4
    width = tokens.ref.shape[1]
    vectors.ref[...] = jnp.zeros_like(vectors.ref)
    gain, tokens, mine, other, resid = gain(), tokens(), mine(), other(), resid()

    @pl.loop(0, 4)
    def _(index):
        span = row_span(index, block)
        normed, inverse = normalize(tokens[span, :].astype(f32))
        grad_first = mine[span, :].astype(f32) + other[span, :].astype(f32)
        out.ref[span, :] = resid[span, :] + norm_back(grad_first, normed, inverse, vector(gain))
        out.send(index)
        vectors.ref[0:1, :] += column_sum(grad_first * normed)
        vectors.ref[1:2, :] += column_sum(grad_first)

    pairs = len(pair_sums)
    for pair, one in enumerate(pair_sums):
        for kind, start in ((0, 0), (2, pairs * LANES)):
            at = start + pair * LANES
            vectors.ref[2:3, at : at + LANES] = one[0:1, kind * LANES : (kind + 1) * LANES]
    vectors.ref[3:6, :] = middle_sums[0:3, :]
    vectors.ref[6:7, :] = down_sums
    for index in range(up_sums.shape[1] // width):
        vectors.ref[7 + index : 8 + index, :] = up_sums[0:1, index * width : (index + 1) * width]


def fold_kernel(joined, folded, given, made):
    at = 0
    for index in range(len(given) // 2):
        keep, came = given[2 * index](), given[2 * index + 1]()
        stays, sent = made[:2] if joined else made[2 * index : 2 * index + 2]
        cols = slice(at, at + keep.shape[1])
        at += keep.shape[1] if joined else 0
        if index < folded:
            stays.ref[:, cols] = keep[...]
            sent.ref[:, cols] = came[...]
            continue
        middle = keep.shape[0] // 2
        sent.ref[:, cols] = (keep[middle:].astype(f32) + came[middle:].astype(f32)).astype(bf16)
        stays.ref[:, cols] = keep[:middle].astype(f32) + came[:middle].astype(f32)


def add_kernel(given, made):
    made[0].ref[...] = given[0]()[...] + given[1]()[...]


def output_kernel(given, made):
    out_bias, down_bias, tokens, part, other, down_part, down_other = given
    out = made[0]
    out_bias, down_bias, down_part, down_other = out_bias(), down_bias(), down_part(), down_other()
    block = out.ref.shape[0] // out.pieces

    @pl.loop(0, out.pieces)
    def _(index):
        span = row_span(index, block)
        for one in (tokens, part, other):
            one.ready(index)
        after = tokens.ref[span, :].astype(f32) + (
            part.ref[span, :].astype(f32) + other.ref[span, :].astype(f32) + vector(out_bias)
        )
        branch = down_part[span, :].astype(f32) + down_other[span, :].astype(f32) + vector(down_bias)
        out.ref[span, :] = (after + branch).astype(bf16)
        out.send(index)


def final_kernel(given, made):
    for index, one in enumerate(made):
        one.ref[...] = given[2 * index]()[...] + given[2 * index + 1]()[...].astype(f32)
        one.send()


def final_qkv_kernel(given, made):
    qkv, out = made
    keep, came = given
    total = keep()[...] + came()[...].astype(f32)
    local = out.ref.shape[1]
    out.ref[...] = total[:, :local]
    for pair in range(local // LANES):
        for kind in range(3):
            at = local + (3 * pair + kind) * LANES
            qkv.ref[kind, :, pair * LANES : (pair + 1) * LANES] = total[:, at : at + LANES]


def swap(values, axis, bit, size):
    return lax.ppermute(values, axis, [(i, i ^ (1 << bit)) for i in range(size)])


class Flow:
    def __init__(self, orders, size, keep, send):
        self.orders, self.size, self.keep, self.send, self.step = orders, size, keep, send, 0

    def exchange(self):
        pairs = [
            (2 * index + core, 2 * (index ^ (1 << order[self.step])) + core)
            for index in range(self.size)
            for core, order in enumerate(self.orders)
        ]
        self.came = lax.ppermute(self.send, ("dp", "mp"), pairs)
        self.step += 1


def fold(chain, flows, ready=()):
    halved = [(flow.keep.shape[0] // 2, flow.keep.shape[1]) for flow in flows]
    if ready:
        columns = sum(flow.keep.shape[1] for flow in (*ready, *flows))
        halved = [(halved[0][0], columns)]
    outs = []
    for rows, columns in halved:
        outs += [Made((rows, columns), f32, "h" if rows <= 48 else "v"), Made((rows, columns), bf16, "v")]
    pairs = [(flow.keep, flow.send) for flow in ready] + [(flow.keep, flow.came) for flow in flows]
    results = call(
        chain,
        functools.partial(fold_kernel, bool(ready), len(ready)),
        "fold",
        outs,
        [Given(array, "v") for pair in pairs for array in pair],
        limit=8,
    )
    for index in range(len(halved)):
        flows[index].keep, flows[index].send = results[2 * index : 2 * index + 2]


def finish(chain, flows, kernel, shapes, covers=True):
    return call(
        chain,
        kernel,
        "final",
        [Made(shape, f32, "h") for shape in shapes],
        [Given(array, kind) for flow in flows for array, kind in ((flow.keep, "h"), (flow.came, "v"))],
        limit=8,
        covers=covers,
    )


def places(orders, size, me, core):
    source = jnp.arange(size, dtype=jnp.int32) ^ me
    found = []
    for order in orders:
        place = jnp.zeros((size,), jnp.int32)
        for step, bit in enumerate(order):
            place = place + (((source >> bit) & 1) << (size.bit_length() - 2 - step))
        found.append(place)
    return jnp.where(core == 0, *found)


def arranged(halves, place, size):
    keep, send = halves
    rows, columns = keep.shape
    if (2 * rows // size) % 16 == 0:
        return halves
    spots = jnp.zeros((size,), jnp.int32).at[place].set(jnp.arange(size, dtype=jnp.int32))
    both = jnp.concatenate(halves, axis=0).reshape(size, 2 * rows // size, columns)[spots]
    both = both.reshape(2 * rows, columns)
    return both[:rows], both[rows:]


def per_device(
    n_dp, tokens, cotangent, lengths, ln1_gain, ln1_bias, qkv_weight, qv_bias, out_weight, out_bias,
    ln2_gain, ln2_bias, up_weight, up_bias, down_weight, down_bias,
):
    chain = Chain()
    rows, width = tokens.shape
    local = qkv_weight.shape[2]
    units = up_weight.shape[1]
    pairs = local // LANES
    me, core = lax.axis_index("dp"), lax.axis_index("mp")
    bits = list(range(n_dp.bit_length() - 1))
    rest = bits[3:]
    near_orders = [[0, 1, 2, *rest], [1, 0, 2, *rest]]
    long_orders = [[2, 0, 1, *rest], [2, 1, 0, *rest]]
    near_place, long_place = (places(orders, n_dp, me, core) for orders in (near_orders, long_orders))
    weight = jnp.transpose(qkv_weight, (1, 0, 2))
    scalars = Given(lengths, "s")
    near = lambda array: Given(array, "v")
    far = lambda array, pieces=1: Given(array, "h", pieces)
    fetch = lambda array: Made(array.shape, array.dtype, "p", source=array)
    halves = lambda columns: [Made((width // 2, columns), bf16, "v")] * 2
    turned = pltpu.VMEM((width + 16, rows), bf16)

    hidden_one, queries, keys, values, id_k, mixed, features, part = call(
        chain,
        qkv_kernel,
        "qkv_attention",
        [
            Made((rows, width), bf16, "h", 4),
            *[Made((rows, local), bf16, "h", 4)] * 3,
            Made((rows, LANES), bf16, "h", 4),
            Made((rows, local), bf16, "h"),
            Made((rows, LANES), bf16, "h"),
            Made((rows, width), bf16, "v", 4),
        ],
        [
            scalars, far(ln1_gain), far(ln1_bias), far(tokens, 4), far(weight), far(qv_bias), far(out_weight)
        ],
        limit=28,
    )
    other = swap(part, "mp", 0, 2)
    (
        hidden_two, normed_two, inverse_two, activated, grad_pre, norm_part, down_sums,
        down_keep, down_send,
    ) = call(
        chain,
        functools.partial(mlp_kernel, n_dp),
        "mlp",
        [
            Made((rows, width), bf16, "v"),
            Made((rows, width), bf16, "h", 4),
            Made((rows, LANES), f32, "h", 4),
            Made((rows, units), bf16, "h", 2),
            Made((rows, units), bf16, "v"),
            Made((rows, width), bf16, "v"),
            Made((1, width), f32, "v"),
            *halves(units),
        ],
        [
            scalars,
            Given(near_place, "s"),
            *map(far, (out_bias, ln2_gain, ln2_bias)),
            far(tokens, 4),
            near(part),
            near(other),
            *map(far, (up_bias, up_weight, down_weight)),
            far(cotangent, 4),
        ],
        scratch=[turned, pltpu.VMEM((rows, width), bf16)],
        limit=30,
    )
    norm_other = swap(norm_part, "mp", 0, 2)

    def weights(name, left, right, place, with_sums=False):
        return call(
        chain,
            functools.partial(weight_kernel, n_dp),
            name,
            [*halves(units), *[Made((8, units), f32, "v")] * with_sums],
            [Given(place, "s"), near(left), near(right)],
            scratch=[turned],
            limit=10,
        )

    flow_down = Flow(near_orders, n_dp, *arranged((down_keep, down_send), near_place, n_dp))
    flow_down.exchange()
    up_keep, up_send, up_sums = weights("up_grad", hidden_two, grad_pre, long_place, True)
    flow_up = Flow(long_orders, n_dp, *arranged((up_keep, up_send), long_place, n_dp))
    flow_up.exchange()
    resid, grad_mixed, middle_sums, out_keep, out_send = call(
        chain,
        functools.partial(middle_kernel, n_dp),
        "middle",
        [
            Made((rows, width), f32, "h", 4),
            Made((rows, local), bf16, "v"),
            Made((8, width), f32, "v"),
            *halves(local),
        ],
        [
            scalars,
            Given(near_place, "s"),
            far(ln2_gain),
            near(norm_part),
            near(norm_other),
            *map(near, (normed_two, inverse_two, cotangent)),
            near(out_weight),
            near(mixed),
        ],
        scratch=[pltpu.VMEM((rows, width), bf16), turned],
        limit=16,
    )
    grads, sums, halves_qkv = [], [], []
    hiddens = [hidden_one]

    def attention_back(pair, before=()):
        columns = 3 * LANES + sum(keep.shape[1] for keep, _ in before)
        three, sums_one, keep, send, *order = call(
            chain,
            functools.partial(attention_back_kernel, pair, n_dp),
            "attention_back%d" % pair,
            [
                Made((rows, 3 * LANES), bf16, "v"),
                Made((8, 3 * LANES), f32, "v"),
                *halves(columns),
                *[Made((width + 16, rows), bf16, "h")] * (pair == 0),
            ],
            [
                Given(near_place, "s"),
                *map(near, (keys, queries, values, id_k, features, grad_mixed)),
                near(hiddens[-1]),
                *(near(array) for pieces in before for array in pieces),
            ],
            scratch=[
                pltpu.VMEM((2, rows, 2 * LANES), bf16),
                pltpu.VMEM((LANES, rows), bf16),
                pltpu.VMEM((rows, LANES), f32),
                pltpu.VMEM((rows, LANES), f32),
            ],
            limit=18,
        )
        hiddens.extend(order)
        grads.append(three)
        sums.append(sums_one)
        halves_qkv.append((keep, send))

    def exchange(*flows):
        for flow in flows:
            flow.exchange()

    def flow_of(pieces):
        return Flow(near_orders, n_dp, *arranged(pieces, near_place, n_dp))

    flow_out = flow_of((out_keep, out_send))
    exchange(flow_out)
    attention_back(0)
    flow_first = flow_of(halves_qkv[0])
    fold(chain, [flow_down, flow_out])
    exchange(flow_down, flow_first)
    for pair in range(1, pairs - 1):
        attention_back(pair)
    flows_next = [flow_of(pieces) for pieces in halves_qkv[1:]]
    fold(chain, [flow_down, flow_up, flow_first])
    exchange(flow_down, flow_up, *flows_next)
    attention_back(pairs - 1)
    flow_qkv = flow_of(halves_qkv[-1])
    exchange(flow_qkv)
    fold(chain, [flow_down, flow_up, *flows_next])
    (first_part,) = call(
        chain,
        first_kernel,
        "first",
        [Made((rows, width), bf16, "v", 4)],
        [*map(near, grads), near(weight)],
        limit=10,
    )
    first_other = swap(first_part, "mp", 0, 2)
    fold(chain, [flow_qkv], [flow_out, flow_first, *flows_next])
    exchange(flow_qkv, flow_up)
    last_step = len(rest) == 1
    if last_step:
        exchange(flow_down)
    (down_part,) = call(
        chain,
        down_kernel,
        "down",
        [Made((rows, width), bf16, "v", 4)],
        [near(down_weight), near(activated)],
        limit=10,
    )
    down_other = swap(down_part, "mp", 0, 2)
    tokens_grad, vectors = call(
        chain,
        last_kernel,
        "last",
        [Made((rows, width), f32, "h", 4), Made((16, width), f32, "v")],
        [
            far(ln1_gain),
            *map(near, (tokens, first_part, first_other, resid, middle_sums, down_sums, up_sums, *sums)),
        ],
        limit=14,
        covers=False,
    )
    shape = (width // n_dp, units)
    if last_step:
        (down_total,) = finish(chain, [flow_down], final_kernel, [shape], False)
    fold(chain, [flow_qkv, flow_up])
    exchange(flow_qkv, flow_up)
    if not last_step:
        exchange(flow_down)

    def all_sum_step(bit):
        nonlocal vectors
        other = swap(vectors, "dp", bit, n_dp)
        (vectors,) = call(
            chain, add_kernel, "add", [Made((16, width), f32, "v")], [near(vectors), near(other)], limit=4
        )

    (output,) = call(
        chain,
        output_kernel,
        "output",
        [Made((rows, width), bf16, "h", 4)],
        [
            far(out_bias), far(down_bias), *(far(array, 4) for array in (tokens, part, other)), near(down_part),
            near(down_other),
        ],
        limit=16,
    )
    all_sum_step(bits[0])
    fold(chain, [flow_qkv])
    exchange(flow_qkv)
    all_sum_step(bits[1])
    if last_step:
        (up_total,) = finish(chain, [flow_up], final_kernel, [shape])
    for bit in bits[2:-1]:
        all_sum_step(bit)
    flows = [flow_qkv, flow_up, flow_down]
    for step in range(1, len(rest)):
        fold(chain, flows)
        exchange(*flows)
    if not last_step:
        down_total, up_total = finish(chain, [flow_down, flow_up], final_kernel, [shape] * 2)
    mine = width // n_dp
    qkv_total, out_total = finish(
        chain, [flow_qkv], final_qkv_kernel, [(3, mine, local), (mine, local)]
    )
    all_sum_step(bits[-1])
    ups = units // width
    return (
        output,
        tokens_grad,
        vectors[0],
        vectors[1],
        jnp.transpose(qkv_total, (1, 0, 2)),
        vectors[2].reshape(2, local),
        out_total.T,
        vectors[5],
        vectors[3],
        vectors[4],
        up_total,
        vectors[7 : 7 + ups].reshape(-1),
        down_total.T,
        vectors[6],
    )


def solution(mesh):
    return jax.shard_map(
        functools.partial(per_device, mesh.shape["dp"]),
        mesh=mesh,
        in_specs=(
            P("dp", None),
            P("dp", None),
            P("dp", None),
            P(),
            P(),
            P(None, None, "mp"),
            P(None, "mp"),
            P("mp", None),
            P(),
            P(),
            P(),
            P(None, "mp"),
            P("mp"),
            P("mp", None),
            P(),
        ),
        out_specs=(
            P("dp", None),
            P("dp", None),
            P(),
            P(),
            P("dp", None, "mp"),
            P(None, "mp"),
            P("mp", "dp"),
            P(),
            P(),
            P(),
            P("dp", "mp"),
            P("mp"),
            P("mp", "dp"),
            P(),
        ),
        check_vma=False,
    )
```

```python
import functools

import jax
import jax.numpy as jnp
from jax import lax
from jax.experimental import pallas as pl
from jax.experimental.pallas import tpu as pltpu
from jax.sharding import PartitionSpec as P

HEAD_DIM = 64
EPSILON = 1e-06
MASKED = 1e30
LANES = 128
TOTALS_AT = (32, 48, 64)
bf16 = jnp.bfloat16
f32 = jnp.float32


class Given:
    def __init__(self, array, kind, pieces=1, columns=None):
        self.array, self.kind, self.pieces, self.columns = array, kind, pieces, columns

    @property
    def shape(self):
        if self.columns is None:
            return self.array.shape
        return (self.array.shape[0], self.columns[1])


class Made:
    def __init__(self, shape, dtype, kind, pieces=1, source=None):
        self.shape, self.dtype, self.kind, self.pieces, self.source = shape, dtype, kind, pieces, source


def piece_span(piece, rows):
    if isinstance(piece, int):
        return pl.ds(piece * rows, rows)
    return pl.ds(pl.multiple_of(piece * rows, rows), rows)


class Arriving:
    def __init__(self, ref, source=None, semaphores=None, pieces=1, columns=None):
        self.ref, self.source, self.semaphores, self.pieces = ref, source, semaphores, pieces
        self.pending, self.columns = source is not None, columns

    def copy(self, piece):
        span = piece_span(piece, self.ref.shape[0] // self.pieces)
        source = self.source.at[span]
        if self.columns is not None:
            source = self.source.at[span, pl.ds(*self.columns)]
        return pltpu.make_async_copy(source, self.ref.at[span], self.semaphores.at[piece])

    def ready(self, piece):
        if self.source is not None:
            self.pending = False
            self.copy(piece).wait()
        return self.ref

    def __call__(self):
        if self.pending:
            for piece in range(self.pieces):
                self.copy(piece).wait()
            self.pending = False
        return self.ref


class Leaving:
    def __init__(self, ref, target, semaphores, pieces):
        self.ref, self.target, self.semaphores, self.pieces = ref, target, semaphores, pieces
        self.started = False

    def copy(self, piece):
        span = piece_span(piece, self.ref.shape[0] // self.pieces)
        return pltpu.make_async_copy(
            self.ref.at[span], self.target.at[span], self.semaphores.at[piece]
        )

    def send(self, piece=0):
        self.started = True
        self.copy(piece).start()

    def finish(self):
        if not self.started:
            for piece in range(self.pieces):
                self.send(piece)

    def wait(self):
        for piece in range(self.pieces):
            self.copy(piece).wait()


class Staying:
    def __init__(self, ref):
        self.ref = ref

    def send(self, piece=0):
        pass


pins = {"v": pltpu.VMEM, "h": pltpu.HBM, "c": pltpu.HBM, "p": pltpu.VMEM, "q": pltpu.HBM, "x": pltpu.HBM}


def pinned(given):
    if given.kind in "sw":
        return given.array
    return pltpu.with_memory_space_constraint(given.array, pins[given.kind])


class Chain:
    last = None


def call(chain, kernel, name, outs, args, scratch=(), limit=9, covers=True):
    if chain.last is not None and all(g.array is not chain.last for g in args):
        args = [*args, Given(chain.last, chain.kind)]
    ahead = [m for m in outs if m.kind == "p"]
    kernel_args = len(args)
    args = [*args, *(Given(m.source, "q") for m in ahead)]
    near = [g for g in args if g.kind == "h"]
    far = [m for m in outs if m.kind == "h"]
    copied = [m for m in outs if m.kind in "hc"]
    scratches = [pltpu.VMEM(g.shape, g.array.dtype) for g in near]
    scratches += [pltpu.VMEM(m.shape, m.dtype) for m in far]
    scratches += [pltpu.SemaphoreType.DMA((g.pieces,)) for g in near]
    scratches += [pltpu.SemaphoreType.DMA((m.pieces,)) for m in copied]
    scratches += [pltpu.SemaphoreType.DMA(()) for _ in ahead]

    def body(*refs):
        refs = list(refs)

        def take(count):
            taken = refs[:count]
            del refs[:count]
            return taken

        ins, results = take(len(args)), take(len(outs))
        arrivals, departures = take(len(near)), take(len(far))
        ready, gone = take(len(near)), take(len(copied))
        fetched = take(len(ahead))
        given, made, fetches = [], [], []
        for m, result in zip(outs, results):
            if m.kind == "p":
                source = ins[kernel_args + len(fetches)]
                fetches.append(pltpu.make_async_copy(source, result, fetched[len(fetches)]))
        for g, ref in zip(args, ins):
            if g.kind == "h":
                given.append(Arriving(arrivals.pop(0), ref, ready.pop(0), g.pieces, g.columns))
            elif g.kind not in "wxq":
                given.append(ref if g.kind == "s" else Arriving(ref))
        waiting = [one for one in given if isinstance(one, Arriving) and one.pending]
        small = [one for one in waiting if len(one.ref.shape) == 1]
        pieced = [one for one in waiting if one.pieces > 1]
        order = [(one, 0) for one in small]
        for piece in range(max((one.pieces for one in pieced), default=0)):
            order += [(one, piece) for one in pieced if piece < one.pieces]
        order += [(one, 0) for one in waiting if one not in small and one not in pieced]
        for one, piece in order:
            one.copy(piece).start()
        for copy in fetches:
            copy.start()
        for m, ref in zip(outs, results):
            if m.kind == "h":
                made.append(Leaving(departures.pop(0), ref, gone.pop(0), m.pieces))
            elif m.kind == "p":
                continue
            elif m.kind == "c":
                made[-1] = Leaving(made[-1].ref, ref, gone.pop(0), m.pieces)
            else:
                made.append(Staying(ref))
        kernel(given, made, *refs)
        for one in waiting:
            one()
        leaving = [one for one in made if isinstance(one, Leaving)]
        for one in leaving:
            one.finish()
        for one in leaving:
            one.wait()
        for copy in fetches:
            copy.wait()

    spaces = {"s": pltpu.SMEM, "v": pltpu.VMEM, "h": pltpu.HBM, "c": pltpu.HBM, "w": pl.ANY, "p": pltpu.VMEM, "q": pltpu.HBM, "x": pltpu.HBM}
    results = pl.pallas_call(
        body,
        name=name,
        out_shape=tuple(pins[m.kind](m.shape, m.dtype) for m in outs),
        in_specs=[pl.BlockSpec(memory_space=spaces[g.kind]) for g in args],
        out_specs=tuple(pl.BlockSpec(memory_space=spaces[m.kind]) for m in outs),
        scratch_shapes=[*scratches, *scratch],
        compiler_params=pltpu.CompilerParams(vmem_limit_bytes=limit << 20),
        cost_estimate=pl.CostEstimate(flops=2 * 10**10 * covers, bytes_accessed=1, transcendentals=0),
    )(*(pinned(g) for g in args))
    size = lambda pair: pair[0].size * pair[0].dtype.itemsize
    chain.last, kind = min(((result, m.kind) for m, result in zip(outs, results)), key=size)
    chain.kind = "x" if kind in "hc" else "w"
    return results


def dot(a, b):
    return jnp.dot(a, b, preferred_element_type=f32)


def dot_t(a, b):
    return lax.dot_general(a, b, (((1,), (1,)), ((), ())), preferred_element_type=f32)


def lane_of(shape):
    return lax.broadcasted_iota(jnp.int32, shape, 1)


def head_half(values, half):
    return jnp.where(lane_of(values.shape) // HEAD_DIM == half, values, jnp.zeros_like(values))


def normalize(values):
    centered = values - jnp.mean(values, axis=-1, keepdims=True)
    variance = jnp.mean(centered * centered, axis=-1, keepdims=True)
    inverse = lax.rsqrt(variance + EPSILON)
    return centered * inverse, inverse


def norm_back(grad_out, normed, inverse, gain):
    scaled = grad_out * gain
    return inverse * (
        scaled
        - jnp.mean(scaled, axis=-1, keepdims=True)
        - normed * jnp.mean(scaled * normed, axis=-1, keepdims=True)
    )


def column_sum(values):
    return jnp.sum(values, axis=0, keepdims=True)


def rows_used(lengths):
    used = jnp.int32(0)
    for slot in range(lengths.shape[1]):
        used = used + lengths[0, slot]
    return used


def row_span(index, size):
    return pl.ds(pl.multiple_of(index * size, size), size)


def vector(ref):
    return ref[...][None, :]


def is_total(lane, head):
    found = lane == TOTALS_AT[0] + head
    for start in TOTALS_AT[1:]:
        found = found | (lane == start + head)
    return found


def in_pieces(values, lane):
    first = values.astype(bf16).astype(f32)
    second = (values - first).astype(bf16).astype(f32)
    third = values - first - second
    return jnp.where(lane < TOTALS_AT[1], first, jnp.where(lane < TOTALS_AT[2], second, third))


def attend(queries, keys, values, id_k, mixed, features, block):
    lane = lane_of((block, LANES))

    @pl.loop(0, queries.shape[0] // block)
    def _(index):
        span = row_span(index, block)
        ids = features[span, :]
        feature = jnp.zeros((block, LANES), f32)
        for pair in range(queries.shape[1] // LANES):
            cols = slice(pair * LANES, (pair + 1) * LANES)
            wide_keys = jnp.concatenate([keys[:, cols], id_k[...]], axis=1)
            query, value = queries[span, cols], values[:, cols]
            total = None
            inverses = []
            for half in range(2):
                wide_query = jnp.concatenate([head_half(query, half), ids], axis=1)
                exponent = jnp.exp(dot_t(wide_query, wide_keys))
                totals = jnp.sum(exponent, axis=1, keepdims=True)
                term = dot(exponent.astype(bf16), head_half(value, half))
                total = term if total is None else total + term
                inverses.append(1.0 / totals)
                feature = jnp.where(is_total(lane, 2 * pair + half), -jnp.log(totals), feature)
            mixed[span, cols] = (
                total * jnp.where(lane < HEAD_DIM, inverses[0], inverses[1])
            ).astype(bf16)
        features[span, :] = ids + in_pieces(feature, lane).astype(bf16)


def attend_shifted(queries, keys, values, id_k, mixed, features, block):
    @pl.loop(0, queries.shape[0] // block)
    def _(index):
        span = row_span(index, block)
        ids = features[span, :]

        @pl.loop(0, queries.shape[1] // LANES)
        def _(pair):
            cols = row_span(pair, LANES)
            total = None
            for half in range(2):
                wide_query = jnp.concatenate([head_half(queries[span, cols], half), ids], axis=1)
                scores = dot_t(wide_query, jnp.concatenate([keys[:, cols], id_k[...]], axis=1))
                largest = jnp.max(scores, axis=1, keepdims=True)
                exponent = jnp.exp(scores - largest)
                totals = jnp.sum(exponent, axis=1, keepdims=True)
                term = dot(exponent.astype(bf16), head_half(values[:, cols], half)) / totals
                total = term if total is None else total + term
                lane = lane_of((block, LANES))
                feature = jnp.where(is_total(lane, 2 * pair + half), -(largest + jnp.log(totals)), 0.0)
                features[span, :] += in_pieces(feature, lane).astype(bf16)
            mixed[span, cols] = total.astype(bf16)


def largest_norms(array):
    found = jnp.zeros((1, 1), f32)
    for start in range(0, array.shape[1], LANES):
        values = array[:, start : start + LANES].astype(f32)
        squares = values * values
        both = jnp.sum(squares, axis=1, keepdims=True)
        one = jnp.sum(head_half(squares, 0), axis=1, keepdims=True)
        found = jnp.maximum(found, jnp.max(jnp.maximum(one, both - one), axis=0, keepdims=True))
    return jnp.max(found)


def qkv_kernel(given, made):
    lengths, gain, bias, tokens, weight, qv_bias, out_weight = given
    hidden, queries, keys, values, id_k, mixed, features, part = made[:8]
    rows = tokens.ref.shape[0]
    slots = lengths.shape[1]
    lane = lane_of((1, LANES))
    starts = jnp.where(lane == 0, 0, rows)
    ends = jnp.full((1, LANES), rows, jnp.int32)
    running = jnp.int32(0)
    for slot in range(slots):
        running = running + lengths[0, slot]
        ends = jnp.where(lane == slot, running, ends)
        starts = jnp.where(lane == slot + 1, running, starts)
    scale = HEAD_DIM**-0.5
    block = rows // tokens.pieces
    gain, bias = gain(), bias()

    def norm(index):
        span = row_span(index, block) if not isinstance(index, int) else pl.ds(index * block, block)
        row = index * block + lax.broadcasted_iota(jnp.int32, (block, LANES), 0)
        same = (row >= starts) & (row < ends)
        features.ref[span, :] = same.astype(f32).astype(bf16)
        id_k.ref[span, :] = jnp.where(same | (lane > slots), 0.0, -MASKED).astype(bf16)
        normed, _ = normalize(tokens.ready(index)[span, :].astype(f32))
        hidden.ref[span, :] = (normed * vector(gain) + vector(bias)).astype(bf16)
        hidden.send(index)
        id_k.send(index)

    def project(index):
        span = row_span(index, block) if not isinstance(index, int) else pl.ds(index * block, block)
        low = hidden.ref[span, :]
        raised = (dot(low, weight[0]) + qv_bias[0:1, :]).astype(bf16)
        queries.ref[span, :] = (raised.astype(f32) * scale).astype(bf16)
        keys.ref[span, :] = dot(low, weight[1]).astype(bf16)
        values.ref[span, :] = (dot(low, weight[2]) + qv_bias[1:2, :]).astype(bf16)
        for one in (queries, keys, values):
            one.send(index)

    norm(0)
    weight, qv_bias = weight(), qv_bias()

    @pl.loop(0, tokens.pieces - 1)
    def _(index):
        project(index)
        norm(index + 1)

    project(tokens.pieces - 1)

    bounded = largest_norms(queries.ref) * largest_norms(keys.ref) <= 4000.0
    operands = [one.ref for one in (queries, keys, values, id_k, mixed, features)]

    @pl.when(bounded)
    def _():
        attend(*operands, rows // 4)

    @pl.when(jnp.logical_not(bounded))
    def _():
        attend_shifted(*operands, LANES)

    mixed.send()
    features.send()
    out_weight = out_weight()

    @pl.loop(0, 4)
    def _(index):
        span = row_span(index, rows // 4)
        part.ref[span, :] = dot(mixed.ref[span, :], out_weight[...]).astype(bf16)
        part.send(index)


def mlp_kernel(blocks, given, made, ordered, grad_mlp):
    lengths, place, out_bias, gain, bias, tokens, mine, other, up_bias, up, down, cotangent = given
    hidden, normed_two, inverse_two, active_out, grad_pre, part, down_bias_grad, keep, send = made
    rows = hidden.ref.shape[0]
    used = rows_used(lengths)
    block, tile = rows // 4, 512
    down_bias_grad.ref[...] = jnp.zeros_like(down_bias_grad.ref)
    out_bias, gain, bias = out_bias(), gain(), bias()

    @pl.loop(0, rows // block)
    def _(index):
        span = row_span(index, block)
        for one in (tokens, mine, other):
            one.ready(index)
        after = tokens.ref[span, :].astype(f32) + (
            mine.ref[span, :].astype(f32) + other.ref[span, :].astype(f32) + vector(out_bias)
        )
        normed, inverse = normalize(after)
        normed_two.ref[span, :] = normed.astype(bf16)
        inverse_two.ref[span, :] = jnp.broadcast_to(inverse, (block, LANES))
        hidden.ref[span, :] = (normed * vector(gain) + vector(bias)).astype(bf16)
        row = index * block + lax.broadcasted_iota(jnp.int32, (block, 1), 0)
        grad = jnp.where(row < used, cotangent.ready(index)[span, :].astype(f32), 0.0)
        down_bias_grad.ref[...] += column_sum(grad)
        grad_mlp[span, :] = grad.astype(bf16)
        for one in (normed_two, inverse_two):
            one.send(index)

    up_bias, up, down = up_bias(), up(), down()

    block = rows // 2

    @pl.loop(0, rows // block)
    def _(index):
        span = row_span(index, block)
        low, grad = hidden.ref[span, :], grad_mlp[span, :]
        total = None
        for start in range(0, up.shape[1], tile):
            cols = slice(start, start + tile)
            pre = dot(low, up[:, cols]) + up_bias[cols][None, :]
            square = pre * pre
            inner = pre * (0.7978845608028654 + (0.7978845608028654 * 0.044715) * square)
            share = 0.5 + 0.5 * jnp.tanh(inner)
            active = pre * share
            active_out.ref[span, cols] = active.astype(bf16)
            slope = share + (active * (1.0 - share)) * (
                (2 * 0.7978845608028654) + (6 * 0.7978845608028654 * 0.044715) * square
            )
            grad_low = (dot_t(grad, down[cols, :]) * slope).astype(bf16)
            grad_pre.ref[span, cols] = grad_low
            term = dot_t(grad_low, up[:, cols])
            total = term if total is None else total + term
        active_out.send(index)
        part.ref[span, :] = total.astype(bf16)

    order_columns(grad_mlp[...], place, ordered, blocks)
    weight_grad(ordered, active_out.ref, keep, send)


def down_kernel(given, made):
    weight, activated = given
    part = made[0]
    rows = activated.ref.shape[0] // 4
    weight = weight()
    activated = activated()

    @pl.loop(0, 4)
    def _(index):
        span = row_span(index, rows)
        part.ref[span, :] = dot(activated[span, :], weight[...]).astype(bf16)


def order_columns(values, place, ordered, blocks):
    turned = values.T
    width = turned.shape[0]
    size = width // blocks
    if size % 16:
        ordered[:width, :] = turned
    else:
        for index in range(blocks):
            at = pl.multiple_of(place[index] * size, size)
            ordered[pl.ds(at, size), :] = turned[index * size : (index + 1) * size]
    ordered[width:, :] = jnp.ones((16, turned.shape[1]), bf16)


def weight_grad(ordered, right, keep, send, sums=None, at=0):
    width = ordered.shape[0] - 16
    middle, columns = width // 2, right.shape[1]
    tile = 512 if columns % 512 == 0 else columns

    def one(start):
        source = pl.ds(start, tile)
        target = pl.ds(at + start, tile)
        result = dot(ordered[...], right[:, source])
        send.ref[:, target] = result[middle:width].astype(bf16)
        keep.ref[:, target] = result[:middle].astype(bf16)
        if sums is not None:
            sums.ref[:, source] = result[width : width + 8]

    if tile == columns:
        one(0)
    else:

        @pl.loop(0, columns // tile)
        def _(index):
            one(pl.multiple_of(index * tile, tile))


def weight_kernel(blocks, given, made, ordered):
    place, left, right = given
    order_columns(left()[...], place, ordered, blocks)
    weight_grad(ordered, right(), *made)


def middle_kernel(blocks, given, made, normed_back, ordered):
    lengths, place, gain, norm_mine, norm_other, normed_two, inverse_two, cotangent, weight, mixed = given
    used = rows_used(lengths)
    resid, grad_mixed, sums, keep, send = made
    rows = norm_mine.ref.shape[0]
    block = 256
    sums.ref[...] = jnp.zeros_like(sums.ref)
    gain = gain()

    @pl.loop(0, rows // block)
    def _(index):
        span = row_span(index, block)
        for one in (normed_two, inverse_two, cotangent):
            one.ready(index)
        normed = normed_two.ref[span, :].astype(f32)
        grad_norm = norm_mine.ready(index)[span, :].astype(f32) + norm_other.ready(index)[
            span, :
        ].astype(f32)
        inverse = inverse_two.ref[span, 0:1]
        row = index * block + lax.broadcasted_iota(jnp.int32, (block, 1), 0)
        grad = jnp.where(row < used, cotangent.ref[span, :].astype(f32), 0.0)
        grad = grad + norm_back(grad_norm, normed, inverse, vector(gain))
        resid.ref[span, :] = grad
        resid.send(index)
        low = grad.astype(bf16)
        normed_back[span, :] = low
        sums.ref[0:1, :] += column_sum(grad_norm * normed)
        sums.ref[1:2, :] += column_sum(grad_norm)
        sums.ref[2:3, :] += column_sum(low.astype(f32))

    grad_mixed.ref[...] = dot_t(normed_back[...], weight()[...]).astype(bf16)
    order_columns(normed_back[...], place, ordered, blocks)
    weight_grad(ordered, mixed(), keep, send)


def attention_back_kernel(pair, blocks, given, made, wide_keys, turned, key_total, value_total):
    given, before = given[:8], given[8:]
    place, keys, queries, values, id_k, features, grad_mixed, hidden = given
    if pair == 0:
        *made, ordered = made
        ordered = ordered.ref
    queries, keys, values, id_k, features, grad_mixed = (
        one() for one in (queries, keys, values, id_k, features, grad_mixed)
    )
    grads, sums, keep, send = made
    rows = queries.shape[0]
    cols = slice(pair * LANES, (pair + 1) * LANES)
    lane = lane_of((1, LANES))
    key = keys[:, cols]
    turned[...] = key.T
    for half in range(2):
        wide_keys[half, :, :LANES] = key
        wide_keys[half, :, LANES:] = id_k[...] + is_total(lane, 2 * pair + half).astype(f32).astype(bf16)
    block = rows // 2
    key_total[...] = jnp.zeros_like(key_total)
    value_total[...] = jnp.zeros_like(value_total)

    @pl.loop(0, 2)
    def _(index):
        span = row_span(index, block)
        query, grad, feature = queries[span, cols], grad_mixed[span, cols], features[span, :]
        value = values[:, cols]
        key_term = value_term = None
        turned_grads = []
        for half in range(2):
            one_query, one_grad = head_half(query, half), head_half(grad, half)
            probs = jnp.exp(dot_t(wide_keys[half], jnp.concatenate([one_query, feature], axis=1)))
            grad_probs = dot_t(value, one_grad)
            centre = jnp.sum(probs * grad_probs, axis=0, keepdims=True)
            grad_scores = (probs * (grad_probs - centre)).astype(bf16)
            value_one = dot(probs.astype(bf16), one_grad)
            key_one = dot(grad_scores, one_query)
            value_term = value_one if half == 0 else value_term + value_one
            key_term = key_one if half == 0 else key_term + key_one
            turned_grads.append(dot(turned[half * HEAD_DIM : (half + 1) * HEAD_DIM, :], grad_scores))
        key_total[...] += key_term
        value_total[...] += value_term
        grads.ref[span, :LANES] = (jnp.concatenate(turned_grads, axis=0).T * HEAD_DIM**-0.5).astype(bf16)

    grads.ref[:, LANES : 2 * LANES] = key_total[...].astype(bf16)
    grads.ref[:, 2 * LANES :] = value_total[...].astype(bf16)
    if pair == 0:
        order_columns(hidden()[...], place, ordered, blocks)
    else:
        ordered = hidden()
    at = 0
    for index in range(0, len(before), 2):
        columns = before[index].ref.shape[1]
        for target, source in zip((keep, send), before[index : index + 2]):
            target.ref[:, at : at + columns] = source()[...]
        at += columns
    weight_grad(ordered, grads.ref, keep, send, sums, at)


def first_kernel(given, made):
    *grads, weight = given
    weight, part = weight(), made[0]
    rows = part.ref.shape[0] // 4
    grads = [one() for one in grads]
    @pl.loop(0, 4)
    def _(index):
        span = row_span(index, rows)
        operand = jnp.concatenate(
            [one[span, kind * LANES : (kind + 1) * LANES] for kind in range(3) for one in grads], axis=1
        )
        full = jnp.concatenate([weight[kind] for kind in range(3)], axis=1)
        part.ref[span, :] = dot_t(operand, full).astype(bf16)


def last_kernel(given, made):
    gain, tokens, mine, other, resid, *sums = given
    out, vectors = made
    middle_sums, down_sums, up_sums, *pair_sums = (one()[...] for one in sums)
    block = tokens.ref.shape[0] // 4
    width = tokens.ref.shape[1]
    vectors.ref[...] = jnp.zeros_like(vectors.ref)
    gain, tokens, mine, other, resid = gain(), tokens(), mine(), other(), resid()

    @pl.loop(0, 4)
    def _(index):
        span = row_span(index, block)
        normed, inverse = normalize(tokens[span, :].astype(f32))
        grad_first = mine[span, :].astype(f32) + other[span, :].astype(f32)
        out.ref[span, :] = resid[span, :] + norm_back(grad_first, normed, inverse, vector(gain))
        out.send(index)
        vectors.ref[0:1, :] += column_sum(grad_first * normed)
        vectors.ref[1:2, :] += column_sum(grad_first)

    pairs = len(pair_sums)
    for pair, one in enumerate(pair_sums):
        for kind, start in ((0, 0), (2, pairs * LANES)):
            at = start + pair * LANES
            vectors.ref[2:3, at : at + LANES] = one[0:1, kind * LANES : (kind + 1) * LANES]
    vectors.ref[3:6, :] = middle_sums[0:3, :]
    vectors.ref[6:7, :] = down_sums
    for index in range(up_sums.shape[1] // width):
        vectors.ref[7 + index : 8 + index, :] = up_sums[0:1, index * width : (index + 1) * width]


def fold_kernel(joined, folded, given, made):
    at = 0
    for index in range(len(given) // 2):
        keep, came = given[2 * index](), given[2 * index + 1]()
        stays, sent = made[:2] if joined else made[2 * index : 2 * index + 2]
        cols = slice(at, at + keep.shape[1])
        at += keep.shape[1] if joined else 0
        if index < folded:
            stays.ref[:, cols] = keep[...]
            sent.ref[:, cols] = came[...]
            continue
        middle = keep.shape[0] // 2
        sent.ref[:, cols] = (keep[middle:].astype(f32) + came[middle:].astype(f32)).astype(bf16)
        stays.ref[:, cols] = keep[:middle].astype(f32) + came[:middle].astype(f32)


def add_kernel(given, made):
    made[0].ref[...] = given[0]()[...] + given[1]()[...]


def spread_kernel(given, made):
    total = given[0]()[...] + given[1]()[...]
    *singles, qv, ups = made
    width = total.shape[1]
    for row, one in zip((0, 1, 3, 4, 5, 6), singles):
        one.ref[...] = total[row]
    local = qv.ref.shape[1]
    for row in range(2):
        qv.ref[row : row + 1] = total[2:3, row * local : (row + 1) * local]
    for row in range(ups.ref.shape[0] // width):
        ups.ref[pl.ds(row * width, width)] = total[7 + row]


def output_kernel(given, made):
    out_bias, down_bias, tokens, part, other, down_part, down_other = given
    out = made[0]
    out_bias, down_bias, down_part, down_other = out_bias(), down_bias(), down_part(), down_other()
    block = out.ref.shape[0] // out.pieces

    @pl.loop(0, out.pieces)
    def _(index):
        span = row_span(index, block)
        for one in (tokens, part, other):
            one.ready(index)
        after = tokens.ref[span, :].astype(f32) + (
            part.ref[span, :].astype(f32) + other.ref[span, :].astype(f32) + vector(out_bias)
        )
        branch = down_part[span, :].astype(f32) + down_other[span, :].astype(f32) + vector(down_bias)
        out.ref[span, :] = (after + branch).astype(bf16)
        out.send(index)


def final_kernel(given, made):
    for index, one in enumerate(made):
        one.ref[...] = given[2 * index]()[...] + given[2 * index + 1]()[...].astype(f32)
        one.send()


def final_qkv_kernel(given, made):
    qkv, out = made
    keep, came = given
    total = keep()[...] + came()[...].astype(f32)
    local = out.ref.shape[1]
    out.ref[...] = total[:, :local]
    for pair in range(local // LANES):
        for kind in range(3):
            at = local + (3 * pair + kind) * LANES
            qkv.ref[kind, :, pair * LANES : (pair + 1) * LANES] = total[:, at : at + LANES]


def swap(values, axis, bit, size):
    return lax.ppermute(values, axis, [(i, i ^ (1 << bit)) for i in range(size)])


class Flow:
    def __init__(self, orders, size, keep, send):
        self.orders, self.size, self.keep, self.send, self.step = orders, size, keep, send, 0

    def exchange(self):
        pairs = [
            (2 * index + core, 2 * (index ^ (1 << order[self.step])) + core)
            for index in range(self.size)
            for core, order in enumerate(self.orders)
        ]
        self.came = lax.ppermute(self.send, ("dp", "mp"), pairs)
        self.step += 1


def fold(chain, flows, ready=()):
    halved = [(flow.keep.shape[0] // 2, flow.keep.shape[1]) for flow in flows]
    if ready:
        columns = sum(flow.keep.shape[1] for flow in (*ready, *flows))
        halved = [(halved[0][0], columns)]
    outs = []
    for rows, columns in halved:
        outs += [Made((rows, columns), f32, "h" if rows <= 48 else "v"), Made((rows, columns), bf16, "v")]
    pairs = [(flow.keep, flow.send) for flow in ready] + [(flow.keep, flow.came) for flow in flows]
    results = call(
        chain,
        functools.partial(fold_kernel, bool(ready), len(ready)),
        "fold",
        outs,
        [Given(array, "v") for pair in pairs for array in pair],
        limit=8,
    )
    for index in range(len(halved)):
        flows[index].keep, flows[index].send = results[2 * index : 2 * index + 2]


def finish(chain, flows, kernel, shapes, covers=True):
    return call(
        chain,
        kernel,
        "final",
        [Made(shape, f32, "h") for shape in shapes],
        [Given(array, kind) for flow in flows for array, kind in ((flow.keep, "h"), (flow.came, "v"))],
        limit=8,
        covers=covers,
    )


def places(orders, size, me, core):
    source = jnp.arange(size, dtype=jnp.int32) ^ me
    found = []
    for order in orders:
        place = jnp.zeros((size,), jnp.int32)
        for step, bit in enumerate(order):
            place = place + (((source >> bit) & 1) << (size.bit_length() - 2 - step))
        found.append(place)
    return jnp.where(core == 0, *found)


def arranged(halves, place, size):
    keep, send = halves
    rows, columns = keep.shape
    if (2 * rows // size) % 16 == 0:
        return halves
    spots = jnp.zeros((size,), jnp.int32).at[place].set(jnp.arange(size, dtype=jnp.int32))
    both = jnp.concatenate(halves, axis=0).reshape(size, 2 * rows // size, columns)[spots]
    both = both.reshape(2 * rows, columns)
    return both[:rows], both[rows:]


def per_device(
    n_dp, tokens, cotangent, lengths, ln1_gain, ln1_bias, qkv_weight, qv_bias, out_weight, out_bias,
    ln2_gain, ln2_bias, up_weight, up_bias, down_weight, down_bias,
):
    chain = Chain()
    rows, width = tokens.shape
    local = qkv_weight.shape[2]
    units = up_weight.shape[1]
    pairs = local // LANES
    me, core = lax.axis_index("dp"), lax.axis_index("mp")
    bits = list(range(n_dp.bit_length() - 1))
    rest = bits[3:]
    near_orders = [[0, 1, 2, *rest], [1, 0, 2, *rest]]
    long_orders = [[2, 0, 1, *rest], [2, 1, 0, *rest]]
    near_place, long_place = (places(orders, n_dp, me, core) for orders in (near_orders, long_orders))
    weight = jnp.transpose(qkv_weight, (1, 0, 2))
    scalars = Given(lengths, "s")
    near = lambda array: Given(array, "v")
    far = lambda array, pieces=1: Given(array, "h", pieces)
    fetch = lambda array: Made(array.shape, array.dtype, "p", source=array)
    halves = lambda columns: [Made((width // 2, columns), bf16, "v")] * 2
    turned = pltpu.VMEM((width + 16, rows), bf16)

    hidden_one, queries, keys, values, id_k, mixed, features, part = call(
        chain,
        qkv_kernel,
        "qkv_attention",
        [
            Made((rows, width), bf16, "h", 4),
            *[Made((rows, local), bf16, "h", 4)] * 3,
            Made((rows, LANES), bf16, "h", 4),
            Made((rows, local), bf16, "h"),
            Made((rows, LANES), bf16, "h"),
            Made((rows, width), bf16, "v", 4),
        ],
        [
            scalars, far(ln1_gain), far(ln1_bias), far(tokens, 4), far(weight), far(qv_bias), far(out_weight)
        ],
        limit=28,
    )
    other = swap(part, "mp", 0, 2)
    (
        hidden_two, normed_two, inverse_two, activated, grad_pre, norm_part, down_sums,
        down_keep, down_send,
    ) = call(
        chain,
        functools.partial(mlp_kernel, n_dp),
        "mlp",
        [
            Made((rows, width), bf16, "v"),
            Made((rows, width), bf16, "h", 4),
            Made((rows, LANES), f32, "h", 4),
            Made((rows, units), bf16, "h", 2),
            Made((rows, units), bf16, "v"),
            Made((rows, width), bf16, "v"),
            Made((1, width), f32, "v"),
            *halves(units),
        ],
        [
            scalars,
            Given(near_place, "s"),
            *map(far, (out_bias, ln2_gain, ln2_bias)),
            far(tokens, 4),
            near(part),
            near(other),
            *map(far, (up_bias, up_weight, down_weight)),
            far(cotangent, 4),
        ],
        scratch=[turned, pltpu.VMEM((rows, width), bf16)],
        limit=30,
    )
    norm_other = swap(norm_part, "mp", 0, 2)

    def weights(name, left, right, place, with_sums=False):
        return call(
        chain,
            functools.partial(weight_kernel, n_dp),
            name,
            [*halves(units), *[Made((8, units), f32, "v")] * with_sums],
            [Given(place, "s"), near(left), near(right)],
            scratch=[turned],
            limit=10,
        )

    flow_down = Flow(near_orders, n_dp, *arranged((down_keep, down_send), near_place, n_dp))
    flow_down.exchange()
    up_keep, up_send, up_sums = weights("up_grad", hidden_two, grad_pre, long_place, True)
    flow_up = Flow(long_orders, n_dp, *arranged((up_keep, up_send), long_place, n_dp))
    flow_up.exchange()
    resid, grad_mixed, middle_sums, out_keep, out_send = call(
        chain,
        functools.partial(middle_kernel, n_dp),
        "middle",
        [
            Made((rows, width), f32, "h", 4),
            Made((rows, local), bf16, "v"),
            Made((8, width), f32, "v"),
            *halves(local),
        ],
        [
            scalars,
            Given(near_place, "s"),
            far(ln2_gain),
            near(norm_part),
            near(norm_other),
            *map(near, (normed_two, inverse_two, cotangent)),
            near(out_weight),
            near(mixed),
        ],
        scratch=[pltpu.VMEM((rows, width), bf16), turned],
        limit=16,
    )
    grads, sums, halves_qkv = [], [], []
    hiddens = [hidden_one]

    def attention_back(pair, before=()):
        columns = 3 * LANES + sum(keep.shape[1] for keep, _ in before)
        three, sums_one, keep, send, *order = call(
            chain,
            functools.partial(attention_back_kernel, pair, n_dp),
            "attention_back%d" % pair,
            [
                Made((rows, 3 * LANES), bf16, "v"),
                Made((8, 3 * LANES), f32, "v"),
                *halves(columns),
                *[Made((width + 16, rows), bf16, "h")] * (pair == 0),
            ],
            [
                Given(near_place, "s"),
                *map(near, (keys, queries, values, id_k, features, grad_mixed)),
                near(hiddens[-1]),
                *(near(array) for pieces in before for array in pieces),
            ],
            scratch=[
                pltpu.VMEM((2, rows, 2 * LANES), bf16),
                pltpu.VMEM((LANES, rows), bf16),
                pltpu.VMEM((rows, LANES), f32),
                pltpu.VMEM((rows, LANES), f32),
            ],
            limit=18,
        )
        hiddens.extend(order)
        grads.append(three)
        sums.append(sums_one)
        halves_qkv.append((keep, send))

    def exchange(*flows):
        for flow in flows:
            flow.exchange()

    def flow_of(pieces):
        return Flow(near_orders, n_dp, *arranged(pieces, near_place, n_dp))

    flow_out = flow_of((out_keep, out_send))
    exchange(flow_out)
    attention_back(0)
    flow_first = flow_of(halves_qkv[0])
    fold(chain, [flow_down, flow_out])
    exchange(flow_down, flow_first)
    for pair in range(1, pairs - 1):
        attention_back(pair)
    flows_next = [flow_of(pieces) for pieces in halves_qkv[1:]]
    fold(chain, [flow_down, flow_up, flow_first])
    exchange(flow_down, flow_up, *flows_next)
    attention_back(pairs - 1)
    flow_qkv = flow_of(halves_qkv[-1])
    exchange(flow_qkv)
    fold(chain, [flow_down, flow_up, *flows_next])
    (first_part,) = call(
        chain,
        first_kernel,
        "first",
        [Made((rows, width), bf16, "v", 4)],
        [*map(near, grads), near(weight)],
        limit=10,
    )
    first_other = swap(first_part, "mp", 0, 2)
    fold(chain, [flow_qkv], [flow_out, flow_first, *flows_next])
    exchange(flow_qkv, flow_up)
    last_step = len(rest) == 1
    if last_step:
        exchange(flow_down)
    (down_part,) = call(
        chain,
        down_kernel,
        "down",
        [Made((rows, width), bf16, "v", 4)],
        [near(down_weight), near(activated)],
        limit=10,
    )
    down_other = swap(down_part, "mp", 0, 2)
    tokens_grad, vectors = call(
        chain,
        last_kernel,
        "last",
        [Made((rows, width), f32, "h", 4), Made((16, width), f32, "v")],
        [
            far(ln1_gain),
            *map(near, (tokens, first_part, first_other, resid, middle_sums, down_sums, up_sums, *sums)),
        ],
        limit=14,
        covers=False,
    )
    shape = (width // n_dp, units)
    if last_step:
        (down_total,) = finish(chain, [flow_down], final_kernel, [shape], False)
    fold(chain, [flow_qkv, flow_up])
    exchange(flow_qkv, flow_up)
    if not last_step:
        exchange(flow_down)

    def all_sum_step(bit):
        nonlocal vectors
        other = swap(vectors, "dp", bit, n_dp)
        (vectors,) = call(
            chain, add_kernel, "add", [Made((16, width), f32, "v")], [near(vectors), near(other)], limit=4
        )

    (output,) = call(
        chain,
        output_kernel,
        "output",
        [Made((rows, width), bf16, "h", 4)],
        [
            far(out_bias), far(down_bias), *(far(array, 4) for array in (tokens, part, other)), near(down_part),
            near(down_other),
        ],
        limit=16,
    )
    all_sum_step(bits[0])
    fold(chain, [flow_qkv])
    exchange(flow_qkv)
    all_sum_step(bits[1])
    if last_step:
        (up_total,) = finish(chain, [flow_up], final_kernel, [shape])
    for bit in bits[2:-1]:
        all_sum_step(bit)
    flows = [flow_qkv, flow_up, flow_down]
    for step in range(1, len(rest)):
        fold(chain, flows)
        exchange(*flows)
    if not last_step:
        down_total, up_total = finish(chain, [flow_down, flow_up], final_kernel, [shape] * 2)
    mine = width // n_dp
    qkv_total, out_total = finish(
        chain, [flow_qkv], final_qkv_kernel, [(3, mine, local), (mine, local)]
    )
    *singles, qv_sum, up_sum = call(
        chain,
        spread_kernel,
        "spread",
        [*[Made((width,), f32, "h")] * 6, Made((2, local), f32, "h"), Made((units,), f32, "h")],
        [near(vectors), near(swap(vectors, "dp", bits[-1], n_dp))],
        limit=4,
    )
    gain_one, bias_one, gain_two, bias_two, out_bias_sum, down_bias_sum = singles
    return (
        output,
        tokens_grad,
        gain_one,
        bias_one,
        jnp.transpose(qkv_total, (1, 0, 2)),
        qv_sum,
        out_total.T,
        out_bias_sum,
        gain_two,
        bias_two,
        up_total,
        up_sum,
        down_total.T,
        down_bias_sum,
    )


def solution(mesh):
    return jax.shard_map(
        functools.partial(per_device, mesh.shape["dp"]),
        mesh=mesh,
        in_specs=(
            P("dp", None),
            P("dp", None),
            P("dp", None),
            P(),
            P(),
            P(None, None, "mp"),
            P(None, "mp"),
            P("mp", None),
            P(),
            P(),
            P(),
            P(None, "mp"),
            P("mp"),
            P("mp", None),
            P(),
        ),
        out_specs=(
            P("dp", None),
            P("dp", None),
            P(),
            P(),
            P("dp", None, "mp"),
            P(None, "mp"),
            P("mp", "dp"),
            P(),
            P(),
            P(),
            P("dp", "mp"),
            P("mp"),
            P("mp", "dp"),
            P(),
        ),
        check_vma=False,
    )
```

```python
import functools

import jax
import jax.numpy as jnp
from jax import lax
from jax.experimental import pallas as pl
from jax.experimental.pallas import tpu as pltpu
from jax.sharding import PartitionSpec as P

HEAD_DIM = 64
EPSILON = 1e-06
MASKED = 1e30
LANES = 128
TOTALS_AT = (32, 48, 64)
bf16 = jnp.bfloat16
f32 = jnp.float32


class Given:
    def __init__(self, array, kind, pieces=1, columns=None):
        self.array, self.kind, self.pieces, self.columns = array, kind, pieces, columns

    @property
    def shape(self):
        if self.columns is None:
            return self.array.shape
        return (self.array.shape[0], self.columns[1])


class Made:
    def __init__(self, shape, dtype, kind, pieces=1, source=None):
        self.shape, self.dtype, self.kind, self.pieces, self.source = shape, dtype, kind, pieces, source


def piece_span(piece, rows):
    if isinstance(piece, int):
        return pl.ds(piece * rows, rows)
    return pl.ds(pl.multiple_of(piece * rows, rows), rows)


class Arriving:
    def __init__(self, ref, source=None, semaphores=None, pieces=1, columns=None):
        self.ref, self.source, self.semaphores, self.pieces = ref, source, semaphores, pieces
        self.pending, self.columns = source is not None, columns

    def copy(self, piece):
        span = piece_span(piece, self.ref.shape[0] // self.pieces)
        source = self.source.at[span]
        if self.columns is not None:
            source = self.source.at[span, pl.ds(*self.columns)]
        return pltpu.make_async_copy(source, self.ref.at[span], self.semaphores.at[piece])

    def ready(self, piece):
        if self.source is not None:
            self.pending = False
            self.copy(piece).wait()
        return self.ref

    def __call__(self):
        if self.pending:
            for piece in range(self.pieces):
                self.copy(piece).wait()
            self.pending = False
        return self.ref


class Leaving:
    def __init__(self, ref, target, semaphores, pieces):
        self.ref, self.target, self.semaphores, self.pieces = ref, target, semaphores, pieces
        self.started = False

    def copy(self, piece):
        span = piece_span(piece, self.ref.shape[0] // self.pieces)
        return pltpu.make_async_copy(
            self.ref.at[span], self.target.at[span], self.semaphores.at[piece]
        )

    def send(self, piece=0):
        self.started = True
        self.copy(piece).start()

    def finish(self):
        if not self.started:
            for piece in range(self.pieces):
                self.send(piece)

    def wait(self):
        for piece in range(self.pieces):
            self.copy(piece).wait()


class Staying:
    def __init__(self, ref):
        self.ref = ref

    def send(self, piece=0):
        pass


pins = {"v": pltpu.VMEM, "h": pltpu.HBM, "c": pltpu.HBM, "p": pltpu.VMEM, "q": pltpu.HBM, "x": pltpu.HBM}


def pinned(given):
    if given.kind in "sw":
        return given.array
    return pltpu.with_memory_space_constraint(given.array, pins[given.kind])


class Chain:
    last = None


def call(chain, kernel, name, outs, args, scratch=(), limit=9, covers=True):
    if chain.last is not None and all(g.array is not chain.last for g in args):
        args = [*args, Given(chain.last, chain.kind)]
    ahead = [m for m in outs if m.kind == "p"]
    kernel_args = len(args)
    args = [*args, *(Given(m.source, "q") for m in ahead)]
    near = [g for g in args if g.kind == "h"]
    far = [m for m in outs if m.kind == "h"]
    copied = [m for m in outs if m.kind in "hc"]
    scratches = [pltpu.VMEM(g.shape, g.array.dtype) for g in near]
    scratches += [pltpu.VMEM(m.shape, m.dtype) for m in far]
    scratches += [pltpu.SemaphoreType.DMA((g.pieces,)) for g in near]
    scratches += [pltpu.SemaphoreType.DMA((m.pieces,)) for m in copied]
    scratches += [pltpu.SemaphoreType.DMA(()) for _ in ahead]

    def body(*refs):
        refs = list(refs)

        def take(count):
            taken = refs[:count]
            del refs[:count]
            return taken

        ins, results = take(len(args)), take(len(outs))
        arrivals, departures = take(len(near)), take(len(far))
        ready, gone = take(len(near)), take(len(copied))
        fetched = take(len(ahead))
        given, made, fetches = [], [], []
        for m, result in zip(outs, results):
            if m.kind == "p":
                source = ins[kernel_args + len(fetches)]
                fetches.append(pltpu.make_async_copy(source, result, fetched[len(fetches)]))
        for g, ref in zip(args, ins):
            if g.kind == "h":
                given.append(Arriving(arrivals.pop(0), ref, ready.pop(0), g.pieces, g.columns))
            elif g.kind not in "wxq":
                given.append(ref if g.kind == "s" else Arriving(ref))
        waiting = [one for one in given if isinstance(one, Arriving) and one.pending]
        small = [one for one in waiting if len(one.ref.shape) == 1]
        pieced = [one for one in waiting if one.pieces > 1]
        order = [(one, 0) for one in small]
        for piece in range(max((one.pieces for one in pieced), default=0)):
            order += [(one, piece) for one in pieced if piece < one.pieces]
        order += [(one, 0) for one in waiting if one not in small and one not in pieced]
        for one, piece in order:
            one.copy(piece).start()
        for copy in fetches:
            copy.start()
        for m, ref in zip(outs, results):
            if m.kind == "h":
                made.append(Leaving(departures.pop(0), ref, gone.pop(0), m.pieces))
            elif m.kind == "p":
                continue
            elif m.kind == "c":
                made[-1] = Leaving(made[-1].ref, ref, gone.pop(0), m.pieces)
            else:
                made.append(Staying(ref))
        kernel(given, made, *refs)
        for one in waiting:
            one()
        leaving = [one for one in made if isinstance(one, Leaving)]
        for one in leaving:
            one.finish()
        for one in leaving:
            one.wait()
        for copy in fetches:
            copy.wait()

    spaces = {"s": pltpu.SMEM, "v": pltpu.VMEM, "h": pltpu.HBM, "c": pltpu.HBM, "w": pl.ANY, "p": pltpu.VMEM, "q": pltpu.HBM, "x": pltpu.HBM}
    results = pl.pallas_call(
        body,
        name=name,
        out_shape=tuple(pins[m.kind](m.shape, m.dtype) for m in outs),
        in_specs=[pl.BlockSpec(memory_space=spaces[g.kind]) for g in args],
        out_specs=tuple(pl.BlockSpec(memory_space=spaces[m.kind]) for m in outs),
        scratch_shapes=[*scratches, *scratch],
        compiler_params=pltpu.CompilerParams(vmem_limit_bytes=limit << 20),
        cost_estimate=pl.CostEstimate(flops=2 * 10**10 * covers, bytes_accessed=1, transcendentals=0),
    )(*(pinned(g) for g in args))
    size = lambda pair: pair[0].size * pair[0].dtype.itemsize
    chain.last, kind = min(((result, m.kind) for m, result in zip(outs, results)), key=size)
    chain.kind = "x" if kind in "hc" else "w"
    return results


def dot(a, b):
    return jnp.dot(a, b, preferred_element_type=f32)


def dot_t(a, b):
    return lax.dot_general(a, b, (((1,), (1,)), ((), ())), preferred_element_type=f32)


def lane_of(shape):
    return lax.broadcasted_iota(jnp.int32, shape, 1)


def head_half(values, half):
    return jnp.where(lane_of(values.shape) // HEAD_DIM == half, values, jnp.zeros_like(values))


def normalize(values):
    centered = values - jnp.mean(values, axis=-1, keepdims=True)
    variance = jnp.mean(centered * centered, axis=-1, keepdims=True)
    inverse = lax.rsqrt(variance + EPSILON)
    return centered * inverse, inverse


def norm_back(grad_out, normed, inverse, gain):
    scaled = grad_out * gain
    return inverse * (
        scaled
        - jnp.mean(scaled, axis=-1, keepdims=True)
        - normed * jnp.mean(scaled * normed, axis=-1, keepdims=True)
    )


def column_sum(values):
    return jnp.sum(values, axis=0, keepdims=True)


def rows_used(lengths):
    used = jnp.int32(0)
    for slot in range(lengths.shape[1]):
        used = used + lengths[0, slot]
    return used


def row_span(index, size):
    return pl.ds(pl.multiple_of(index * size, size), size)


def vector(ref):
    return ref[...][None, :]


def is_total(lane, head):
    found = lane == TOTALS_AT[0] + head
    for start in TOTALS_AT[1:]:
        found = found | (lane == start + head)
    return found


def in_pieces(values, lane):
    first = values.astype(bf16).astype(f32)
    second = (values - first).astype(bf16).astype(f32)
    third = values - first - second
    return jnp.where(lane < TOTALS_AT[1], first, jnp.where(lane < TOTALS_AT[2], second, third))


def attend(queries, keys, values, id_k, mixed, wide, features, block):
    lane = lane_of((block, LANES))

    @pl.loop(0, queries.shape[0] // block)
    def _(index):
        span = row_span(index, block)
        ids = features[span, :]
        feature = jnp.zeros((block, LANES), f32)
        for pair in range(queries.shape[1] // LANES):
            cols = slice(pair * LANES, (pair + 1) * LANES)
            wide_keys = jnp.concatenate([keys[:, cols], id_k[...]], axis=1)
            query, value = queries[span, cols], values[:, cols]
            total = None
            inverses = []
            for half in range(2):
                wide_query = jnp.concatenate([head_half(query, half), ids], axis=1)
                exponent = jnp.exp(dot_t(wide_query, wide_keys))
                totals = jnp.sum(exponent, axis=1, keepdims=True)
                term = dot(exponent.astype(bf16), head_half(value, half))
                total = term if total is None else total + term
                inverses.append(1.0 / totals)
                feature = jnp.where(is_total(lane, 2 * pair + half), -jnp.log(totals), feature)
            total = total * jnp.where(lane < HEAD_DIM, inverses[0], inverses[1])
            wide[span, cols] = total
            mixed[span, cols] = total.astype(bf16)
        features[span, :] = ids + in_pieces(feature, lane).astype(bf16)


def attend_shifted(queries, keys, values, id_k, mixed, wide, features, block):
    @pl.loop(0, queries.shape[0] // block)
    def _(index):
        span = row_span(index, block)
        ids = features[span, :]

        @pl.loop(0, queries.shape[1] // LANES)
        def _(pair):
            cols = row_span(pair, LANES)
            total = None
            for half in range(2):
                wide_query = jnp.concatenate([head_half(queries[span, cols], half), ids], axis=1)
                scores = dot_t(wide_query, jnp.concatenate([keys[:, cols], id_k[...]], axis=1))
                largest = jnp.max(scores, axis=1, keepdims=True)
                exponent = jnp.exp(scores - largest)
                totals = jnp.sum(exponent, axis=1, keepdims=True)
                term = dot(exponent.astype(bf16), head_half(values[:, cols], half)) / totals
                total = term if total is None else total + term
                lane = lane_of((block, LANES))
                feature = jnp.where(is_total(lane, 2 * pair + half), -(largest + jnp.log(totals)), 0.0)
                features[span, :] += in_pieces(feature, lane).astype(bf16)
            wide[span, cols] = total
            mixed[span, cols] = total.astype(bf16)


def largest_norms(array):
    found = jnp.zeros((1, 1), f32)
    for start in range(0, array.shape[1], LANES):
        values = array[:, start : start + LANES].astype(f32)
        squares = values * values
        both = jnp.sum(squares, axis=1, keepdims=True)
        one = jnp.sum(head_half(squares, 0), axis=1, keepdims=True)
        found = jnp.maximum(found, jnp.max(jnp.maximum(one, both - one), axis=0, keepdims=True))
    return jnp.max(found)


def qkv_kernel(given, made):
    lengths, gain, bias, tokens, weight, qv_bias, out_weight = given
    hidden, queries, keys, values, id_k, mixed, wide, features, part = made
    rows = tokens.ref.shape[0]
    slots = lengths.shape[1]
    lane = lane_of((1, LANES))
    starts = jnp.where(lane == 0, 0, rows)
    ends = jnp.full((1, LANES), rows, jnp.int32)
    running = jnp.int32(0)
    for slot in range(slots):
        running = running + lengths[0, slot]
        ends = jnp.where(lane == slot, running, ends)
        starts = jnp.where(lane == slot + 1, running, starts)
    scale = HEAD_DIM**-0.5
    block = rows // tokens.pieces
    gain, bias = gain(), bias()

    def norm(index):
        span = row_span(index, block) if not isinstance(index, int) else pl.ds(index * block, block)
        row = index * block + lax.broadcasted_iota(jnp.int32, (block, LANES), 0)
        same = (row >= starts) & (row < ends)
        features.ref[span, :] = same.astype(f32).astype(bf16)
        id_k.ref[span, :] = jnp.where(same | (lane > slots), 0.0, -MASKED).astype(bf16)
        normed, _ = normalize(tokens.ready(index)[span, :].astype(f32))
        hidden.ref[span, :] = (normed * vector(gain) + vector(bias)).astype(bf16)
        hidden.send(index)
        id_k.send(index)

    def project(index):
        span = row_span(index, block) if not isinstance(index, int) else pl.ds(index * block, block)
        low = hidden.ref[span, :]
        raised = (dot(low, weight[0]) + qv_bias[0:1, :]).astype(bf16)
        queries.ref[span, :] = (raised.astype(f32) * scale).astype(bf16)
        keys.ref[span, :] = dot(low, weight[1]).astype(bf16)
        values.ref[span, :] = (dot(low, weight[2]) + qv_bias[1:2, :]).astype(bf16)
        for one in (queries, keys, values):
            one.send(index)

    norm(0)
    weight, qv_bias = weight(), qv_bias()

    @pl.loop(0, tokens.pieces - 1)
    def _(index):
        project(index)
        norm(index + 1)

    project(tokens.pieces - 1)

    bounded = largest_norms(queries.ref) * largest_norms(keys.ref) <= 4000.0
    operands = [one.ref for one in (queries, keys, values, id_k, mixed, wide, features)]

    @pl.when(bounded)
    def _():
        attend(*operands, rows // 4)

    @pl.when(jnp.logical_not(bounded))
    def _():
        attend_shifted(*operands, LANES)

    for one in (mixed, wide, features):
        one.send()
    out_weight = out_weight()

    @pl.loop(0, 4)
    def _(index):
        span = row_span(index, rows // 4)
        part.ref[span, :] = dot(mixed.ref[span, :], out_weight[...]).astype(bf16)
        part.send(index)


def mlp_kernel(blocks, given, made, ordered, grad_mlp):
    lengths, place, out_bias, gain, bias, tokens, mine, other, up_bias, up, down, cotangent = given
    hidden, normed_two, inverse_two, active_out, grad_pre, part, down_bias_grad, keep, send = made
    rows = hidden.ref.shape[0]
    used = rows_used(lengths)
    block, tile = rows // 4, 512
    down_bias_grad.ref[...] = jnp.zeros_like(down_bias_grad.ref)
    out_bias, gain, bias = out_bias(), gain(), bias()

    @pl.loop(0, rows // block)
    def _(index):
        span = row_span(index, block)
        for one in (tokens, mine, other):
            one.ready(index)
        after = tokens.ref[span, :].astype(f32) + (
            mine.ref[span, :].astype(f32) + other.ref[span, :].astype(f32) + vector(out_bias)
        )
        normed, inverse = normalize(after)
        normed_two.ref[span, :] = normed.astype(bf16)
        inverse_two.ref[span, :] = jnp.broadcast_to(inverse, (block, LANES))
        hidden.ref[span, :] = (normed * vector(gain) + vector(bias)).astype(bf16)
        row = index * block + lax.broadcasted_iota(jnp.int32, (block, 1), 0)
        grad = jnp.where(row < used, cotangent.ready(index)[span, :].astype(f32), 0.0)
        down_bias_grad.ref[...] += column_sum(grad)
        grad_mlp[span, :] = grad.astype(bf16)
        for one in (normed_two, inverse_two):
            one.send(index)

    up_bias, up, down = up_bias(), up(), down()

    block = rows // 2

    @pl.loop(0, rows // block)
    def _(index):
        span = row_span(index, block)
        low, grad = hidden.ref[span, :], grad_mlp[span, :]
        total = None
        for start in range(0, up.shape[1], tile):
            cols = slice(start, start + tile)
            pre = dot(low, up[:, cols]) + up_bias[cols][None, :]
            square = pre * pre
            inner = pre * (0.7978845608028654 + (0.7978845608028654 * 0.044715) * square)
            share = 0.5 + 0.5 * jnp.tanh(inner)
            active = pre * share
            active_out.ref[span, cols] = active.astype(bf16)
            slope = share + (active * (1.0 - share)) * (
                (2 * 0.7978845608028654) + (6 * 0.7978845608028654 * 0.044715) * square
            )
            grad_low = (dot_t(grad, down[cols, :]) * slope).astype(bf16)
            grad_pre.ref[span, cols] = grad_low
            term = dot_t(grad_low, up[:, cols])
            total = term if total is None else total + term
        active_out.send(index)
        part.ref[span, :] = total.astype(bf16)

    order_columns(grad_mlp[...], place, ordered, blocks)
    weight_grad(ordered, active_out.ref, keep, send)


def down_kernel(given, made):
    weight, activated = given
    part = made[0]
    rows = activated.ref.shape[0] // 4
    weight = weight()
    activated = activated()

    @pl.loop(0, 4)
    def _(index):
        span = row_span(index, rows)
        part.ref[span, :] = dot(activated[span, :], weight[...]).astype(bf16)


def order_columns(values, place, ordered, blocks):
    turned = values.T
    width = turned.shape[0]
    size = width // blocks
    if size % 16:
        ordered[:width, :] = turned
    else:
        for index in range(blocks):
            at = pl.multiple_of(place[index] * size, size)
            ordered[pl.ds(at, size), :] = turned[index * size : (index + 1) * size]
    ordered[width:, :] = jnp.ones((16, turned.shape[1]), bf16)


def weight_grad(ordered, right, keep, send, sums=None, at=0):
    width = ordered.shape[0] - 16
    middle, columns = width // 2, right.shape[1]
    tile = 512 if columns % 512 == 0 else columns

    def one(start):
        source = pl.ds(start, tile)
        target = pl.ds(at + start, tile)
        result = dot(ordered[...], right[:, source])
        send.ref[:, target] = result[middle:width].astype(bf16)
        keep.ref[:, target] = result[:middle].astype(bf16)
        if sums is not None:
            sums.ref[:, source] = result[width : width + 8]

    if tile == columns:
        one(0)
    else:

        @pl.loop(0, columns // tile)
        def _(index):
            one(pl.multiple_of(index * tile, tile))


def weight_kernel(blocks, given, made, ordered):
    place, left, right = given
    order_columns(left()[...], place, ordered, blocks)
    weight_grad(ordered, right(), *made)


def middle_kernel(blocks, given, made, normed_back, ordered):
    lengths, place, gain, norm_mine, norm_other, normed_two, inverse_two, cotangent, weight, mixed, wide = given
    used = rows_used(lengths)
    resid, grad_mixed, grad_features, sums, keep, send = made
    rows = norm_mine.ref.shape[0]
    block = 256
    sums.ref[...] = jnp.zeros_like(sums.ref)
    gain = gain()

    @pl.loop(0, rows // block)
    def _(index):
        span = row_span(index, block)
        for one in (normed_two, inverse_two, cotangent):
            one.ready(index)
        normed = normed_two.ref[span, :].astype(f32)
        grad_norm = norm_mine.ready(index)[span, :].astype(f32) + norm_other.ready(index)[
            span, :
        ].astype(f32)
        inverse = inverse_two.ref[span, 0:1]
        row = index * block + lax.broadcasted_iota(jnp.int32, (block, 1), 0)
        grad = jnp.where(row < used, cotangent.ref[span, :].astype(f32), 0.0)
        grad = grad + norm_back(grad_norm, normed, inverse, vector(gain))
        resid.ref[span, :] = grad
        resid.send(index)
        low = grad.astype(bf16)
        normed_back[span, :] = low
        sums.ref[0:1, :] += column_sum(grad_norm * normed)
        sums.ref[1:2, :] += column_sum(grad_norm)
        sums.ref[2:3, :] += column_sum(low.astype(f32))

    grad_mixed.ref[...] = dot_t(normed_back[...], weight()[...]).astype(bf16)
    wide = wide()

    @pl.loop(0, rows // block)
    def _(index):
        span = row_span(index, block)
        lane = lane_of((block, LANES))
        centres = jnp.zeros((block, LANES), f32)
        for pair in range(wide.shape[1] // LANES):
            cols = slice(pair * LANES, (pair + 1) * LANES)
            product = grad_mixed.ref[span, cols].astype(f32) * wide[span, cols]
            for half in range(2):
                centre = jnp.sum(head_half(product, half), axis=1, keepdims=True)
                centres = jnp.where(is_total(lane, 2 * pair + half), -centre, centres)
        grad_features.ref[span, :] = in_pieces(centres, lane).astype(bf16)

    order_columns(normed_back[...], place, ordered, blocks)
    weight_grad(ordered, mixed(), keep, send)


def attention_back_kernel(pair, blocks, given, made, wide_keys, wide_values, turned, key_total, value_total):
    given, before = given[:9], given[9:]
    place, keys, queries, values, id_k, features, grad_mixed, grad_features, hidden = given
    if pair == 0:
        *made, ordered = made
        ordered = ordered.ref
    queries, keys, values, id_k, features, grad_mixed, grad_features = (
        one() for one in (queries, keys, values, id_k, features, grad_mixed, grad_features)
    )
    grads, sums, keep, send = made
    rows = queries.shape[0]
    cols = slice(pair * LANES, (pair + 1) * LANES)
    lane = lane_of((1, LANES))
    key = keys[:, cols]
    turned[...] = key.T
    for half in range(2):
        wide_keys[half, :, :LANES] = key
        ones = is_total(lane, 2 * pair + half).astype(f32).astype(bf16)
        wide_keys[half, :, LANES:] = id_k[...] + ones
        wide_values[half, :, :LANES] = values[:, cols]
        wide_values[half, :, LANES:] = jnp.broadcast_to(ones, (rows, LANES))
    block = rows // 2
    key_total[...] = jnp.zeros_like(key_total)
    value_total[...] = jnp.zeros_like(value_total)

    @pl.loop(0, 2)
    def _(index):
        span = row_span(index, block)
        query, grad, feature = queries[span, cols], grad_mixed[span, cols], features[span, :]
        grad_feature = grad_features[span, :]
        key_term = value_term = None
        turned_grads = []
        for half in range(2):
            one_query, one_grad = head_half(query, half), head_half(grad, half)
            probs = jnp.exp(dot_t(wide_keys[half], jnp.concatenate([one_query, feature], axis=1)))
            centred = dot_t(wide_values[half], jnp.concatenate([one_grad, grad_feature], axis=1))
            grad_scores = (probs * centred).astype(bf16)
            value_one = dot(probs.astype(bf16), one_grad)
            key_one = dot(grad_scores, one_query)
            value_term = value_one if half == 0 else value_term + value_one
            key_term = key_one if half == 0 else key_term + key_one
            turned_grads.append(dot(turned[half * HEAD_DIM : (half + 1) * HEAD_DIM, :], grad_scores))
        key_total[...] += key_term
        value_total[...] += value_term
        grads.ref[span, :LANES] = (jnp.concatenate(turned_grads, axis=0).T * HEAD_DIM**-0.5).astype(bf16)

    grads.ref[:, LANES : 2 * LANES] = key_total[...].astype(bf16)
    grads.ref[:, 2 * LANES :] = value_total[...].astype(bf16)
    if pair == 0:
        order_columns(hidden()[...], place, ordered, blocks)
    else:
        ordered = hidden()
    at = 0
    for index in range(0, len(before), 2):
        columns = before[index].ref.shape[1]
        for target, source in zip((keep, send), before[index : index + 2]):
            target.ref[:, at : at + columns] = source()[...]
        at += columns
    weight_grad(ordered, grads.ref, keep, send, sums, at)


def first_kernel(given, made):
    *grads, weight = given
    weight, part = weight(), made[0]
    rows = part.ref.shape[0] // 4
    grads = [one() for one in grads]
    @pl.loop(0, 4)
    def _(index):
        span = row_span(index, rows)
        operand = jnp.concatenate(
            [one[span, kind * LANES : (kind + 1) * LANES] for kind in range(3) for one in grads], axis=1
        )
        full = jnp.concatenate([weight[kind] for kind in range(3)], axis=1)
        part.ref[span, :] = dot_t(operand, full).astype(bf16)


def last_kernel(given, made):
    gain, tokens, mine, other, resid, *sums = given
    out, vectors = made
    middle_sums, down_sums, up_sums, *pair_sums = (one()[...] for one in sums)
    block = tokens.ref.shape[0] // 4
    width = tokens.ref.shape[1]
    vectors.ref[...] = jnp.zeros_like(vectors.ref)
    gain, tokens, mine, other, resid = gain(), tokens(), mine(), other(), resid()

    @pl.loop(0, 4)
    def _(index):
        span = row_span(index, block)
        normed, inverse = normalize(tokens[span, :].astype(f32))
        grad_first = mine[span, :].astype(f32) + other[span, :].astype(f32)
        out.ref[span, :] = resid[span, :] + norm_back(grad_first, normed, inverse, vector(gain))
        out.send(index)
        vectors.ref[0:1, :] += column_sum(grad_first * normed)
        vectors.ref[1:2, :] += column_sum(grad_first)

    pairs = len(pair_sums)
    for pair, one in enumerate(pair_sums):
        for kind, start in ((0, 0), (2, pairs * LANES)):
            at = start + pair * LANES
            vectors.ref[2:3, at : at + LANES] = one[0:1, kind * LANES : (kind + 1) * LANES]
    vectors.ref[3:6, :] = middle_sums[0:3, :]
    vectors.ref[6:7, :] = down_sums
    for index in range(up_sums.shape[1] // width):
        vectors.ref[7 + index : 8 + index, :] = up_sums[0:1, index * width : (index + 1) * width]


def fold_kernel(joined, folded, given, made):
    at = 0
    for index in range(len(given) // 2):
        keep, came = given[2 * index](), given[2 * index + 1]()
        stays, sent = made[:2] if joined else made[2 * index : 2 * index + 2]
        cols = slice(at, at + keep.shape[1])
        at += keep.shape[1] if joined else 0
        if index < folded:
            stays.ref[:, cols] = keep[...]
            sent.ref[:, cols] = came[...]
            continue
        middle = keep.shape[0] // 2
        sent.ref[:, cols] = (keep[middle:].astype(f32) + came[middle:].astype(f32)).astype(bf16)
        stays.ref[:, cols] = keep[:middle].astype(f32) + came[:middle].astype(f32)


def add_kernel(given, made):
    made[0].ref[...] = given[0]()[...] + given[1]()[...]


def spread_kernel(given, made):
    total = given[0]()[...] + given[1]()[...]
    *singles, qv, ups = made
    width = total.shape[1]
    for row, one in zip((0, 1, 3, 4, 5, 6), singles):
        one.ref[...] = total[row]
    local = qv.ref.shape[1]
    for row in range(2):
        qv.ref[row : row + 1] = total[2:3, row * local : (row + 1) * local]
    for row in range(ups.ref.shape[0] // width):
        ups.ref[pl.ds(row * width, width)] = total[7 + row]


def output_kernel(given, made):
    out_bias, down_bias, tokens, part, other, down_part, down_other = given
    out = made[0]
    out_bias, down_bias, down_part, down_other = out_bias(), down_bias(), down_part(), down_other()
    block = out.ref.shape[0] // out.pieces

    @pl.loop(0, out.pieces)
    def _(index):
        span = row_span(index, block)
        for one in (tokens, part, other):
            one.ready(index)
        after = tokens.ref[span, :].astype(f32) + (
            part.ref[span, :].astype(f32) + other.ref[span, :].astype(f32) + vector(out_bias)
        )
        branch = down_part[span, :].astype(f32) + down_other[span, :].astype(f32) + vector(down_bias)
        out.ref[span, :] = (after + branch).astype(bf16)
        out.send(index)


def final_kernel(given, made):
    for index, one in enumerate(made):
        one.ref[...] = given[2 * index]()[...] + given[2 * index + 1]()[...].astype(f32)
        one.send()


def final_qkv_kernel(given, made):
    qkv, out = made
    keep, came = given
    total = keep()[...] + came()[...].astype(f32)
    local = out.ref.shape[1]
    out.ref[...] = total[:, :local]
    for pair in range(local // LANES):
        for kind in range(3):
            at = local + (3 * pair + kind) * LANES
            qkv.ref[kind, :, pair * LANES : (pair + 1) * LANES] = total[:, at : at + LANES]


def swap(values, axis, bit, size):
    return lax.ppermute(values, axis, [(i, i ^ (1 << bit)) for i in range(size)])


class Flow:
    def __init__(self, orders, size, keep, send):
        self.orders, self.size, self.keep, self.send, self.step = orders, size, keep, send, 0

    def exchange(self):
        pairs = [
            (2 * index + core, 2 * (index ^ (1 << order[self.step])) + core)
            for index in range(self.size)
            for core, order in enumerate(self.orders)
        ]
        self.came = lax.ppermute(self.send, ("dp", "mp"), pairs)
        self.step += 1


def fold(chain, flows, ready=(), covers=True):
    halved = [(flow.keep.shape[0] // 2, flow.keep.shape[1]) for flow in flows]
    if ready:
        columns = sum(flow.keep.shape[1] for flow in (*ready, *flows))
        halved = [(halved[0][0], columns)]
    outs = []
    for rows, columns in halved:
        outs += [Made((rows, columns), f32, "h" if rows <= 48 else "v"), Made((rows, columns), bf16, "v")]
    pairs = [(flow.keep, flow.send) for flow in ready] + [(flow.keep, flow.came) for flow in flows]
    results = call(
        chain,
        functools.partial(fold_kernel, bool(ready), len(ready)),
        "fold",
        outs,
        [Given(array, "v") for pair in pairs for array in pair],
        limit=8,
        covers=covers,
    )
    for index in range(len(halved)):
        flows[index].keep, flows[index].send = results[2 * index : 2 * index + 2]


def finish(chain, flows, kernel, shapes, covers=True):
    return call(
        chain,
        kernel,
        "final",
        [Made(shape, f32, "h") for shape in shapes],
        [Given(array, kind) for flow in flows for array, kind in ((flow.keep, "h"), (flow.came, "v"))],
        limit=8,
        covers=covers,
    )


def places(orders, size, me, core):
    source = jnp.arange(size, dtype=jnp.int32) ^ me
    found = []
    for order in orders:
        place = jnp.zeros((size,), jnp.int32)
        for step, bit in enumerate(order):
            place = place + (((source >> bit) & 1) << (size.bit_length() - 2 - step))
        found.append(place)
    return jnp.where(core == 0, *found)


def arranged(halves, place, size):
    keep, send = halves
    rows, columns = keep.shape
    if (2 * rows // size) % 16 == 0:
        return halves
    spots = jnp.zeros((size,), jnp.int32).at[place].set(jnp.arange(size, dtype=jnp.int32))
    both = jnp.concatenate(halves, axis=0).reshape(size, 2 * rows // size, columns)[spots]
    both = both.reshape(2 * rows, columns)
    return both[:rows], both[rows:]


def per_device(
    n_dp, tokens, cotangent, lengths, ln1_gain, ln1_bias, qkv_weight, qv_bias, out_weight, out_bias,
    ln2_gain, ln2_bias, up_weight, up_bias, down_weight, down_bias,
):
    chain = Chain()
    rows, width = tokens.shape
    local = qkv_weight.shape[2]
    units = up_weight.shape[1]
    pairs = local // LANES
    me, core = lax.axis_index("dp"), lax.axis_index("mp")
    bits = list(range(n_dp.bit_length() - 1))
    rest = bits[3:]
    near_orders = [[0, 1, 2, *rest], [1, 0, 2, *rest]]
    long_orders = [[2, 0, 1, *rest], [2, 1, 0, *rest]]
    near_place, long_place = (places(orders, n_dp, me, core) for orders in (near_orders, long_orders))
    weight = jnp.transpose(qkv_weight, (1, 0, 2))
    scalars = Given(lengths, "s")
    near = lambda array: Given(array, "v")
    far = lambda array, pieces=1: Given(array, "h", pieces)
    fetch = lambda array: Made(array.shape, array.dtype, "p", source=array)
    halves = lambda columns: [Made((width // 2, columns), bf16, "v")] * 2
    turned = pltpu.VMEM((width + 16, rows), bf16)

    hidden_one, queries, keys, values, id_k, mixed, mixed_wide, features, part = call(
        chain,
        qkv_kernel,
        "qkv_attention",
        [
            Made((rows, width), bf16, "h", 4),
            *[Made((rows, local), bf16, "h", 4)] * 3,
            Made((rows, LANES), bf16, "h", 4),
            Made((rows, local), bf16, "h"),
            Made((rows, local), f32, "h"),
            Made((rows, LANES), bf16, "h"),
            Made((rows, width), bf16, "v", 4),
        ],
        [
            scalars, far(ln1_gain), far(ln1_bias), far(tokens, 4), far(weight), far(qv_bias), far(out_weight)
        ],
        limit=28,
    )
    other = swap(part, "mp", 0, 2)
    (
        hidden_two, normed_two, inverse_two, activated, grad_pre, norm_part, down_sums,
        down_keep, down_send,
    ) = call(
        chain,
        functools.partial(mlp_kernel, n_dp),
        "mlp",
        [
            Made((rows, width), bf16, "v"),
            Made((rows, width), bf16, "h", 4),
            Made((rows, LANES), f32, "h", 4),
            Made((rows, units), bf16, "h", 2),
            Made((rows, units), bf16, "v"),
            Made((rows, width), bf16, "v"),
            Made((1, width), f32, "v"),
            *halves(units),
        ],
        [
            scalars,
            Given(near_place, "s"),
            *map(far, (out_bias, ln2_gain, ln2_bias)),
            far(tokens, 4),
            near(part),
            near(other),
            *map(far, (up_bias, up_weight, down_weight)),
            far(cotangent, 4),
        ],
        scratch=[turned, pltpu.VMEM((rows, width), bf16)],
        limit=30,
    )
    norm_other = swap(norm_part, "mp", 0, 2)

    def weights(name, left, right, place, with_sums=False):
        return call(
        chain,
            functools.partial(weight_kernel, n_dp),
            name,
            [*halves(units), *[Made((8, units), f32, "v")] * with_sums],
            [Given(place, "s"), near(left), near(right)],
            scratch=[turned],
            limit=10,
        )

    flow_down = Flow(near_orders, n_dp, *arranged((down_keep, down_send), near_place, n_dp))
    flow_down.exchange()
    up_keep, up_send, up_sums = weights("up_grad", hidden_two, grad_pre, long_place, True)
    flow_up = Flow(long_orders, n_dp, *arranged((up_keep, up_send), long_place, n_dp))
    flow_up.exchange()
    resid, grad_mixed, grad_features, middle_sums, out_keep, out_send = call(
        chain,
        functools.partial(middle_kernel, n_dp),
        "middle",
        [
            Made((rows, width), f32, "h", 4),
            Made((rows, local), bf16, "v"),
            Made((rows, LANES), bf16, "v"),
            Made((8, width), f32, "v"),
            *halves(local),
        ],
        [
            scalars,
            Given(near_place, "s"),
            far(ln2_gain),
            near(norm_part),
            near(norm_other),
            *map(near, (normed_two, inverse_two, cotangent)),
            near(out_weight),
            near(mixed),
            near(mixed_wide),
        ],
        scratch=[pltpu.VMEM((rows, width), bf16), turned],
        limit=16,
    )
    grads, sums, halves_qkv = [], [], []
    hiddens = [hidden_one]

    def attention_back(pair, before=()):
        columns = 3 * LANES + sum(keep.shape[1] for keep, _ in before)
        three, sums_one, keep, send, *order = call(
            chain,
            functools.partial(attention_back_kernel, pair, n_dp),
            "attention_back%d" % pair,
            [
                Made((rows, 3 * LANES), bf16, "v"),
                Made((8, 3 * LANES), f32, "v"),
                *halves(columns),
                *[Made((width + 16, rows), bf16, "h")] * (pair == 0),
            ],
            [
                Given(near_place, "s"),
                *map(near, (keys, queries, values, id_k, features, grad_mixed, grad_features)),
                near(hiddens[-1]),
                *(near(array) for pieces in before for array in pieces),
            ],
            scratch=[
                pltpu.VMEM((2, rows, 2 * LANES), bf16),
                pltpu.VMEM((2, rows, 2 * LANES), bf16),
                pltpu.VMEM((LANES, rows), bf16),
                pltpu.VMEM((rows, LANES), f32),
                pltpu.VMEM((rows, LANES), f32),
            ],
            limit=18,
        )
        hiddens.extend(order)
        grads.append(three)
        sums.append(sums_one)
        halves_qkv.append((keep, send))

    def exchange(*flows):
        for flow in flows:
            flow.exchange()

    def flow_of(pieces):
        return Flow(near_orders, n_dp, *arranged(pieces, near_place, n_dp))

    flow_out = flow_of((out_keep, out_send))
    exchange(flow_out)
    attention_back(0)
    flow_first = flow_of(halves_qkv[0])
    fold(chain, [flow_down, flow_out])
    exchange(flow_down, flow_first)
    for pair in range(1, pairs - 1):
        attention_back(pair)
    flows_next = [flow_of(pieces) for pieces in halves_qkv[1:]]
    fold(chain, [flow_down, flow_up, flow_first])
    exchange(flow_down, flow_up, *flows_next)
    attention_back(pairs - 1)
    flow_qkv = flow_of(halves_qkv[-1])
    exchange(flow_qkv)
    fold(chain, [flow_down, flow_up, *flows_next])
    exchange(flow_up)
    (first_part,) = call(
        chain,
        first_kernel,
        "first",
        [Made((rows, width), bf16, "v", 4)],
        [*map(near, grads), near(weight)],
        limit=10,
    )
    first_other = swap(first_part, "mp", 0, 2)
    fold(chain, [flow_qkv], [flow_out, flow_first, *flows_next])
    exchange(flow_qkv)
    fold(chain, [flow_up])
    last_step = len(rest) == 1
    if last_step:
        exchange(flow_down, flow_up)
    tokens_grad, vectors = call(
        chain,
        last_kernel,
        "last",
        [Made((rows, width), f32, "h", 4), Made((16, width), f32, "v")],
        [
            far(ln1_gain),
            *map(near, (tokens, first_part, first_other, resid, middle_sums, down_sums, up_sums, *sums)),
        ],
        limit=14,
    )
    shape = (width // n_dp, units)
    fold(chain, [flow_qkv], covers=False)
    exchange(flow_qkv)
    if last_step:
        down_total, up_total = finish(chain, [flow_down, flow_up], final_kernel, [shape] * 2, False)
    if not last_step:
        exchange(flow_down, flow_up)

    def all_sum_step(bit, covers=True):
        nonlocal vectors
        other = swap(vectors, "dp", bit, n_dp)
        (vectors,) = call(
            chain,
            add_kernel,
            "add",
            [Made((16, width), f32, "v")],
            [near(vectors), near(other)],
            limit=4,
            covers=covers,
        )

    all_sum_step(bits[0], False)
    (down_part,) = call(
        chain,
        down_kernel,
        "down",
        [Made((rows, width), bf16, "v", 4)],
        [near(down_weight), near(activated)],
        limit=10,
    )
    down_other = swap(down_part, "mp", 0, 2)
    fold(chain, [flow_qkv])
    exchange(flow_qkv)
    all_sum_step(bits[1], False)
    (output,) = call(
        chain,
        output_kernel,
        "output",
        [Made((rows, width), bf16, "h", 4)],
        [
            far(out_bias), far(down_bias), *(far(array, 4) for array in (tokens, part, other)), near(down_part),
            near(down_other),
        ],
        limit=16,
    )
    for bit in bits[2:-1]:
        all_sum_step(bit, False)
    flows = [flow_qkv, flow_up, flow_down]
    for step in range(1, len(rest)):
        fold(chain, flows)
        exchange(*flows)
    if not last_step:
        down_total, up_total = finish(chain, [flow_down, flow_up], final_kernel, [shape] * 2)
    mine = width // n_dp
    qkv_total, out_total = finish(
        chain, [flow_qkv], final_qkv_kernel, [(3, mine, local), (mine, local)]
    )
    *singles, qv_sum, up_sum = call(
        chain,
        spread_kernel,
        "spread",
        [*[Made((width,), f32, "h")] * 6, Made((2, local), f32, "h"), Made((units,), f32, "h")],
        [near(vectors), near(swap(vectors, "dp", bits[-1], n_dp))],
        limit=4,
    )
    gain_one, bias_one, gain_two, bias_two, out_bias_sum, down_bias_sum = singles
    return (
        output,
        tokens_grad,
        gain_one,
        bias_one,
        jnp.transpose(qkv_total, (1, 0, 2)),
        qv_sum,
        out_total.T,
        out_bias_sum,
        gain_two,
        bias_two,
        up_total,
        up_sum,
        down_total.T,
        down_bias_sum,
    )


def solution(mesh):
    return jax.shard_map(
        functools.partial(per_device, mesh.shape["dp"]),
        mesh=mesh,
        in_specs=(
            P("dp", None),
            P("dp", None),
            P("dp", None),
            P(),
            P(),
            P(None, None, "mp"),
            P(None, "mp"),
            P("mp", None),
            P(),
            P(),
            P(),
            P(None, "mp"),
            P("mp"),
            P("mp", None),
            P(),
        ),
        out_specs=(
            P("dp", None),
            P("dp", None),
            P(),
            P(),
            P("dp", None, "mp"),
            P(None, "mp"),
            P("mp", "dp"),
            P(),
            P(),
            P(),
            P("dp", "mp"),
            P("mp"),
            P("mp", "dp"),
            P(),
        ),
        check_vma=False,
    )
```

```python
import functools

import jax
import jax.numpy as jnp
from jax import lax
from jax.experimental import pallas as pl
from jax.experimental.pallas import tpu as pltpu
from jax.sharding import PartitionSpec as P

HEAD_DIM = 64
EPSILON = 1e-06
MASKED = 1e30
LANES = 128
TOTALS_AT = (32, 48, 64)
bf16 = jnp.bfloat16
f32 = jnp.float32


class Given:
    def __init__(self, array, kind, pieces=1, columns=None):
        self.array, self.kind, self.pieces, self.columns = array, kind, pieces, columns

    @property
    def shape(self):
        if self.columns is None:
            return self.array.shape
        return (self.array.shape[0], self.columns[1])


class Made:
    def __init__(self, shape, dtype, kind, pieces=1, source=None):
        self.shape, self.dtype, self.kind, self.pieces, self.source = shape, dtype, kind, pieces, source


def piece_span(piece, rows):
    if isinstance(piece, int):
        return pl.ds(piece * rows, rows)
    return pl.ds(pl.multiple_of(piece * rows, rows), rows)


class Arriving:
    def __init__(self, ref, source=None, semaphores=None, pieces=1, columns=None):
        self.ref, self.source, self.semaphores, self.pieces = ref, source, semaphores, pieces
        self.pending, self.columns = source is not None, columns

    def copy(self, piece):
        span = piece_span(piece, self.ref.shape[0] // self.pieces)
        source = self.source.at[span]
        if self.columns is not None:
            source = self.source.at[span, pl.ds(*self.columns)]
        return pltpu.make_async_copy(source, self.ref.at[span], self.semaphores.at[piece])

    def ready(self, piece):
        if self.source is not None:
            self.pending = False
            self.copy(piece).wait()
        return self.ref

    def __call__(self):
        if self.pending:
            for piece in range(self.pieces):
                self.copy(piece).wait()
            self.pending = False
        return self.ref


class Leaving:
    def __init__(self, ref, target, semaphores, pieces):
        self.ref, self.target, self.semaphores, self.pieces = ref, target, semaphores, pieces
        self.started = False

    def copy(self, piece):
        span = piece_span(piece, self.ref.shape[0] // self.pieces)
        return pltpu.make_async_copy(
            self.ref.at[span], self.target.at[span], self.semaphores.at[piece]
        )

    def send(self, piece=0):
        self.started = True
        self.copy(piece).start()

    def finish(self):
        if not self.started:
            for piece in range(self.pieces):
                self.send(piece)

    def wait(self):
        for piece in range(self.pieces):
            self.copy(piece).wait()


class Staying:
    def __init__(self, ref):
        self.ref = ref

    def send(self, piece=0):
        pass


pins = {"v": pltpu.VMEM, "h": pltpu.HBM, "c": pltpu.HBM, "p": pltpu.VMEM, "q": pltpu.HBM, "x": pltpu.HBM}


def pinned(given):
    if given.kind in "sw":
        return given.array
    return pltpu.with_memory_space_constraint(given.array, pins[given.kind])


class Chain:
    last = None


def call(chain, kernel, name, outs, args, scratch=(), limit=9, covers=True):
    if chain.last is not None and all(g.array is not chain.last for g in args):
        args = [*args, Given(chain.last, chain.kind)]
    ahead = [m for m in outs if m.kind == "p"]
    kernel_args = len(args)
    args = [*args, *(Given(m.source, "q") for m in ahead)]
    near = [g for g in args if g.kind == "h"]
    far = [m for m in outs if m.kind == "h"]
    copied = [m for m in outs if m.kind in "hc"]
    scratches = [pltpu.VMEM(g.shape, g.array.dtype) for g in near]
    scratches += [pltpu.VMEM(m.shape, m.dtype) for m in far]
    scratches += [pltpu.SemaphoreType.DMA((g.pieces,)) for g in near]
    scratches += [pltpu.SemaphoreType.DMA((m.pieces,)) for m in copied]
    scratches += [pltpu.SemaphoreType.DMA(()) for _ in ahead]

    def body(*refs):
        refs = list(refs)

        def take(count):
            taken = refs[:count]
            del refs[:count]
            return taken

        ins, results = take(len(args)), take(len(outs))
        arrivals, departures = take(len(near)), take(len(far))
        ready, gone = take(len(near)), take(len(copied))
        fetched = take(len(ahead))
        given, made, fetches = [], [], []
        for m, result in zip(outs, results):
            if m.kind == "p":
                source = ins[kernel_args + len(fetches)]
                fetches.append(pltpu.make_async_copy(source, result, fetched[len(fetches)]))
        for g, ref in zip(args, ins):
            if g.kind == "h":
                given.append(Arriving(arrivals.pop(0), ref, ready.pop(0), g.pieces, g.columns))
            elif g.kind not in "wxq":
                given.append(ref if g.kind == "s" else Arriving(ref))
        waiting = [one for one in given if isinstance(one, Arriving) and one.pending]
        small = [one for one in waiting if len(one.ref.shape) == 1]
        pieced = [one for one in waiting if one.pieces > 1]
        order = [(one, 0) for one in small]
        for piece in range(max((one.pieces for one in pieced), default=0)):
            order += [(one, piece) for one in pieced if piece < one.pieces]
        order += [(one, 0) for one in waiting if one not in small and one not in pieced]
        for one, piece in order:
            one.copy(piece).start()
        for copy in fetches:
            copy.start()
        for m, ref in zip(outs, results):
            if m.kind == "h":
                made.append(Leaving(departures.pop(0), ref, gone.pop(0), m.pieces))
            elif m.kind == "p":
                continue
            elif m.kind == "c":
                made[-1] = Leaving(made[-1].ref, ref, gone.pop(0), m.pieces)
            else:
                made.append(Staying(ref))
        kernel(given, made, *refs)
        for one in waiting:
            one()
        leaving = [one for one in made if isinstance(one, Leaving)]
        for one in leaving:
            one.finish()
        for one in leaving:
            one.wait()
        for copy in fetches:
            copy.wait()

    spaces = {"s": pltpu.SMEM, "v": pltpu.VMEM, "h": pltpu.HBM, "c": pltpu.HBM, "w": pl.ANY, "p": pltpu.VMEM, "q": pltpu.HBM, "x": pltpu.HBM}
    results = pl.pallas_call(
        body,
        name=name,
        out_shape=tuple(pins[m.kind](m.shape, m.dtype) for m in outs),
        in_specs=[pl.BlockSpec(memory_space=spaces[g.kind]) for g in args],
        out_specs=tuple(pl.BlockSpec(memory_space=spaces[m.kind]) for m in outs),
        scratch_shapes=[*scratches, *scratch],
        compiler_params=pltpu.CompilerParams(vmem_limit_bytes=limit << 20),
        cost_estimate=pl.CostEstimate(flops=2 * 10**10 * covers, bytes_accessed=1, transcendentals=0),
    )(*(pinned(g) for g in args))
    size = lambda pair: pair[0].size * pair[0].dtype.itemsize
    chain.last, kind = min(((result, m.kind) for m, result in zip(outs, results)), key=size)
    chain.kind = "x" if kind in "hc" else "w"
    return results


def dot(a, b):
    return jnp.dot(a, b, preferred_element_type=f32)


def dot_t(a, b):
    return lax.dot_general(a, b, (((1,), (1,)), ((), ())), preferred_element_type=f32)


def lane_of(shape):
    return lax.broadcasted_iota(jnp.int32, shape, 1)


def head_half(values, half):
    return jnp.where(lane_of(values.shape) // HEAD_DIM == half, values, jnp.zeros_like(values))


def normalize(values):
    centered = values - jnp.mean(values, axis=-1, keepdims=True)
    variance = jnp.mean(centered * centered, axis=-1, keepdims=True)
    inverse = lax.rsqrt(variance + EPSILON)
    return centered * inverse, inverse


def norm_back(grad_out, normed, inverse, gain):
    scaled = grad_out * gain
    return inverse * (
        scaled
        - jnp.mean(scaled, axis=-1, keepdims=True)
        - normed * jnp.mean(scaled * normed, axis=-1, keepdims=True)
    )


def column_sum(values):
    return jnp.sum(values, axis=0, keepdims=True)


def rows_used(lengths):
    used = jnp.int32(0)
    for slot in range(lengths.shape[1]):
        used = used + lengths[0, slot]
    return used


def row_span(index, size):
    if isinstance(index, int):
        return pl.ds(index * size, size)
    return pl.ds(pl.multiple_of(index * size, size), size)


def vector(ref):
    return ref[...][None, :]


def is_total(lane, head):
    found = lane == TOTALS_AT[0] + head
    for start in TOTALS_AT[1:]:
        found = found | (lane == start + head)
    return found


def in_pieces(values, lane):
    first = values.astype(bf16).astype(f32)
    second = (values - first).astype(bf16).astype(f32)
    third = values - first - second
    return jnp.where(lane < TOTALS_AT[1], first, jnp.where(lane < TOTALS_AT[2], second, third))


def attend(queries, keys, values, id_k, mixed, wide, features, block):
    lane = lane_of((block, LANES))

    @pl.loop(0, queries.shape[0] // block)
    def _(index):
        span = row_span(index, block)
        ids = features[span, :]
        feature = jnp.zeros((block, LANES), f32)
        for pair in range(queries.shape[1] // LANES):
            cols = slice(pair * LANES, (pair + 1) * LANES)
            wide_keys = jnp.concatenate([keys[:, cols], id_k[...]], axis=1)
            query, value = queries[span, cols], values[:, cols]
            total = None
            inverses = []
            for half in range(2):
                wide_query = jnp.concatenate([head_half(query, half), ids], axis=1)
                exponent = jnp.exp(dot_t(wide_query, wide_keys))
                totals = jnp.sum(exponent, axis=1, keepdims=True)
                term = dot(exponent.astype(bf16), head_half(value, half))
                total = term if total is None else total + term
                inverses.append(1.0 / totals)
                feature = jnp.where(is_total(lane, 2 * pair + half), -jnp.log(totals), feature)
            total = total * jnp.where(lane < HEAD_DIM, inverses[0], inverses[1])
            wide[span, cols] = total
            mixed[span, cols] = total.astype(bf16)
        features[span, :] = ids + in_pieces(feature, lane).astype(bf16)


def attend_shifted(queries, keys, values, id_k, mixed, wide, features, block):
    @pl.loop(0, queries.shape[0] // block)
    def _(index):
        span = row_span(index, block)
        ids = features[span, :]

        @pl.loop(0, queries.shape[1] // LANES)
        def _(pair):
            cols = row_span(pair, LANES)
            total = None
            for half in range(2):
                wide_query = jnp.concatenate([head_half(queries[span, cols], half), ids], axis=1)
                scores = dot_t(wide_query, jnp.concatenate([keys[:, cols], id_k[...]], axis=1))
                largest = jnp.max(scores, axis=1, keepdims=True)
                exponent = jnp.exp(scores - largest)
                totals = jnp.sum(exponent, axis=1, keepdims=True)
                term = dot(exponent.astype(bf16), head_half(values[:, cols], half)) / totals
                total = term if total is None else total + term
                lane = lane_of((block, LANES))
                feature = jnp.where(is_total(lane, 2 * pair + half), -(largest + jnp.log(totals)), 0.0)
                features[span, :] += in_pieces(feature, lane).astype(bf16)
            wide[span, cols] = total
            mixed[span, cols] = total.astype(bf16)


def largest_norms(array):
    found = jnp.zeros((1, 1), f32)
    for start in range(0, array.shape[1], LANES):
        values = array[:, start : start + LANES].astype(f32)
        squares = values * values
        both = jnp.sum(squares, axis=1, keepdims=True)
        one = jnp.sum(head_half(squares, 0), axis=1, keepdims=True)
        found = jnp.maximum(found, jnp.max(jnp.maximum(one, both - one), axis=0, keepdims=True))
    return jnp.max(found)


def qkv_kernel(given, made):
    lengths, gain, bias, tokens, weight, qv_bias, out_weight = given
    hidden, queries, keys, values, id_k, mixed, wide, features, part = made
    rows = tokens.ref.shape[0]
    slots = lengths.shape[1]
    lane = lane_of((1, LANES))
    starts = jnp.where(lane == 0, 0, rows)
    ends = jnp.full((1, LANES), rows, jnp.int32)
    running = jnp.int32(0)
    for slot in range(slots):
        running = running + lengths[0, slot]
        ends = jnp.where(lane == slot, running, ends)
        starts = jnp.where(lane == slot + 1, running, starts)
    scale = HEAD_DIM**-0.5
    block = rows // tokens.pieces
    gain, bias = gain(), bias()

    def norm(index):
        span = row_span(index, block) if not isinstance(index, int) else pl.ds(index * block, block)
        row = index * block + lax.broadcasted_iota(jnp.int32, (block, LANES), 0)
        same = (row >= starts) & (row < ends)
        features.ref[span, :] = same.astype(f32).astype(bf16)
        id_k.ref[span, :] = jnp.where(same | (lane > slots), 0.0, -MASKED).astype(bf16)
        normed, _ = normalize(tokens.ready(index)[span, :].astype(f32))
        hidden.ref[span, :] = (normed * vector(gain) + vector(bias)).astype(bf16)
        hidden.send(index)
        id_k.send(index)

    def project(index):
        span = row_span(index, block) if not isinstance(index, int) else pl.ds(index * block, block)
        low = hidden.ref[span, :]
        raised = (dot(low, weight[0]) + qv_bias[0:1, :]).astype(bf16)
        queries.ref[span, :] = (raised.astype(f32) * scale).astype(bf16)
        keys.ref[span, :] = dot(low, weight[1]).astype(bf16)
        values.ref[span, :] = (dot(low, weight[2]) + qv_bias[1:2, :]).astype(bf16)
        for one in (queries, keys, values):
            one.send(index)

    norm(0)
    weight, qv_bias = weight(), qv_bias()

    @pl.loop(0, tokens.pieces - 1)
    def _(index):
        project(index)
        norm(index + 1)

    project(tokens.pieces - 1)

    bounded = largest_norms(queries.ref) * largest_norms(keys.ref) <= 4000.0
    operands = [one.ref for one in (queries, keys, values, id_k, mixed, wide, features)]

    @pl.when(bounded)
    def _():
        attend(*operands, rows // 4)

    @pl.when(jnp.logical_not(bounded))
    def _():
        attend_shifted(*operands, LANES)

    for one in (mixed, wide, features):
        one.send()
    out_weight = out_weight()

    @pl.loop(0, 4)
    def _(index):
        span = row_span(index, rows // 4)
        part.ref[span, :] = dot(mixed.ref[span, :], out_weight[...]).astype(bf16)
        part.send(index)


def grad_active_kernel(blocks, given, made, grad_mlp):
    lengths, place, cotangent, down = given
    ordered, grad_active, down_bias_grad = made[:3]
    used = rows_used(lengths)
    rows = grad_mlp.shape[0]
    block = rows // cotangent.pieces
    down_bias_grad.ref[...] = jnp.zeros_like(down_bias_grad.ref)

    @pl.loop(0, cotangent.pieces)
    def _(index):
        span = row_span(index, block)
        row = index * block + lax.broadcasted_iota(jnp.int32, (block, 1), 0)
        grad = jnp.where(row < used, cotangent.ready(index)[span, :].astype(f32), 0.0)
        down_bias_grad.ref[...] += column_sum(grad)
        grad_mlp[span, :] = grad.astype(bf16)

    order_columns(grad_mlp[...], place, ordered.ref, blocks)
    down = down()

    @pl.loop(0, cotangent.pieces)
    def _(index):
        span = row_span(index, block)
        grad_active.ref[span, :] = dot_t(grad_mlp[span, :], down[...])


def mlp_kernel(given, made):
    out_bias, gain, bias, tokens, mine, other, up_bias, up, ordered, grad_active = given
    hidden, normed_two, inverse_two, active_out, grad_pre, part, keep, send = made
    rows = hidden.ref.shape[0]
    block, tile = rows // 4, 512
    out_bias, gain, bias = out_bias(), gain(), bias()

    @pl.loop(0, rows // block)
    def _(index):
        span = row_span(index, block)
        for one in (tokens, mine, other):
            one.ready(index)
        after = tokens.ref[span, :].astype(f32) + (
            mine.ref[span, :].astype(f32) + other.ref[span, :].astype(f32) + vector(out_bias)
        )
        normed, inverse = normalize(after)
        normed_two.ref[span, :] = normed.astype(bf16)
        inverse_two.ref[span, :] = jnp.broadcast_to(inverse, (block, LANES))
        hidden.ref[span, :] = (normed * vector(gain) + vector(bias)).astype(bf16)
        for one in (normed_two, inverse_two):
            one.send(index)

    up_bias, up, grad_active = up_bias(), up(), grad_active()

    block = rows // 2

    @pl.loop(0, rows // block)
    def _(index):
        span = row_span(index, block)
        low = hidden.ref[span, :]
        total = None
        for start in range(0, up.shape[1], tile):
            cols = slice(start, start + tile)
            pre = dot(low, up[:, cols]) + up_bias[cols][None, :]
            square = pre * pre
            inner = pre * (0.7978845608028654 + (0.7978845608028654 * 0.044715) * square)
            share = 0.5 + 0.5 * jnp.tanh(inner)
            active = pre * share
            active_out.ref[span, cols] = active.astype(bf16)
            slope = share + (active * (1.0 - share)) * (
                (2 * 0.7978845608028654) + (6 * 0.7978845608028654 * 0.044715) * square
            )
            grad_low = (grad_active[span, cols] * slope).astype(bf16)
            grad_pre.ref[span, cols] = grad_low
            term = dot_t(grad_low, up[:, cols])
            total = term if total is None else total + term
        active_out.send(index)
        part.ref[span, :] = total.astype(bf16)

    weight_grad(ordered(), active_out.ref, keep, send)


def down_kernel(given, made):
    weight, activated = given
    part = made[0]
    rows = activated.ref.shape[0] // 4
    weight = weight()
    activated = activated()

    @pl.loop(0, 4)
    def _(index):
        span = row_span(index, rows)
        part.ref[span, :] = dot(activated[span, :], weight[...]).astype(bf16)


def order_columns(values, place, ordered, blocks):
    turned = values.T
    width = turned.shape[0]
    size = width // blocks
    if size % 16:
        ordered[:width, :] = turned
    else:
        for index in range(blocks):
            at = pl.multiple_of(place[index] * size, size)
            ordered[pl.ds(at, size), :] = turned[index * size : (index + 1) * size]
    ordered[width:, :] = jnp.ones((16, turned.shape[1]), bf16)


def weight_grad(ordered, right, keep, send, sums=None, at=0):
    width = ordered.shape[0] - 16
    middle, columns = width // 2, right.shape[1]
    tile = 512 if columns % 512 == 0 else columns

    def one(start):
        source = pl.ds(start, tile)
        target = pl.ds(at + start, tile)
        result = dot(ordered[...], right[:, source])
        send.ref[:, target] = result[middle:width].astype(bf16)
        keep.ref[:, target] = result[:middle].astype(bf16)
        if sums is not None:
            sums.ref[:, source] = result[width : width + 8]

    if tile == columns:
        one(0)
    else:

        @pl.loop(0, columns // tile)
        def _(index):
            one(pl.multiple_of(index * tile, tile))


def weight_kernel(blocks, given, made, ordered):
    place, left, right = given
    order_columns(left()[...], place, ordered, blocks)
    weight_grad(ordered, right(), *made)


def middle_kernel(blocks, given, made, normed_back, ordered):
    lengths, place, gain, norm_mine, norm_other, normed_two, inverse_two, cotangent, weight, mixed, wide = given
    used = rows_used(lengths)
    resid, grad_mixed, grad_features, sums, keep, send = made
    rows = norm_mine.ref.shape[0]
    block = 256
    sums.ref[...] = jnp.zeros_like(sums.ref)
    gain = gain()

    @pl.loop(0, rows // block)
    def _(index):
        span = row_span(index, block)
        for one in (normed_two, inverse_two, cotangent):
            one.ready(index)
        normed = normed_two.ref[span, :].astype(f32)
        grad_norm = norm_mine.ready(index)[span, :].astype(f32) + norm_other.ready(index)[
            span, :
        ].astype(f32)
        inverse = inverse_two.ref[span, 0:1]
        row = index * block + lax.broadcasted_iota(jnp.int32, (block, 1), 0)
        grad = jnp.where(row < used, cotangent.ref[span, :].astype(f32), 0.0)
        grad = grad + norm_back(grad_norm, normed, inverse, vector(gain))
        resid.ref[span, :] = grad
        resid.send(index)
        low = grad.astype(bf16)
        normed_back[span, :] = low
        sums.ref[0:1, :] += column_sum(grad_norm * normed)
        sums.ref[1:2, :] += column_sum(grad_norm)
        sums.ref[2:3, :] += column_sum(low.astype(f32))

    grad_mixed.ref[...] = dot_t(normed_back[...], weight()[...]).astype(bf16)
    wide = wide()

    @pl.loop(0, rows // block)
    def _(index):
        span = row_span(index, block)
        lane = lane_of((block, LANES))
        centres = jnp.zeros((block, LANES), f32)
        for pair in range(wide.shape[1] // LANES):
            cols = slice(pair * LANES, (pair + 1) * LANES)
            product = grad_mixed.ref[span, cols].astype(f32) * wide[span, cols]
            for half in range(2):
                centre = jnp.sum(head_half(product, half), axis=1, keepdims=True)
                centres = jnp.where(is_total(lane, 2 * pair + half), -centre, centres)
        grad_features.ref[span, :] = in_pieces(centres, lane).astype(bf16)

    order_columns(normed_back[...], place, ordered, blocks)
    weight_grad(ordered, mixed(), keep, send)


def attention_back_kernel(pair, blocks, given, made, wide_keys, wide_values, turned, key_total, value_total):
    given, before = given[:9], given[9:]
    place, keys, queries, values, id_k, features, grad_mixed, grad_features, hidden = given
    if pair == 0:
        *made, ordered = made
        ordered = ordered.ref
    queries, keys, values, id_k, features, grad_mixed, grad_features = (
        one() for one in (queries, keys, values, id_k, features, grad_mixed, grad_features)
    )
    grads, sums, keep, send = made
    rows = queries.shape[0]
    cols = slice(pair * LANES, (pair + 1) * LANES)
    lane = lane_of((1, LANES))
    key = keys[:, cols]
    turned[...] = key.T
    for half in range(2):
        wide_keys[half, :, :LANES] = key
        ones = is_total(lane, 2 * pair + half).astype(f32).astype(bf16)
        wide_keys[half, :, LANES:] = id_k[...] + ones
        wide_values[half, :, :LANES] = values[:, cols]
        wide_values[half, :, LANES:] = jnp.broadcast_to(ones, (rows, LANES))
    block = rows // 2
    key_total[...] = jnp.zeros_like(key_total)
    value_total[...] = jnp.zeros_like(value_total)

    def half_of_queries(index):
        span = row_span(index, block)
        query, grad, feature = queries[span, cols], grad_mixed[span, cols], features[span, :]
        grad_feature = grad_features[span, :]
        key_term = value_term = None
        turned_grads = []
        for half in range(2):
            one_query, one_grad = head_half(query, half), head_half(grad, half)
            probs = jnp.exp(dot_t(wide_keys[half], jnp.concatenate([one_query, feature], axis=1)))
            centred = dot_t(wide_values[half], jnp.concatenate([one_grad, grad_feature], axis=1))
            grad_scores = (probs * centred).astype(bf16)
            value_one = dot(probs.astype(bf16), one_grad)
            key_one = dot(grad_scores, one_query)
            value_term = value_one if half == 0 else value_term + value_one
            key_term = key_one if half == 0 else key_term + key_one
            turned_grads.append(dot(turned[half * HEAD_DIM : (half + 1) * HEAD_DIM, :], grad_scores))
        key_total[...] += key_term
        value_total[...] += value_term
        grads.ref[span, :LANES] = (jnp.concatenate(turned_grads, axis=0).T * HEAD_DIM**-0.5).astype(bf16)

    if pair == 0:
        half_of_queries(0)
        half_of_queries(1)
    else:
        pl.loop(0, 2)(half_of_queries)

    grads.ref[:, LANES : 2 * LANES] = key_total[...].astype(bf16)
    grads.ref[:, 2 * LANES :] = value_total[...].astype(bf16)
    if pair == 0:
        order_columns(hidden()[...], place, ordered, blocks)
    else:
        ordered = hidden()
    at = 0
    for index in range(0, len(before), 2):
        columns = before[index].ref.shape[1]
        for target, source in zip((keep, send), before[index : index + 2]):
            target.ref[:, at : at + columns] = source()[...]
        at += columns
    weight_grad(ordered, grads.ref, keep, send, sums, at)


def first_kernel(given, made):
    *grads, weight = given
    weight, part = weight(), made[0]
    rows = part.ref.shape[0] // 4
    grads = [one() for one in grads]
    @pl.loop(0, 4)
    def _(index):
        span = row_span(index, rows)
        operand = jnp.concatenate(
            [one[span, kind * LANES : (kind + 1) * LANES] for kind in range(3) for one in grads], axis=1
        )
        full = jnp.concatenate([weight[kind] for kind in range(3)], axis=1)
        part.ref[span, :] = dot_t(operand, full).astype(bf16)


def last_kernel(given, made):
    gain, tokens, mine, other, resid, *sums = given
    out, vectors = made
    middle_sums, down_sums, up_sums, *pair_sums = (one()[...] for one in sums)
    block = tokens.ref.shape[0] // 4
    width = tokens.ref.shape[1]
    vectors.ref[...] = jnp.zeros_like(vectors.ref)
    gain, tokens, mine, other, resid = gain(), tokens(), mine(), other(), resid()

    @pl.loop(0, 4)
    def _(index):
        span = row_span(index, block)
        normed, inverse = normalize(tokens[span, :].astype(f32))
        grad_first = mine[span, :].astype(f32) + other[span, :].astype(f32)
        out.ref[span, :] = resid[span, :] + norm_back(grad_first, normed, inverse, vector(gain))
        out.send(index)
        vectors.ref[0:1, :] += column_sum(grad_first * normed)
        vectors.ref[1:2, :] += column_sum(grad_first)

    pairs = len(pair_sums)
    for pair, one in enumerate(pair_sums):
        for kind, start in ((0, 0), (2, pairs * LANES)):
            at = start + pair * LANES
            vectors.ref[2:3, at : at + LANES] = one[0:1, kind * LANES : (kind + 1) * LANES]
    vectors.ref[3:6, :] = middle_sums[0:3, :]
    vectors.ref[6:7, :] = down_sums
    for index in range(up_sums.shape[1] // width):
        vectors.ref[7 + index : 8 + index, :] = up_sums[0:1, index * width : (index + 1) * width]


def fold_kernel(joined, folded, given, made):
    at = 0
    for index in range(len(given) // 2):
        keep, came = given[2 * index](), given[2 * index + 1]()
        stays, sent = made[:2] if joined else made[2 * index : 2 * index + 2]
        cols = slice(at, at + keep.shape[1])
        at += keep.shape[1] if joined else 0
        if index < folded:
            stays.ref[:, cols] = keep[...]
            sent.ref[:, cols] = came[...]
            continue
        middle = keep.shape[0] // 2
        sent.ref[:, cols] = (keep[middle:].astype(f32) + came[middle:].astype(f32)).astype(bf16)
        stays.ref[:, cols] = keep[:middle].astype(f32) + came[:middle].astype(f32)


def add_kernel(given, made):
    made[0].ref[...] = given[0]()[...] + given[1]()[...]


def spread_kernel(given, made):
    total = given[0]()[...] + given[1]()[...]
    *singles, qv, ups = made
    width = total.shape[1]
    for row, one in zip((0, 1, 3, 4, 5, 6), singles):
        one.ref[...] = total[row]
    local = qv.ref.shape[1]
    for row in range(2):
        qv.ref[row : row + 1] = total[2:3, row * local : (row + 1) * local]
    for row in range(ups.ref.shape[0] // width):
        ups.ref[pl.ds(row * width, width)] = total[7 + row]


def output_kernel(given, made):
    out_bias, down_bias, tokens, part, other, down_part, down_other = given
    out = made[0]
    out_bias, down_bias, down_part, down_other = out_bias(), down_bias(), down_part(), down_other()
    block = out.ref.shape[0] // out.pieces

    @pl.loop(0, out.pieces)
    def _(index):
        span = row_span(index, block)
        for one in (tokens, part, other):
            one.ready(index)
        after = tokens.ref[span, :].astype(f32) + (
            part.ref[span, :].astype(f32) + other.ref[span, :].astype(f32) + vector(out_bias)
        )
        branch = down_part[span, :].astype(f32) + down_other[span, :].astype(f32) + vector(down_bias)
        out.ref[span, :] = (after + branch).astype(bf16)
        out.send(index)


def final_kernel(given, made):
    for index, one in enumerate(made):
        one.ref[...] = given[2 * index]()[...] + given[2 * index + 1]()[...].astype(f32)
        one.send()


def final_qkv_kernel(given, made):
    qkv, out = made
    keep, came = given
    total = keep()[...] + came()[...].astype(f32)
    local = out.ref.shape[1]
    out.ref[...] = total[:, :local]
    for pair in range(local // LANES):
        for kind in range(3):
            at = local + (3 * pair + kind) * LANES
            qkv.ref[kind, :, pair * LANES : (pair + 1) * LANES] = total[:, at : at + LANES]


def swap(values, axis, bit, size):
    return lax.ppermute(values, axis, [(i, i ^ (1 << bit)) for i in range(size)])


class Flow:
    def __init__(self, orders, size, keep, send):
        self.orders, self.size, self.keep, self.send, self.step = orders, size, keep, send, 0

    def exchange(self):
        pairs = [
            (2 * index + core, 2 * (index ^ (1 << order[self.step])) + core)
            for index in range(self.size)
            for core, order in enumerate(self.orders)
        ]
        self.came = lax.ppermute(self.send, ("dp", "mp"), pairs)
        self.step += 1


def fold(chain, flows, ready=(), covers=True):
    halved = [(flow.keep.shape[0] // 2, flow.keep.shape[1]) for flow in flows]
    if ready:
        columns = sum(flow.keep.shape[1] for flow in (*ready, *flows))
        halved = [(halved[0][0], columns)]
    outs = []
    for rows, columns in halved:
        outs += [Made((rows, columns), f32, "h" if rows <= 48 else "v"), Made((rows, columns), bf16, "v")]
    pairs = [(flow.keep, flow.send) for flow in ready] + [(flow.keep, flow.came) for flow in flows]
    results = call(
        chain,
        functools.partial(fold_kernel, bool(ready), len(ready)),
        "fold",
        outs,
        [Given(array, "v") for pair in pairs for array in pair],
        limit=8,
        covers=covers,
    )
    for index in range(len(halved)):
        flows[index].keep, flows[index].send = results[2 * index : 2 * index + 2]


def finish(chain, flows, kernel, shapes, covers=True):
    return call(
        chain,
        kernel,
        "final",
        [Made(shape, f32, "h") for shape in shapes],
        [Given(array, kind) for flow in flows for array, kind in ((flow.keep, "h"), (flow.came, "v"))],
        limit=8,
        covers=covers,
    )


def places(orders, size, me, core):
    source = jnp.arange(size, dtype=jnp.int32) ^ me
    found = []
    for order in orders:
        place = jnp.zeros((size,), jnp.int32)
        for step, bit in enumerate(order):
            place = place + (((source >> bit) & 1) << (size.bit_length() - 2 - step))
        found.append(place)
    return jnp.where(core == 0, *found)


def arranged(halves, place, size):
    keep, send = halves
    rows, columns = keep.shape
    if (2 * rows // size) % 16 == 0:
        return halves
    spots = jnp.zeros((size,), jnp.int32).at[place].set(jnp.arange(size, dtype=jnp.int32))
    both = jnp.concatenate(halves, axis=0).reshape(size, 2 * rows // size, columns)[spots]
    both = both.reshape(2 * rows, columns)
    return both[:rows], both[rows:]


def per_device(
    n_dp, tokens, cotangent, lengths, ln1_gain, ln1_bias, qkv_weight, qv_bias, out_weight, out_bias,
    ln2_gain, ln2_bias, up_weight, up_bias, down_weight, down_bias,
):
    chain = Chain()
    rows, width = tokens.shape
    local = qkv_weight.shape[2]
    units = up_weight.shape[1]
    pairs = local // LANES
    me, core = lax.axis_index("dp"), lax.axis_index("mp")
    bits = list(range(n_dp.bit_length() - 1))
    rest = bits[3:]
    near_orders = [[0, 1, 2, *rest], [1, 0, 2, *rest]]
    long_orders = [[2, 0, 1, *rest], [2, 1, 0, *rest]]
    near_place, long_place = (places(orders, n_dp, me, core) for orders in (near_orders, long_orders))
    weight = jnp.transpose(qkv_weight, (1, 0, 2))
    scalars = Given(lengths, "s")
    near = lambda array: Given(array, "v")
    far = lambda array, pieces=1: Given(array, "h", pieces)
    fetch = lambda array: Made(array.shape, array.dtype, "p", source=array)
    halves = lambda columns: [Made((width // 2, columns), bf16, "v")] * 2
    turned = pltpu.VMEM((width + 16, rows), bf16)

    hidden_one, queries, keys, values, id_k, mixed, mixed_wide, features, part = call(
        chain,
        qkv_kernel,
        "qkv_attention",
        [
            Made((rows, width), bf16, "h", 4),
            *[Made((rows, local), bf16, "h", 4)] * 3,
            Made((rows, LANES), bf16, "h", 4),
            Made((rows, local), bf16, "h"),
            Made((rows, local), f32, "h"),
            Made((rows, LANES), bf16, "h"),
            Made((rows, width), bf16, "v", 4),
        ],
        [
            scalars, far(ln1_gain), far(ln1_bias), far(tokens, 4), far(weight), far(qv_bias), far(out_weight)
        ],
        limit=28,
    )
    other = swap(part, "mp", 0, 2)
    turned_grad, grad_active, down_sums, near_tokens, near_up = call(
        chain,
        functools.partial(grad_active_kernel, n_dp),
        "grad_active",
        [
            Made((width + 16, rows), bf16, "v"),
            Made((rows, units), f32, "v"),
            Made((1, width), f32, "v"),
            fetch(tokens),
            fetch(up_weight),
        ],
        [scalars, Given(near_place, "s"), far(cotangent, 4), far(down_weight)],
        scratch=[pltpu.VMEM((rows, width), bf16)],
        limit=16,
    )
    hidden_two, normed_two, inverse_two, activated, grad_pre, norm_part, down_keep, down_send = call(
        chain,
        mlp_kernel,
        "mlp",
        [
            Made((rows, width), bf16, "v"),
            Made((rows, width), bf16, "h", 4),
            Made((rows, LANES), f32, "h", 4),
            Made((rows, units), bf16, "h", 2),
            Made((rows, units), bf16, "v"),
            Made((rows, width), bf16, "v"),
            *halves(units),
        ],
        [
            *map(far, (out_bias, ln2_gain, ln2_bias)),
            *map(near, (near_tokens, part, other)),
            far(up_bias),
            near(near_up),
            near(turned_grad),
            near(grad_active),
        ],
        limit=22,
    )
    norm_other = swap(norm_part, "mp", 0, 2)

    def weights(name, left, right, place, with_sums=False):
        return call(
        chain,
            functools.partial(weight_kernel, n_dp),
            name,
            [*halves(units), *[Made((8, units), f32, "v")] * with_sums],
            [Given(place, "s"), near(left), near(right)],
            scratch=[turned],
            limit=10,
        )

    flow_down = Flow(near_orders, n_dp, *arranged((down_keep, down_send), near_place, n_dp))
    flow_down.exchange()
    up_keep, up_send, up_sums = weights("up_grad", hidden_two, grad_pre, long_place, True)
    flow_up = Flow(long_orders, n_dp, *arranged((up_keep, up_send), long_place, n_dp))
    flow_up.exchange()
    resid, grad_mixed, grad_features, middle_sums, out_keep, out_send = call(
        chain,
        functools.partial(middle_kernel, n_dp),
        "middle",
        [
            Made((rows, width), f32, "h", 4),
            Made((rows, local), bf16, "v"),
            Made((rows, LANES), bf16, "v"),
            Made((8, width), f32, "v"),
            *halves(local),
        ],
        [
            scalars,
            Given(near_place, "s"),
            far(ln2_gain),
            near(norm_part),
            near(norm_other),
            *map(near, (normed_two, inverse_two, cotangent)),
            near(out_weight),
            near(mixed),
            near(mixed_wide),
        ],
        scratch=[pltpu.VMEM((rows, width), bf16), turned],
        limit=16,
    )
    grads, sums, halves_qkv = [], [], []
    hiddens = [hidden_one]

    def attention_back(pair, before=()):
        columns = 3 * LANES + sum(keep.shape[1] for keep, _ in before)
        three, sums_one, keep, send, *order = call(
            chain,
            functools.partial(attention_back_kernel, pair, n_dp),
            "attention_back%d" % pair,
            [
                Made((rows, 3 * LANES), bf16, "v"),
                Made((8, 3 * LANES), f32, "v"),
                *halves(columns),
                *[Made((width + 16, rows), bf16, "h")] * (pair == 0),
            ],
            [
                Given(near_place, "s"),
                *map(near, (keys, queries, values, id_k, features, grad_mixed, grad_features)),
                near(hiddens[-1]),
                *(near(array) for pieces in before for array in pieces),
            ],
            scratch=[
                pltpu.VMEM((2, rows, 2 * LANES), bf16),
                pltpu.VMEM((2, rows, 2 * LANES), bf16),
                pltpu.VMEM((LANES, rows), bf16),
                pltpu.VMEM((rows, LANES), f32),
                pltpu.VMEM((rows, LANES), f32),
            ],
            limit=18,
        )
        hiddens.extend(order)
        grads.append(three)
        sums.append(sums_one)
        halves_qkv.append((keep, send))

    def exchange(*flows):
        for flow in flows:
            flow.exchange()

    def flow_of(pieces):
        return Flow(near_orders, n_dp, *arranged(pieces, near_place, n_dp))

    flow_out = flow_of((out_keep, out_send))
    exchange(flow_out)
    attention_back(0)
    flow_first = flow_of(halves_qkv[0])
    fold(chain, [flow_down, flow_out])
    exchange(flow_down, flow_first)
    for pair in range(1, pairs - 1):
        attention_back(pair)
    flows_next = [flow_of(pieces) for pieces in halves_qkv[1:]]
    fold(chain, [flow_down, flow_up, flow_first])
    exchange(flow_down, flow_up, *flows_next)
    attention_back(pairs - 1)
    flow_qkv = flow_of(halves_qkv[-1])
    exchange(flow_qkv)
    fold(chain, [flow_down, flow_up, *flows_next])
    exchange(flow_up)
    (first_part,) = call(
        chain,
        first_kernel,
        "first",
        [Made((rows, width), bf16, "v", 4)],
        [*map(near, grads), near(weight)],
        limit=10,
    )
    first_other = swap(first_part, "mp", 0, 2)
    fold(chain, [flow_qkv], [flow_out, flow_first, *flows_next])
    exchange(flow_qkv)
    fold(chain, [flow_up])
    last_step = len(rest) == 1
    if last_step:
        exchange(flow_down, flow_up)
    tokens_grad, vectors = call(
        chain,
        last_kernel,
        "last",
        [Made((rows, width), f32, "h", 4), Made((16, width), f32, "v")],
        [
            far(ln1_gain),
            *map(near, (tokens, first_part, first_other, resid, middle_sums, down_sums, up_sums, *sums)),
        ],
        limit=14,
    )
    shape = (width // n_dp, units)
    fold(chain, [flow_qkv], covers=False)
    exchange(flow_qkv)
    if last_step:
        down_total, up_total = finish(chain, [flow_down, flow_up], final_kernel, [shape] * 2, False)
    if not last_step:
        exchange(flow_down, flow_up)

    def all_sum_step(bit, covers=True):
        nonlocal vectors
        other = swap(vectors, "dp", bit, n_dp)
        (vectors,) = call(
            chain,
            add_kernel,
            "add",
            [Made((16, width), f32, "v")],
            [near(vectors), near(other)],
            limit=4,
            covers=covers,
        )

    all_sum_step(bits[0], False)
    (down_part,) = call(
        chain,
        down_kernel,
        "down",
        [Made((rows, width), bf16, "v", 4)],
        [near(down_weight), near(activated)],
        limit=10,
    )
    down_other = swap(down_part, "mp", 0, 2)
    fold(chain, [flow_qkv])
    exchange(flow_qkv)
    all_sum_step(bits[1], False)
    (output,) = call(
        chain,
        output_kernel,
        "output",
        [Made((rows, width), bf16, "h", 4)],
        [
            far(out_bias), far(down_bias), *(far(array, 4) for array in (tokens, part, other)), near(down_part),
            near(down_other),
        ],
        limit=16,
    )
    for bit in bits[2:-1]:
        all_sum_step(bit, False)
    flows = [flow_qkv, flow_up, flow_down]
    for step in range(1, len(rest)):
        fold(chain, flows)
        exchange(*flows)
    if not last_step:
        down_total, up_total = finish(chain, [flow_down, flow_up], final_kernel, [shape] * 2)
    mine = width // n_dp
    qkv_total, out_total = finish(
        chain, [flow_qkv], final_qkv_kernel, [(3, mine, local), (mine, local)]
    )
    *singles, qv_sum, up_sum = call(
        chain,
        spread_kernel,
        "spread",
        [*[Made((width,), f32, "h")] * 6, Made((2, local), f32, "h"), Made((units,), f32, "h")],
        [near(vectors), near(swap(vectors, "dp", bits[-1], n_dp))],
        limit=4,
    )
    gain_one, bias_one, gain_two, bias_two, out_bias_sum, down_bias_sum = singles
    return (
        output,
        tokens_grad,
        gain_one,
        bias_one,
        jnp.transpose(qkv_total, (1, 0, 2)),
        qv_sum,
        out_total.T,
        out_bias_sum,
        gain_two,
        bias_two,
        up_total,
        up_sum,
        down_total.T,
        down_bias_sum,
    )


def solution(mesh):
    return jax.shard_map(
        functools.partial(per_device, mesh.shape["dp"]),
        mesh=mesh,
        in_specs=(
            P("dp", None),
            P("dp", None),
            P("dp", None),
            P(),
            P(),
            P(None, None, "mp"),
            P(None, "mp"),
            P("mp", None),
            P(),
            P(),
            P(),
            P(None, "mp"),
            P("mp"),
            P("mp", None),
            P(),
        ),
        out_specs=(
            P("dp", None),
            P("dp", None),
            P(),
            P(),
            P("dp", None, "mp"),
            P(None, "mp"),
            P("mp", "dp"),
            P(),
            P(),
            P(),
            P("dp", "mp"),
            P("mp"),
            P("mp", "dp"),
            P(),
        ),
        check_vma=False,
    )
```

```python
import functools

import jax
import jax.numpy as jnp
from jax import lax
from jax.experimental import pallas as pl
from jax.experimental.pallas import tpu as pltpu
from jax.sharding import PartitionSpec as P

HEAD_DIM = 64
EPSILON = 1e-06
MASKED = 1e30
LANES = 128
TOTALS_AT = (32, 48, 64)
bf16 = jnp.bfloat16
f32 = jnp.float32


class Given:
    def __init__(self, array, kind, pieces=1, columns=None):
        self.array, self.kind, self.pieces, self.columns = array, kind, pieces, columns

    @property
    def shape(self):
        if self.columns is None:
            return self.array.shape
        return (self.array.shape[0], self.columns[1])


class Made:
    def __init__(self, shape, dtype, kind, pieces=1, source=None):
        self.shape, self.dtype, self.kind, self.pieces, self.source = shape, dtype, kind, pieces, source


def piece_span(piece, rows):
    if isinstance(piece, int):
        return pl.ds(piece * rows, rows)
    return pl.ds(pl.multiple_of(piece * rows, rows), rows)


class Arriving:
    def __init__(self, ref, source=None, semaphores=None, pieces=1, columns=None):
        self.ref, self.source, self.semaphores, self.pieces = ref, source, semaphores, pieces
        self.pending, self.columns = source is not None, columns

    def copy(self, piece):
        span = piece_span(piece, self.ref.shape[0] // self.pieces)
        source = self.source.at[span]
        if self.columns is not None:
            source = self.source.at[span, pl.ds(*self.columns)]
        return pltpu.make_async_copy(source, self.ref.at[span], self.semaphores.at[piece])

    def ready(self, piece):
        if self.source is not None:
            self.pending = False
            self.copy(piece).wait()
        return self.ref

    def __call__(self):
        if self.pending:
            for piece in range(self.pieces):
                self.copy(piece).wait()
            self.pending = False
        return self.ref


class Leaving:
    def __init__(self, ref, target, semaphores, pieces):
        self.ref, self.target, self.semaphores, self.pieces = ref, target, semaphores, pieces
        self.started = False

    def copy(self, piece):
        span = piece_span(piece, self.ref.shape[0] // self.pieces)
        return pltpu.make_async_copy(
            self.ref.at[span], self.target.at[span], self.semaphores.at[piece]
        )

    def send(self, piece=0):
        self.started = True
        self.copy(piece).start()

    def finish(self):
        if not self.started:
            for piece in range(self.pieces):
                self.send(piece)

    def wait(self):
        for piece in range(self.pieces):
            self.copy(piece).wait()


class Staying:
    def __init__(self, ref):
        self.ref = ref

    def send(self, piece=0):
        pass


pins = {"v": pltpu.VMEM, "h": pltpu.HBM, "c": pltpu.HBM, "p": pltpu.VMEM, "q": pltpu.HBM, "x": pltpu.HBM}


def pinned(given):
    if given.kind in "sw":
        return given.array
    return pltpu.with_memory_space_constraint(given.array, pins[given.kind])


class Chain:
    last = None


def call(chain, kernel, name, outs, args, scratch=(), limit=9, covers=True):
    if chain.last is not None and all(g.array is not chain.last for g in args):
        args = [*args, Given(chain.last, chain.kind)]
    ahead = [m for m in outs if m.kind == "p"]
    kernel_args = len(args)
    args = [*args, *(Given(m.source, "q") for m in ahead)]
    near = [g for g in args if g.kind == "h"]
    far = [m for m in outs if m.kind == "h"]
    copied = [m for m in outs if m.kind in "hc"]
    scratches = [pltpu.VMEM(g.shape, g.array.dtype) for g in near]
    scratches += [pltpu.VMEM(m.shape, m.dtype) for m in far]
    scratches += [pltpu.SemaphoreType.DMA((g.pieces,)) for g in near]
    scratches += [pltpu.SemaphoreType.DMA((m.pieces,)) for m in copied]
    scratches += [pltpu.SemaphoreType.DMA(()) for _ in ahead]

    def body(*refs):
        refs = list(refs)

        def take(count):
            taken = refs[:count]
            del refs[:count]
            return taken

        ins, results = take(len(args)), take(len(outs))
        arrivals, departures = take(len(near)), take(len(far))
        ready, gone = take(len(near)), take(len(copied))
        fetched = take(len(ahead))
        given, made, fetches = [], [], []
        for m, result in zip(outs, results):
            if m.kind == "p":
                source = ins[kernel_args + len(fetches)]
                fetches.append(pltpu.make_async_copy(source, result, fetched[len(fetches)]))
        for g, ref in zip(args, ins):
            if g.kind == "h":
                given.append(Arriving(arrivals.pop(0), ref, ready.pop(0), g.pieces, g.columns))
            elif g.kind not in "wxq":
                given.append(ref if g.kind == "s" else Arriving(ref))
        waiting = [one for one in given if isinstance(one, Arriving) and one.pending]
        small = [one for one in waiting if len(one.ref.shape) == 1]
        pieced = [one for one in waiting if one.pieces > 1]
        order = [(one, 0) for one in small]
        for piece in range(max((one.pieces for one in pieced), default=0)):
            order += [(one, piece) for one in pieced if piece < one.pieces]
        order += [(one, 0) for one in waiting if one not in small and one not in pieced]
        for one, piece in order:
            one.copy(piece).start()
        for copy in fetches:
            copy.start()
        for m, ref in zip(outs, results):
            if m.kind == "h":
                made.append(Leaving(departures.pop(0), ref, gone.pop(0), m.pieces))
            elif m.kind == "p":
                continue
            elif m.kind == "c":
                made[-1] = Leaving(made[-1].ref, ref, gone.pop(0), m.pieces)
            else:
                made.append(Staying(ref))
        kernel(given, made, *refs)
        for one in waiting:
            one()
        leaving = [one for one in made if isinstance(one, Leaving)]
        for one in leaving:
            one.finish()
        for one in leaving:
            one.wait()
        for copy in fetches:
            copy.wait()

    spaces = {"s": pltpu.SMEM, "v": pltpu.VMEM, "h": pltpu.HBM, "c": pltpu.HBM, "w": pl.ANY, "p": pltpu.VMEM, "q": pltpu.HBM, "x": pltpu.HBM}
    results = pl.pallas_call(
        body,
        name=name,
        out_shape=tuple(pins[m.kind](m.shape, m.dtype) for m in outs),
        in_specs=[pl.BlockSpec(memory_space=spaces[g.kind]) for g in args],
        out_specs=tuple(pl.BlockSpec(memory_space=spaces[m.kind]) for m in outs),
        scratch_shapes=[*scratches, *scratch],
        compiler_params=pltpu.CompilerParams(vmem_limit_bytes=limit << 20),
        cost_estimate=pl.CostEstimate(flops=2 * 10**10 * covers, bytes_accessed=1, transcendentals=0),
    )(*(pinned(g) for g in args))
    size = lambda pair: pair[0].size * pair[0].dtype.itemsize
    chain.last, kind = min(((result, m.kind) for m, result in zip(outs, results)), key=size)
    chain.kind = "x" if kind in "hc" else "w"
    return results


def dot(a, b):
    return jnp.dot(a, b, preferred_element_type=f32)


def dot_t(a, b):
    return lax.dot_general(a, b, (((1,), (1,)), ((), ())), preferred_element_type=f32)


def lane_of(shape):
    return lax.broadcasted_iota(jnp.int32, shape, 1)


def head_half(values, half):
    return jnp.where(lane_of(values.shape) // HEAD_DIM == half, values, jnp.zeros_like(values))


def normalize(values):
    centered = values - jnp.mean(values, axis=-1, keepdims=True)
    variance = jnp.mean(centered * centered, axis=-1, keepdims=True)
    inverse = lax.rsqrt(variance + EPSILON)
    return centered * inverse, inverse


def norm_back(grad_out, normed, inverse, gain):
    scaled = grad_out * gain
    return inverse * (
        scaled
        - jnp.mean(scaled, axis=-1, keepdims=True)
        - normed * jnp.mean(scaled * normed, axis=-1, keepdims=True)
    )


def column_sum(values):
    return jnp.sum(values, axis=0, keepdims=True)


def rows_used(lengths):
    used = jnp.int32(0)
    for slot in range(lengths.shape[1]):
        used = used + lengths[0, slot]
    return used


def row_span(index, size):
    if isinstance(index, int):
        return pl.ds(index * size, size)
    return pl.ds(pl.multiple_of(index * size, size), size)


def vector(ref):
    return ref[...][None, :]


def is_total(lane, head):
    found = lane == TOTALS_AT[0] + head
    for start in TOTALS_AT[1:]:
        found = found | (lane == start + head)
    return found


def in_pieces(values, lane):
    first = values.astype(bf16).astype(f32)
    second = (values - first).astype(bf16).astype(f32)
    third = values - first - second
    return jnp.where(lane < TOTALS_AT[1], first, jnp.where(lane < TOTALS_AT[2], second, third))


def attend(queries, keys, values, id_k, mixed, wide, features, block):
    lane = lane_of((block, LANES))

    @pl.loop(0, queries.shape[0] // block)
    def _(index):
        span = row_span(index, block)
        ids = features[span, :]
        feature = jnp.zeros((block, LANES), f32)
        for pair in range(queries.shape[1] // LANES):
            cols = slice(pair * LANES, (pair + 1) * LANES)
            wide_keys = jnp.concatenate([keys[:, cols], id_k[...]], axis=1)
            query, value = queries[span, cols], values[:, cols]
            total = None
            inverses = []
            for half in range(2):
                wide_query = jnp.concatenate([head_half(query, half), ids], axis=1)
                exponent = jnp.exp(dot_t(wide_query, wide_keys))
                totals = jnp.sum(exponent, axis=1, keepdims=True)
                term = dot(exponent.astype(bf16), head_half(value, half))
                total = term if total is None else total + term
                inverses.append(1.0 / totals)
                feature = jnp.where(is_total(lane, 2 * pair + half), -jnp.log(totals), feature)
            total = total * jnp.where(lane < HEAD_DIM, inverses[0], inverses[1])
            wide[span, cols] = total
            mixed[span, cols] = total.astype(bf16)
        features[span, :] = ids + in_pieces(feature, lane).astype(bf16)


def attend_shifted(queries, keys, values, id_k, mixed, wide, features, block):
    @pl.loop(0, queries.shape[0] // block)
    def _(index):
        span = row_span(index, block)
        ids = features[span, :]

        @pl.loop(0, queries.shape[1] // LANES)
        def _(pair):
            cols = row_span(pair, LANES)
            total = None
            for half in range(2):
                wide_query = jnp.concatenate([head_half(queries[span, cols], half), ids], axis=1)
                scores = dot_t(wide_query, jnp.concatenate([keys[:, cols], id_k[...]], axis=1))
                largest = jnp.max(scores, axis=1, keepdims=True)
                exponent = jnp.exp(scores - largest)
                totals = jnp.sum(exponent, axis=1, keepdims=True)
                term = dot(exponent.astype(bf16), head_half(values[:, cols], half)) / totals
                total = term if total is None else total + term
                lane = lane_of((block, LANES))
                feature = jnp.where(is_total(lane, 2 * pair + half), -(largest + jnp.log(totals)), 0.0)
                features[span, :] += in_pieces(feature, lane).astype(bf16)
            wide[span, cols] = total
            mixed[span, cols] = total.astype(bf16)


def largest_norms(array):
    found = jnp.zeros((1, 1), f32)
    for start in range(0, array.shape[1], LANES):
        values = array[:, start : start + LANES].astype(f32)
        squares = values * values
        both = jnp.sum(squares, axis=1, keepdims=True)
        one = jnp.sum(head_half(squares, 0), axis=1, keepdims=True)
        found = jnp.maximum(found, jnp.max(jnp.maximum(one, both - one), axis=0, keepdims=True))
    return jnp.max(found)


def qkv_kernel(given, made):
    lengths, gain, bias, tokens, weight, qv_bias, out_weight = given
    hidden, queries, keys, values, id_k, mixed, wide, features, part = made
    rows = tokens.ref.shape[0]
    slots = lengths.shape[1]
    lane = lane_of((1, LANES))
    starts = jnp.where(lane == 0, 0, rows)
    ends = jnp.full((1, LANES), rows, jnp.int32)
    running = jnp.int32(0)
    for slot in range(slots):
        running = running + lengths[0, slot]
        ends = jnp.where(lane == slot, running, ends)
        starts = jnp.where(lane == slot + 1, running, starts)
    scale = HEAD_DIM**-0.5
    block = rows // tokens.pieces
    gain, bias = gain(), bias()

    def norm(index):
        span = row_span(index, block) if not isinstance(index, int) else pl.ds(index * block, block)
        row = index * block + lax.broadcasted_iota(jnp.int32, (block, LANES), 0)
        same = (row >= starts) & (row < ends)
        features.ref[span, :] = same.astype(f32).astype(bf16)
        id_k.ref[span, :] = jnp.where(same | (lane > slots), 0.0, -MASKED).astype(bf16)
        normed, _ = normalize(tokens.ready(index)[span, :].astype(f32))
        hidden.ref[span, :] = (normed * vector(gain) + vector(bias)).astype(bf16)
        hidden.send(index)
        id_k.send(index)

    def project(index):
        span = row_span(index, block) if not isinstance(index, int) else pl.ds(index * block, block)
        low = hidden.ref[span, :]
        raised = (dot(low, weight[0]) + qv_bias[0:1, :]).astype(bf16)
        queries.ref[span, :] = (raised.astype(f32) * scale).astype(bf16)
        keys.ref[span, :] = dot(low, weight[1]).astype(bf16)
        values.ref[span, :] = (dot(low, weight[2]) + qv_bias[1:2, :]).astype(bf16)
        for one in (queries, keys, values):
            one.send(index)

    norm(0)
    weight, qv_bias = weight(), qv_bias()

    @pl.loop(0, tokens.pieces - 1)
    def _(index):
        project(index)
        norm(index + 1)

    project(tokens.pieces - 1)

    bounded = largest_norms(queries.ref) * largest_norms(keys.ref) <= 4000.0
    operands = [one.ref for one in (queries, keys, values, id_k, mixed, wide, features)]

    @pl.when(bounded)
    def _():
        attend(*operands, rows // 4)

    @pl.when(jnp.logical_not(bounded))
    def _():
        attend_shifted(*operands, LANES)

    for one in (mixed, wide, features):
        one.send()
    out_weight = out_weight()

    @pl.loop(0, 4)
    def _(index):
        span = row_span(index, rows // 4)
        part.ref[span, :] = dot(mixed.ref[span, :], out_weight[...]).astype(bf16)
        part.send(index)


def grad_active_kernel(blocks, given, made, grad_mlp):
    lengths, place, cotangent, down = given
    ordered, grad_active, down_bias_grad = made[:3]
    used = rows_used(lengths)
    rows = grad_mlp.shape[0]
    block = rows // cotangent.pieces
    down_bias_grad.ref[...] = jnp.zeros_like(down_bias_grad.ref)

    @pl.loop(0, cotangent.pieces)
    def _(index):
        span = row_span(index, block)
        row = index * block + lax.broadcasted_iota(jnp.int32, (block, 1), 0)
        grad = jnp.where(row < used, cotangent.ready(index)[span, :].astype(f32), 0.0)
        down_bias_grad.ref[...] += column_sum(grad)
        grad_mlp[span, :] = grad.astype(bf16)

    order_columns(grad_mlp[...], place, ordered.ref, blocks)
    down = down()

    @pl.loop(0, cotangent.pieces)
    def _(index):
        span = row_span(index, block)
        grad_active.ref[span, :] = dot_t(grad_mlp[span, :], down[...])


def mlp_kernel(given, made):
    out_bias, gain, bias, tokens, mine, other, up_bias, up, ordered, grad_active = given
    hidden, normed_two, inverse_two, active_out, grad_pre, part, keep, send = made
    rows = hidden.ref.shape[0]
    block, tile = rows // 4, 512
    out_bias, gain, bias = out_bias(), gain(), bias()

    @pl.loop(0, rows // block)
    def _(index):
        span = row_span(index, block)
        for one in (tokens, mine, other):
            one.ready(index)
        after = tokens.ref[span, :].astype(f32) + (
            mine.ref[span, :].astype(f32) + other.ref[span, :].astype(f32) + vector(out_bias)
        )
        normed, inverse = normalize(after)
        normed_two.ref[span, :] = normed.astype(bf16)
        inverse_two.ref[span, :] = jnp.broadcast_to(inverse, (block, LANES))
        hidden.ref[span, :] = (normed * vector(gain) + vector(bias)).astype(bf16)
        for one in (normed_two, inverse_two):
            one.send(index)

    up_bias, up, grad_active = up_bias(), up(), grad_active()

    block = rows // 2

    @pl.loop(0, rows // block)
    def _(index):
        span = row_span(index, block)
        low = hidden.ref[span, :]
        total = None
        for start in range(0, up.shape[1], tile):
            cols = slice(start, start + tile)
            pre = dot(low, up[:, cols]) + up_bias[cols][None, :]
            square = pre * pre
            inner = pre * (0.7978845608028654 + (0.7978845608028654 * 0.044715) * square)
            share = 0.5 + 0.5 * jnp.tanh(inner)
            active = pre * share
            active_out.ref[span, cols] = active.astype(bf16)
            slope = share + (active * (1.0 - share)) * (
                (2 * 0.7978845608028654) + (6 * 0.7978845608028654 * 0.044715) * square
            )
            grad_low = (grad_active[span, cols] * slope).astype(bf16)
            grad_pre.ref[span, cols] = grad_low
            term = dot_t(grad_low, up[:, cols])
            total = term if total is None else total + term
        active_out.send(index)
        part.ref[span, :] = total.astype(bf16)

    weight_grad(ordered(), active_out.ref, keep, send)


def down_kernel(given, made):
    weight, activated = given
    part = made[0]
    rows = activated.ref.shape[0] // 4
    weight = weight()
    activated = activated()

    @pl.loop(0, 4)
    def _(index):
        span = row_span(index, rows)
        part.ref[span, :] = dot(activated[span, :], weight[...]).astype(bf16)


def order_columns(values, place, ordered, blocks):
    turned = values.T
    width = turned.shape[0]
    size = width // blocks
    if size % 16:
        ordered[:width, :] = turned
    else:
        for index in range(blocks):
            at = pl.multiple_of(place[index] * size, size)
            ordered[pl.ds(at, size), :] = turned[index * size : (index + 1) * size]
    ordered[width:, :] = jnp.ones((16, turned.shape[1]), bf16)


def weight_grad(ordered, right, keep, send, sums=None, at=0):
    width = ordered.shape[0] - 16
    middle, columns = width // 2, right.shape[1]
    tile = 512 if columns % 512 == 0 else columns

    def one(start):
        source = pl.ds(start, tile)
        target = pl.ds(at + start, tile)
        result = dot(ordered[...], right[:, source])
        send.ref[:, target] = result[middle:width].astype(bf16)
        keep.ref[:, target] = result[:middle].astype(bf16)
        if sums is not None:
            sums.ref[:, source] = result[width : width + 8]

    if tile == columns:
        one(0)
    else:

        @pl.loop(0, columns // tile)
        def _(index):
            one(pl.multiple_of(index * tile, tile))


def weight_kernel(blocks, given, made, ordered):
    place, left, right = given
    order_columns(left()[...], place, ordered, blocks)
    weight_grad(ordered, right(), *made)


def middle_kernel(blocks, given, made, normed_back, ordered):
    lengths, place, gain, norm_mine, norm_other, normed_two, inverse_two, cotangent, weight, mixed, wide = given
    used = rows_used(lengths)
    resid, grad_mixed, grad_features, sums, keep, send = made
    rows = norm_mine.ref.shape[0]
    block = 256
    sums.ref[...] = jnp.zeros_like(sums.ref)
    gain = gain()

    @pl.loop(0, rows // block)
    def _(index):
        span = row_span(index, block)
        for one in (normed_two, inverse_two, cotangent):
            one.ready(index)
        normed = normed_two.ref[span, :].astype(f32)
        grad_norm = norm_mine.ready(index)[span, :].astype(f32) + norm_other.ready(index)[
            span, :
        ].astype(f32)
        inverse = inverse_two.ref[span, 0:1]
        row = index * block + lax.broadcasted_iota(jnp.int32, (block, 1), 0)
        grad = jnp.where(row < used, cotangent.ref[span, :].astype(f32), 0.0)
        grad = grad + norm_back(grad_norm, normed, inverse, vector(gain))
        resid.ref[span, :] = grad
        resid.send(index)
        low = grad.astype(bf16)
        normed_back[span, :] = low
        sums.ref[0:1, :] += column_sum(grad_norm * normed)
        sums.ref[1:2, :] += column_sum(grad_norm)
        sums.ref[2:3, :] += column_sum(low.astype(f32))

    grad_mixed.ref[...] = dot_t(normed_back[...], weight()[...]).astype(bf16)
    wide = wide()

    @pl.loop(0, rows // block)
    def _(index):
        span = row_span(index, block)
        lane = lane_of((block, LANES))
        centres = jnp.zeros((block, LANES), f32)
        for pair in range(wide.shape[1] // LANES):
            cols = slice(pair * LANES, (pair + 1) * LANES)
            product = grad_mixed.ref[span, cols].astype(f32) * wide[span, cols]
            for half in range(2):
                centre = jnp.sum(head_half(product, half), axis=1, keepdims=True)
                centres = jnp.where(is_total(lane, 2 * pair + half), -centre, centres)
        grad_features.ref[span, :] = in_pieces(centres, lane).astype(bf16)

    order_columns(normed_back[...], place, ordered, blocks)
    weight_grad(ordered, mixed(), keep, send)


def attention_back_kernel(pair, blocks, given, made, wide_keys, wide_values, turned, key_total, value_total):
    given, before = given[:9], given[9:]
    place, keys, queries, values, id_k, features, grad_mixed, grad_features, hidden = given
    if pair == 0:
        *made, ordered = made
        ordered = ordered.ref
    queries, keys, values, id_k, features, grad_mixed, grad_features = (
        one() for one in (queries, keys, values, id_k, features, grad_mixed, grad_features)
    )
    grads, sums, keep, send = made
    rows = queries.shape[0]
    cols = slice(pair * LANES, (pair + 1) * LANES)
    lane = lane_of((1, LANES))
    key = keys[:, cols]
    turned[...] = key.T
    for half in range(2):
        wide_keys[half, :, :LANES] = key
        ones = is_total(lane, 2 * pair + half).astype(f32).astype(bf16)
        wide_keys[half, :, LANES:] = id_k[...] + ones
        wide_values[half, :, :LANES] = values[:, cols]
        wide_values[half, :, LANES:] = jnp.broadcast_to(ones, (rows, LANES))
    block = rows // 2
    key_total[...] = jnp.zeros_like(key_total)
    value_total[...] = jnp.zeros_like(value_total)

    def half_of_queries(index):
        span = row_span(index, block)
        query, grad, feature = queries[span, cols], grad_mixed[span, cols], features[span, :]
        grad_feature = grad_features[span, :]
        key_term = value_term = None
        turned_grads = []
        for half in range(2):
            one_query, one_grad = head_half(query, half), head_half(grad, half)
            probs = jnp.exp(dot_t(wide_keys[half], jnp.concatenate([one_query, feature], axis=1)))
            centred = dot_t(wide_values[half], jnp.concatenate([one_grad, grad_feature], axis=1))
            grad_scores = (probs * centred).astype(bf16)
            value_one = dot(probs.astype(bf16), one_grad)
            key_one = dot(grad_scores, one_query)
            value_term = value_one if half == 0 else value_term + value_one
            key_term = key_one if half == 0 else key_term + key_one
            turned_grads.append(dot(turned[half * HEAD_DIM : (half + 1) * HEAD_DIM, :], grad_scores))
        key_total[...] += key_term
        value_total[...] += value_term
        grads.ref[span, :LANES] = (jnp.concatenate(turned_grads, axis=0).T * HEAD_DIM**-0.5).astype(bf16)

    if pair % 2 == 0:
        half_of_queries(0)
        half_of_queries(1)
    else:
        pl.loop(0, 2)(half_of_queries)

    grads.ref[:, LANES : 2 * LANES] = key_total[...].astype(bf16)
    grads.ref[:, 2 * LANES :] = value_total[...].astype(bf16)
    if pair == 0:
        order_columns(hidden()[...], place, ordered, blocks)
    else:
        ordered = hidden()
    at = 0
    for index in range(0, len(before), 2):
        columns = before[index].ref.shape[1]
        for target, source in zip((keep, send), before[index : index + 2]):
            target.ref[:, at : at + columns] = source()[...]
        at += columns
    weight_grad(ordered, grads.ref, keep, send, sums, at)


def first_kernel(given, made):
    *grads, weight = given
    weight, part = weight(), made[0]
    rows = part.ref.shape[0] // 4
    grads = [one() for one in grads]
    @pl.loop(0, 4)
    def _(index):
        span = row_span(index, rows)
        operand = jnp.concatenate(
            [one[span, kind * LANES : (kind + 1) * LANES] for kind in range(3) for one in grads], axis=1
        )
        full = jnp.concatenate([weight[kind] for kind in range(3)], axis=1)
        part.ref[span, :] = dot_t(operand, full).astype(bf16)


def last_kernel(given, made):
    gain, tokens, mine, other, resid, *sums = given
    out, vectors = made
    middle_sums, down_sums, up_sums, *pair_sums = (one()[...] for one in sums)
    block = tokens.ref.shape[0] // 4
    width = tokens.ref.shape[1]
    vectors.ref[...] = jnp.zeros_like(vectors.ref)
    gain, tokens, mine, other, resid = gain(), tokens(), mine(), other(), resid()

    @pl.loop(0, 4)
    def _(index):
        span = row_span(index, block)
        normed, inverse = normalize(tokens[span, :].astype(f32))
        grad_first = mine[span, :].astype(f32) + other[span, :].astype(f32)
        out.ref[span, :] = resid[span, :] + norm_back(grad_first, normed, inverse, vector(gain))
        out.send(index)
        vectors.ref[0:1, :] += column_sum(grad_first * normed)
        vectors.ref[1:2, :] += column_sum(grad_first)

    pairs = len(pair_sums)
    for pair, one in enumerate(pair_sums):
        for kind, start in ((0, 0), (2, pairs * LANES)):
            at = start + pair * LANES
            vectors.ref[2:3, at : at + LANES] = one[0:1, kind * LANES : (kind + 1) * LANES]
    vectors.ref[3:6, :] = middle_sums[0:3, :]
    vectors.ref[6:7, :] = down_sums
    for index in range(up_sums.shape[1] // width):
        vectors.ref[7 + index : 8 + index, :] = up_sums[0:1, index * width : (index + 1) * width]


def fold_kernel(joined, folded, given, made):
    at = 0
    for index in range(len(given) // 2):
        keep, came = given[2 * index](), given[2 * index + 1]()
        stays, sent = made[:2] if joined else made[2 * index : 2 * index + 2]
        cols = slice(at, at + keep.shape[1])
        at += keep.shape[1] if joined else 0
        if index < folded:
            stays.ref[:, cols] = keep[...]
            sent.ref[:, cols] = came[...]
            continue
        middle = keep.shape[0] // 2
        sent.ref[:, cols] = (keep[middle:].astype(f32) + came[middle:].astype(f32)).astype(bf16)
        stays.ref[:, cols] = keep[:middle].astype(f32) + came[:middle].astype(f32)


def add_kernel(given, made):
    made[0].ref[...] = given[0]()[...] + given[1]()[...]


def spread_kernel(given, made):
    total = given[0]()[...] + given[1]()[...]
    *singles, qv, ups = made
    width = total.shape[1]
    for row, one in zip((0, 1, 3, 4, 5, 6), singles):
        one.ref[...] = total[row]
    local = qv.ref.shape[1]
    for row in range(2):
        qv.ref[row : row + 1] = total[2:3, row * local : (row + 1) * local]
    for row in range(ups.ref.shape[0] // width):
        ups.ref[pl.ds(row * width, width)] = total[7 + row]


def output_kernel(given, made):
    out_bias, down_bias, tokens, part, other, down_part, down_other = given
    out = made[0]
    out_bias, down_bias, down_part, down_other = out_bias(), down_bias(), down_part(), down_other()
    block = out.ref.shape[0] // out.pieces

    @pl.loop(0, out.pieces)
    def _(index):
        span = row_span(index, block)
        for one in (tokens, part, other):
            one.ready(index)
        after = tokens.ref[span, :].astype(f32) + (
            part.ref[span, :].astype(f32) + other.ref[span, :].astype(f32) + vector(out_bias)
        )
        branch = down_part[span, :].astype(f32) + down_other[span, :].astype(f32) + vector(down_bias)
        out.ref[span, :] = (after + branch).astype(bf16)
        out.send(index)


def final_kernel(given, made):
    for index, one in enumerate(made):
        one.ref[...] = given[2 * index]()[...] + given[2 * index + 1]()[...].astype(f32)
        one.send()


def final_qkv_kernel(given, made):
    qkv, out = made
    keep, came = given
    total = keep()[...] + came()[...].astype(f32)
    local = out.ref.shape[1]
    out.ref[...] = total[:, :local]
    for pair in range(local // LANES):
        for kind in range(3):
            at = local + (3 * pair + kind) * LANES
            qkv.ref[kind, :, pair * LANES : (pair + 1) * LANES] = total[:, at : at + LANES]


def swap(values, axis, bit, size):
    return lax.ppermute(values, axis, [(i, i ^ (1 << bit)) for i in range(size)])


class Flow:
    def __init__(self, orders, size, keep, send):
        self.orders, self.size, self.keep, self.send, self.step = orders, size, keep, send, 0

    def exchange(self):
        pairs = [
            (2 * index + core, 2 * (index ^ (1 << order[self.step])) + core)
            for index in range(self.size)
            for core, order in enumerate(self.orders)
        ]
        self.came = lax.ppermute(self.send, ("dp", "mp"), pairs)
        self.step += 1


def fold(chain, flows, ready=(), covers=True):
    halved = [(flow.keep.shape[0] // 2, flow.keep.shape[1]) for flow in flows]
    if ready:
        columns = sum(flow.keep.shape[1] for flow in (*ready, *flows))
        halved = [(halved[0][0], columns)]
    outs = []
    for rows, columns in halved:
        outs += [Made((rows, columns), f32, "h" if rows <= 48 else "v"), Made((rows, columns), bf16, "v")]
    pairs = [(flow.keep, flow.send) for flow in ready] + [(flow.keep, flow.came) for flow in flows]
    results = call(
        chain,
        functools.partial(fold_kernel, bool(ready), len(ready)),
        "fold",
        outs,
        [Given(array, "v") for pair in pairs for array in pair],
        limit=8,
        covers=covers,
    )
    for index in range(len(halved)):
        flows[index].keep, flows[index].send = results[2 * index : 2 * index + 2]


def finish(chain, flows, kernel, shapes, covers=True):
    return call(
        chain,
        kernel,
        "final",
        [Made(shape, f32, "h") for shape in shapes],
        [Given(array, kind) for flow in flows for array, kind in ((flow.keep, "h"), (flow.came, "v"))],
        limit=8,
        covers=covers,
    )


def places(orders, size, me, core):
    source = jnp.arange(size, dtype=jnp.int32) ^ me
    found = []
    for order in orders:
        place = jnp.zeros((size,), jnp.int32)
        for step, bit in enumerate(order):
            place = place + (((source >> bit) & 1) << (size.bit_length() - 2 - step))
        found.append(place)
    return jnp.where(core == 0, *found)


def arranged(halves, place, size):
    keep, send = halves
    rows, columns = keep.shape
    if (2 * rows // size) % 16 == 0:
        return halves
    spots = jnp.zeros((size,), jnp.int32).at[place].set(jnp.arange(size, dtype=jnp.int32))
    both = jnp.concatenate(halves, axis=0).reshape(size, 2 * rows // size, columns)[spots]
    both = both.reshape(2 * rows, columns)
    return both[:rows], both[rows:]


def per_device(
    n_dp, tokens, cotangent, lengths, ln1_gain, ln1_bias, qkv_weight, qv_bias, out_weight, out_bias,
    ln2_gain, ln2_bias, up_weight, up_bias, down_weight, down_bias,
):
    chain = Chain()
    rows, width = tokens.shape
    local = qkv_weight.shape[2]
    units = up_weight.shape[1]
    pairs = local // LANES
    me, core = lax.axis_index("dp"), lax.axis_index("mp")
    bits = list(range(n_dp.bit_length() - 1))
    rest = bits[3:]
    near_orders = [[0, 1, 2, *rest], [1, 0, 2, *rest]]
    long_orders = [[2, 0, 1, *rest], [2, 1, 0, *rest]]
    near_place, long_place = (places(orders, n_dp, me, core) for orders in (near_orders, long_orders))
    weight = jnp.transpose(qkv_weight, (1, 0, 2))
    scalars = Given(lengths, "s")
    near = lambda array: Given(array, "v")
    far = lambda array, pieces=1: Given(array, "h", pieces)
    fetch = lambda array: Made(array.shape, array.dtype, "p", source=array)
    halves = lambda columns: [Made((width // 2, columns), bf16, "v")] * 2
    turned = pltpu.VMEM((width + 16, rows), bf16)

    hidden_one, queries, keys, values, id_k, mixed, mixed_wide, features, part = call(
        chain,
        qkv_kernel,
        "qkv_attention",
        [
            Made((rows, width), bf16, "h", 4),
            *[Made((rows, local), bf16, "h", 4)] * 3,
            Made((rows, LANES), bf16, "h", 4),
            Made((rows, local), bf16, "h"),
            Made((rows, local), f32, "h"),
            Made((rows, LANES), bf16, "h"),
            Made((rows, width), bf16, "v", 4),
        ],
        [
            scalars, far(ln1_gain), far(ln1_bias), far(tokens, 4), far(weight), far(qv_bias), far(out_weight)
        ],
        limit=28,
    )
    other = swap(part, "mp", 0, 2)
    turned_grad, grad_active, down_sums, near_tokens, near_up = call(
        chain,
        functools.partial(grad_active_kernel, n_dp),
        "grad_active",
        [
            Made((width + 16, rows), bf16, "v"),
            Made((rows, units), f32, "v"),
            Made((1, width), f32, "v"),
            fetch(tokens),
            fetch(up_weight),
        ],
        [scalars, Given(near_place, "s"), far(cotangent, 4), far(down_weight)],
        scratch=[pltpu.VMEM((rows, width), bf16)],
        limit=16,
    )
    hidden_two, normed_two, inverse_two, activated, grad_pre, norm_part, down_keep, down_send = call(
        chain,
        mlp_kernel,
        "mlp",
        [
            Made((rows, width), bf16, "v"),
            Made((rows, width), bf16, "h", 4),
            Made((rows, LANES), f32, "h", 4),
            Made((rows, units), bf16, "h", 2),
            Made((rows, units), bf16, "v"),
            Made((rows, width), bf16, "v"),
            *halves(units),
        ],
        [
            *map(far, (out_bias, ln2_gain, ln2_bias)),
            *map(near, (near_tokens, part, other)),
            far(up_bias),
            near(near_up),
            near(turned_grad),
            near(grad_active),
        ],
        limit=22,
    )
    norm_other = swap(norm_part, "mp", 0, 2)

    def weights(name, left, right, place, with_sums=False):
        return call(
        chain,
            functools.partial(weight_kernel, n_dp),
            name,
            [*halves(units), *[Made((8, units), f32, "v")] * with_sums],
            [Given(place, "s"), near(left), near(right)],
            scratch=[turned],
            limit=10,
        )

    flow_down = Flow(near_orders, n_dp, *arranged((down_keep, down_send), near_place, n_dp))
    flow_down.exchange()
    up_keep, up_send, up_sums = weights("up_grad", hidden_two, grad_pre, long_place, True)
    flow_up = Flow(long_orders, n_dp, *arranged((up_keep, up_send), long_place, n_dp))
    flow_up.exchange()
    resid, grad_mixed, grad_features, middle_sums, out_keep, out_send = call(
        chain,
        functools.partial(middle_kernel, n_dp),
        "middle",
        [
            Made((rows, width), f32, "h", 4),
            Made((rows, local), bf16, "v"),
            Made((rows, LANES), bf16, "v"),
            Made((8, width), f32, "v"),
            *halves(local),
        ],
        [
            scalars,
            Given(near_place, "s"),
            far(ln2_gain),
            near(norm_part),
            near(norm_other),
            *map(near, (normed_two, inverse_two, cotangent)),
            near(out_weight),
            near(mixed),
            near(mixed_wide),
        ],
        scratch=[pltpu.VMEM((rows, width), bf16), turned],
        limit=16,
    )
    grads, sums, halves_qkv = [], [], []
    hiddens = [hidden_one]

    def attention_back(pair, before=()):
        columns = 3 * LANES + sum(keep.shape[1] for keep, _ in before)
        three, sums_one, keep, send, *order = call(
            chain,
            functools.partial(attention_back_kernel, pair, n_dp),
            "attention_back%d" % pair,
            [
                Made((rows, 3 * LANES), bf16, "v"),
                Made((8, 3 * LANES), f32, "v"),
                *halves(columns),
                *[Made((width + 16, rows), bf16, "h")] * (pair == 0),
            ],
            [
                Given(near_place, "s"),
                *map(near, (keys, queries, values, id_k, features, grad_mixed, grad_features)),
                near(hiddens[-1]),
                *(near(array) for pieces in before for array in pieces),
            ],
            scratch=[
                pltpu.VMEM((2, rows, 2 * LANES), bf16),
                pltpu.VMEM((2, rows, 2 * LANES), bf16),
                pltpu.VMEM((LANES, rows), bf16),
                pltpu.VMEM((rows, LANES), f32),
                pltpu.VMEM((rows, LANES), f32),
            ],
            limit=18,
        )
        hiddens.extend(order)
        grads.append(three)
        sums.append(sums_one)
        halves_qkv.append((keep, send))

    def exchange(*flows):
        for flow in flows:
            flow.exchange()

    def flow_of(pieces):
        return Flow(near_orders, n_dp, *arranged(pieces, near_place, n_dp))

    flow_out = flow_of((out_keep, out_send))
    exchange(flow_out)
    attention_back(0)
    flow_first = flow_of(halves_qkv[0])
    fold(chain, [flow_down, flow_out])
    exchange(flow_down, flow_first)
    for pair in range(1, pairs - 1):
        attention_back(pair)
    flows_next = [flow_of(pieces) for pieces in halves_qkv[1:]]
    fold(chain, [flow_down, flow_up, flow_first])
    exchange(flow_down, flow_up, *flows_next)
    attention_back(pairs - 1)
    flow_qkv = flow_of(halves_qkv[-1])
    exchange(flow_qkv)
    fold(chain, [flow_down, flow_up, *flows_next])
    exchange(flow_up)
    (first_part,) = call(
        chain,
        first_kernel,
        "first",
        [Made((rows, width), bf16, "v", 4)],
        [*map(near, grads), near(weight)],
        limit=10,
    )
    first_other = swap(first_part, "mp", 0, 2)
    fold(chain, [flow_qkv], [flow_out, flow_first, *flows_next])
    exchange(flow_qkv)
    fold(chain, [flow_up])
    last_step = len(rest) == 1
    if last_step:
        exchange(flow_down, flow_up)
    tokens_grad, vectors = call(
        chain,
        last_kernel,
        "last",
        [Made((rows, width), f32, "h", 4), Made((16, width), f32, "v")],
        [
            far(ln1_gain),
            *map(near, (tokens, first_part, first_other, resid, middle_sums, down_sums, up_sums, *sums)),
        ],
        limit=14,
    )
    shape = (width // n_dp, units)
    fold(chain, [flow_qkv], covers=False)
    exchange(flow_qkv)
    if last_step:
        down_total, up_total = finish(chain, [flow_down, flow_up], final_kernel, [shape] * 2, False)
    if not last_step:
        exchange(flow_down, flow_up)

    def all_sum_step(bit, covers=True):
        nonlocal vectors
        other = swap(vectors, "dp", bit, n_dp)
        (vectors,) = call(
            chain,
            add_kernel,
            "add",
            [Made((16, width), f32, "v")],
            [near(vectors), near(other)],
            limit=4,
            covers=covers,
        )

    all_sum_step(bits[0], False)
    (down_part,) = call(
        chain,
        down_kernel,
        "down",
        [Made((rows, width), bf16, "v", 4)],
        [near(down_weight), near(activated)],
        limit=10,
    )
    down_other = swap(down_part, "mp", 0, 2)
    fold(chain, [flow_qkv])
    exchange(flow_qkv)
    all_sum_step(bits[1], False)
    (output,) = call(
        chain,
        output_kernel,
        "output",
        [Made((rows, width), bf16, "h", 4)],
        [
            far(out_bias), far(down_bias), *(far(array, 4) for array in (tokens, part, other)), near(down_part),
            near(down_other),
        ],
        limit=16,
    )
    for bit in bits[2:-1]:
        all_sum_step(bit, False)
    flows = [flow_qkv, flow_up, flow_down]
    for step in range(1, len(rest)):
        fold(chain, flows)
        exchange(*flows)
    if not last_step:
        down_total, up_total = finish(chain, [flow_down, flow_up], final_kernel, [shape] * 2)
    mine = width // n_dp
    qkv_total, out_total = finish(
        chain, [flow_qkv], final_qkv_kernel, [(3, mine, local), (mine, local)]
    )
    *singles, qv_sum, up_sum = call(
        chain,
        spread_kernel,
        "spread",
        [*[Made((width,), f32, "h")] * 6, Made((2, local), f32, "h"), Made((units,), f32, "h")],
        [near(vectors), near(swap(vectors, "dp", bits[-1], n_dp))],
        limit=4,
    )
    gain_one, bias_one, gain_two, bias_two, out_bias_sum, down_bias_sum = singles
    return (
        output,
        tokens_grad,
        gain_one,
        bias_one,
        jnp.transpose(qkv_total, (1, 0, 2)),
        qv_sum,
        out_total.T,
        out_bias_sum,
        gain_two,
        bias_two,
        up_total,
        up_sum,
        down_total.T,
        down_bias_sum,
    )


def solution(mesh):
    return jax.shard_map(
        functools.partial(per_device, mesh.shape["dp"]),
        mesh=mesh,
        in_specs=(
            P("dp", None),
            P("dp", None),
            P("dp", None),
            P(),
            P(),
            P(None, None, "mp"),
            P(None, "mp"),
            P("mp", None),
            P(),
            P(),
            P(),
            P(None, "mp"),
            P("mp"),
            P("mp", None),
            P(),
        ),
        out_specs=(
            P("dp", None),
            P("dp", None),
            P(),
            P(),
            P("dp", None, "mp"),
            P(None, "mp"),
            P("mp", "dp"),
            P(),
            P(),
            P(),
            P("dp", "mp"),
            P("mp"),
            P("mp", "dp"),
            P(),
        ),
        check_vma=False,
    )
```
